32 devices in a mesh: groups: 2 (over y), ctx: 4 (over z), exp: 2 (over x), tp: 2 (over core).
Axes of the slice: x: 2, y: 2, z: 4, core: 2. Of those that a mesh axis runs over, the one named last changes fastest.
Arguments:
- queries: bfloat16 [4, 512, 20, 128], P(('groups', 'exp'), 'ctx', 'tp'), parts along dimension 0, may hold values from -9 to 9
- key_states: bfloat16 [4, 512, 4, 128], P(('groups', 'exp'), 'ctx', 'tp'), parts along dimension 0, may hold values from -9 to 9
- values: bfloat16 [4, 512, 4, 128], P(('groups', 'exp'), 'ctx', 'tp'), parts along dimension 0, may hold values from -6 to 6
- doc_ids: int32 [4, 512], P(('groups', 'exp'), 'ctx'), parts along dimension 0, may hold values from 0 to 3, never falling along the last dimension, each value on 1 to 256 neighbouring positions
- residual: bfloat16 [4, 512, 5120], P(('groups', 'exp'), ('ctx', 'tp')), parts along dimension 0, may hold values from -6 to 6
- out_proj: bfloat16 [2560, 5120], P('tp', 'ctx'), may hold values from -0.125 to 0.125
- norm_gain: bfloat16 [5120], replicated, may hold values from 0.5 to 1.5
- router: bfloat16 [5120, 64], P(None, 'exp'), may hold values from -0.078125 to 0.078125
- expert_ids: int32 [4, 512, 1], P(('groups', 'exp'), ('ctx', 'tp')), parts along dimension 0, may hold values from 0 to 63; in each aligned block of 64 rows (0 to 63, 64 to 127, ..., all dimensions but the last counted through in order) at most 2 rows name the same one
- keep_counts: int32 [128], P('groups'), parts along dimension 0, may hold values from 1 to 2
Outputs:
- expert_inputs: bfloat16 [32, 64, 2, 5120], P(('groups', 'ctx', 'tp'), 'exp'), parts along dimension 0
The draws below stay inside these ranges and needn't reach their ends.
There are 2 independent parts, one for each index of `groups`. The reference program is written for one: setup_inputs(seed, part) draws one part's arguments, and reference() takes and returns one part's arrays. A program takes and returns all parts, laid end to end along the dimension named above; an argument that names none is the same for every part. Nothing has to cross between parts.
Inputs may be any that keep to these rules, and one draw needn't show every extreme that they name: `doc_ids`: doc ids never fall along a request; a document holds at most 256 tokens, and some document holds exactly that many. `expert_ids`: in each aligned block of 64 tokens (the rows of one device) no expert is named more than 2 times, and in some blocks one expert is named exactly 2 times.
All inputs are finite; a program needn't handle non-finite values.
Results may differ from the reference program's by a relative error of at most 0.013.
Values may be sent and summed in bfloat16 or wider, within the bound.
A program may use at most 64 MiB of HBM per device.

```python
import math
import jax
import jax.numpy as jnp
import numpy as np
from jax import lax

D = 5120
HEAD_DIMENSION = 128
EXPERTS = 64
QUERY_HEADS = 20
KEY_VALUE_HEADS = 4
CAP = 2
DOCS = 4
TOK_DEV = 128
REQUEST_COUNT = 2
REQUEST_TOKENS = 512
N_CTX = 4
N_TP = 2


def query_key_pair(key):
    folded = jax.random.fold_in(key, 5)
    query_key, state_random_key = jax.random.split(folded, 2)
    sampled_query = jnp.clip(jax.random.normal(query_key, (REQUEST_COUNT, REQUEST_TOKENS, QUERY_HEADS, HEAD_DIMENSION), jnp.float32), -4.0, 4.0)
    sampled_state = jnp.clip(jax.random.normal(state_random_key, (REQUEST_COUNT, REQUEST_TOKENS, KEY_VALUE_HEADS, HEAD_DIMENSION), jnp.float32), -4.0, 4.0)
    return (sampled_query, sampled_state)


def draw_queries(key, part):
    return query_key_pair(key)[0].astype(jnp.bfloat16)


def draw_key_states(key, part):
    return query_key_pair(key)[1].astype(jnp.bfloat16)


def draw_residual(key, part):
    folded = jax.random.fold_in(key, 11)
    noise_key, row_key, column_key = jax.random.split(folded, 3)
    row_scale = jnp.exp(jax.random.uniform(row_key, (REQUEST_COUNT, REQUEST_TOKENS, 1), jnp.float32, math.log(0.02), math.log(0.2)))
    column_scale = jnp.exp(jax.random.uniform(column_key, (1, 1, D), jnp.float32, math.log(0.33), math.log(3.3)))
    noise = jnp.clip(jax.random.normal(noise_key, (REQUEST_COUNT, REQUEST_TOKENS, D), jnp.float32), -4.0, 4.0)
    return (noise * row_scale * column_scale).astype(jnp.bfloat16)


def plant(result, own_key, least, largest):
    longest = result.shape.index(max(result.shape))
    spots = []
    for shift in (0, 1):
        where = [jax.random.randint(jax.random.fold_in(own_key, axis), (), 0, length) for axis, length in enumerate(result.shape)]
        where[longest] = (where[longest] + shift) % result.shape[longest]
        spots.append(tuple(where))
    return result.at[spots[0]].set(least).at[spots[1]].set(largest)


def level_of(key, dims, shards, smallest, top_value):
    level = 1.0
    for dim, shards_of in shards:
        steps = jax.random.uniform(jax.random.fold_in(jax.random.fold_in(key, 6), dim), (shards_of,), jnp.float32, smallest / len(shards), top_value / len(shards))
        level = level * jnp.repeat(jnp.exp(steps), dims[dim] // shards_of).reshape((-1,) + (1,) * (len(dims) - 1 - dim))
    return level


def length_profile(amount, total, most, skew):
    portions = [(1 << 20) // math.isqrt(rank ** skew) + 1 for rank in range(2, amount + 1)]
    spare, counts = total - most - (amount - 1), [1] * (amount - 1)
    while spare > 0:
        free = [i for i in range(amount - 1) if counts[i] < most]
        pool, left = sum([portions[i] for i in free]), spare
        for i in free:
            addition = min(most - counts[i], max(1, left * portions[i] // pool), spare)
            counts[i] = counts[i] + addition
            spare = spare - addition
    return np.array([most] + counts)


def uneven(key, count, total, most, lean):
    if count == 2:
        one = jax.random.randint(key, (), max(1, total - most), min(most, total - 1) + 1)
        return jnp.stack([one, total - one])
    tallies = jnp.asarray(length_profile(count, total, most, lean), jnp.int32)
    twos = (count - 1) // 2
    donor, receiver = tallies[1:1 + 2 * twos:2], tallies[2:2 + 2 * twos:2]
    room = jnp.minimum(donor - 1, most - receiver)
    shifted = jax.random.randint(jax.random.fold_in(key, 1), (twos,), 0, 1 << 20) % (room + 1)
    tallies = tallies.at[1:1 + 2 * twos:2].set(donor - shifted).at[2:2 + 2 * twos:2].set(receiver + shifted)
    return tallies[jax.random.permutation(jax.random.fold_in(key, 2), count)]


def assign_block(key, own, number, rows, number_of, top, reach, lean):
    order = jax.random.permutation(key, number_of)
    crowded, usual = load_shares(number_of, rows * top, reach, lean, True), load_shares(number_of, rows * top, reach, lean, False)
    places = jnp.arange(number_of)

    def named(lengths, rotation):
        used = int((lengths > 0).sum())
        fixed = max(1, used // 4)
        passed = fixed + (places - fixed + rotation * (used - fixed)) % max(1, number_of - fixed)
        return jnp.zeros((number_of,), jnp.int32).at[order[jnp.where(places < fixed, places, passed)]].set(jnp.asarray(lengths, jnp.int32))

    lengths = jnp.where(number % 4 == 0, named(crowded, number // 4), named(usual, number - number // 4 - 1))
    mixed = jax.random.permutation(jax.random.fold_in(own, 3), number_of)
    source_of, receiver = mixed[0:number_of // 2 * 2:2], mixed[1:number_of // 2 * 2:2]
    room = jnp.minimum(lengths[source_of] - 1, reach - lengths[receiver]) // 2
    room = jnp.where((source_of == order[0]) | (receiver == order[0]) | (lengths[receiver] == 0), 0, jnp.maximum(room, 0))
    passed = jax.random.randint(jax.random.fold_in(own, 4), (number_of // 2,), 0, 1 << 20) % (room + 1)
    lengths = lengths.at[source_of].add(-passed).at[receiver].add(passed)
    items = jnp.searchsorted(jnp.cumsum(lengths), jnp.arange(rows * top), side="right").astype(jnp.int32)
    listing = items.reshape(top, rows).T
    listing = listing[jax.random.permutation(jax.random.fold_in(own, 1), rows)]
    rotation = jax.random.randint(jax.random.fold_in(own, 2), (rows, 1), 0, top)
    return jnp.take_along_axis(listing, (jnp.arange(top)[None, :] + rotation) % top, axis=1)


def load_shares(amount, total, limit, skew, full):
    loads = [(1 << 20) // math.isqrt(rank ** skew) + 1 for rank in range(1, amount + 1)]
    largest = limit if full else min(limit, max(-(-total // amount), total * loads[0] // sum(loads)))
    least = 1 if total - largest >= amount - 1 else 0
    holding, spare = [largest] + [least] * (amount - 1), total - largest - least * (amount - 1)
    while spare > 0:
        movable = [i for i in range(1, amount) if holding[i] < largest] or [i for i in range(1, amount) if holding[i] < limit]
        pool, remaining = sum([loads[i] for i in movable]), spare
        for i in movable:
            more = min(limit - holding[i], max(1, remaining * loads[i] // pool), spare)
            holding[i] = holding[i] + more
            spare = spare - more
    return np.array(holding)


def scatter_about(own_key, shape, deviation, reach, cuts=(), kind=jnp.bfloat16):
    entries = jax.random.normal(own_key, shape, jnp.float32) * deviation
    if len(cuts) > 0:
        entries = level_of(own_key, shape, cuts, -0.22, 0.18) * entries
    return jnp.clip(entries, min=-reach, max=reach).astype(kind)


def setup_inputs(seed: int = 0, part: int = 0) -> dict:
    key_of = jax.random.split(jax.random.key(seed), 11)
    part_splits = jax.random.split(jax.random.fold_in(key_of[10], part), 11)
    queries = draw_queries(jax.random.fold_in(jax.random.fold_in(key_of[10], part), 71), part)
    key_states = draw_key_states(jax.random.fold_in(jax.random.fold_in(key_of[10], part), 71), part)
    values = scatter_about(part_splits[2], (REQUEST_COUNT, REQUEST_TOKENS, KEY_VALUE_HEADS, HEAD_DIMENSION), 1.0, 6.0, ((0, 2), (1, 4), (2, 2)))
    doc_ids = jax.vmap(lambda own: jnp.searchsorted(jnp.cumsum(uneven(own, DOCS, REQUEST_TOKENS, REQUEST_TOKENS // 2, 0)), jnp.arange(REQUEST_TOKENS), side="right"))(jax.random.split(part_splits[3], REQUEST_COUNT)).reshape((REQUEST_COUNT, REQUEST_TOKENS)).astype(jnp.int32)
    residual = draw_residual(jax.random.fold_in(jax.random.fold_in(key_of[10], part), 71), part)
    out_proj = scatter_about(key_of[5], (QUERY_HEADS * HEAD_DIMENSION, D), (QUERY_HEADS * HEAD_DIMENSION) ** -0.5, 0.125, ((0, 2), (1, 4)))
    norm_gain = jnp.clip(1.0 + 0.1 * jax.random.normal(key_of[6], (D,), jnp.float32), 0.5, 1.5).astype(jnp.bfloat16)
    router = scatter_about(key_of[7], (D, EXPERTS), D ** -0.5, 0.078125, ((1, 2),))
    expert_ids_keys = jax.random.split(jax.random.fold_in(part_splits[8], 1), REQUEST_COUNT * REQUEST_TOKENS // (TOK_DEV // N_TP))
    expert_ids_turns = jax.random.permutation(jax.random.fold_in(part_splits[8], 3), REQUEST_COUNT * REQUEST_TOKENS // (TOK_DEV // N_TP))
    expert_ids = jax.vmap(lambda own, number: assign_block(jax.random.fold_in(part_splits[8], 2), own, number, TOK_DEV // N_TP, EXPERTS, 1, CAP, 2))(expert_ids_keys, expert_ids_turns).reshape((REQUEST_COUNT, REQUEST_TOKENS, 1))
    keep_counts = plant(jax.random.randint(part_splits[9], (EXPERTS,), 1, CAP + 1), jax.random.fold_in(part_splits[9], 1), 1, CAP).astype(jnp.int32)
    return dict(queries=queries, key_states=key_states, values=values, doc_ids=doc_ids, residual=residual, out_proj=out_proj, norm_gain=norm_gain, router=router, expert_ids=expert_ids, keep_counts=keep_counts)


EPSILON = 1e-05

def reference(queries, key_states, values, doc_ids, residual, out_proj, norm_gain, router, expert_ids, keep_counts):
    mixing_ratio = QUERY_HEADS // KEY_VALUE_HEADS
    scale = 1.0 / math.sqrt(HEAD_DIMENSION)
    position = jnp.arange(REQUEST_TOKENS, dtype=jnp.int32)

    def attend_head_group(flattened_index):
        request_number = flattened_index // KEY_VALUE_HEADS
        head_group = flattened_index % KEY_VALUE_HEADS
        query_rows = lax.dynamic_index_in_dim(queries, request_number, 0, False)
        query_rows = lax.dynamic_slice_in_dim(query_rows, head_group * mixing_ratio, mixing_ratio, 1)
        key_rows = lax.dynamic_index_in_dim(lax.dynamic_index_in_dim(key_states, request_number, 0, False), head_group, 1, False)
        value_rows = lax.dynamic_index_in_dim(lax.dynamic_index_in_dim(values, request_number, 0, False), head_group, 1, False)
        documents = lax.dynamic_index_in_dim(doc_ids, request_number, 0, False)
        scores = jnp.einsum('qrd,kd->rqk', query_rows.astype(jnp.float32), key_rows.astype(jnp.float32)) * scale
        allowed = (position[None, :] <= position[:, None]) & (documents[None, :] == documents[:, None])
        masked = jnp.where(allowed[None], scores, -jnp.inf)
        highest = lax.optimization_barrier(jnp.max(masked, axis=2, keepdims=True))
        weights = jnp.where(allowed[None], jnp.exp(scores - highest), 0.0)
        totals = lax.optimization_barrier(jnp.sum(weights, axis=2, keepdims=True))
        rounded = weights.astype(jnp.bfloat16).astype(jnp.float32)
        summed = jnp.einsum('rqk,kd->rqd', rounded, value_rows.astype(jnp.float32))
        return (summed / totals).astype(jnp.bfloat16)
    head_list = lax.map(attend_head_group, jnp.arange(REQUEST_COUNT * KEY_VALUE_HEADS, dtype=jnp.int32))
    blended_output = head_list.reshape(REQUEST_COUNT, KEY_VALUE_HEADS, mixing_ratio, REQUEST_TOKENS, HEAD_DIMENSION).transpose(0, 3, 1, 2, 4).reshape(REQUEST_COUNT * REQUEST_TOKENS, QUERY_HEADS * HEAD_DIMENSION)
    projected = jnp.dot(blended_output, out_proj, preferred_element_type=jnp.float32).reshape(REQUEST_COUNT, REQUEST_TOKENS, D)
    hidden = residual.astype(jnp.float32) + projected
    power = lax.optimization_barrier(jnp.mean(hidden * hidden, axis=2, keepdims=True))
    normed = (hidden * lax.rsqrt(power + EPSILON) * norm_gain.astype(jnp.float32)).astype(jnp.bfloat16)
    blocks = N_CTX * N_TP
    block_rows = TOK_DEV // N_TP
    normed_blocks = normed.reshape(REQUEST_COUNT, blocks, block_rows, D)
    id_blocks = expert_ids.reshape(REQUEST_COUNT, blocks, block_rows)
    expert_iota = jnp.arange(EXPERTS, dtype=jnp.int32)
    slot_iota = jnp.arange(EXPERTS * CAP, dtype=jnp.int32)
    router_wide = router.astype(jnp.float32)

    def route_block(flattened_index):
        block = flattened_index // REQUEST_COUNT
        request_number = flattened_index % REQUEST_COUNT
        token_rows = lax.dynamic_index_in_dim(lax.dynamic_index_in_dim(normed_blocks, request_number, 0, False), block, 0, False)
        chosen = lax.dynamic_index_in_dim(lax.dynamic_index_in_dim(id_blocks, request_number, 0, False), block, 0, False)
        onehot = (chosen[:, None] == expert_iota[None, :]).astype(jnp.int32)
        earlier = jnp.cumsum(onehot, axis=0) - onehot
        ranking = lax.optimization_barrier(jnp.sum(onehot * earlier, axis=1))
        limits = lax.optimization_barrier(jnp.sum(onehot * keep_counts[None, :], axis=1))
        kept = ranking < limits
        target = chosen * CAP + ranking
        table = (slot_iota[:, None] == target[None, :]) & kept[None, :]
        slots = jnp.dot(table.astype(jnp.bfloat16), token_rows, preferred_element_type=jnp.float32)
        slots = slots.astype(jnp.bfloat16).astype(jnp.float32).reshape(EXPERTS, CAP, D)
        logits = jnp.einsum('ecd,de->ec', slots, router_wide)
        return (slots * jax.nn.sigmoid(logits)[..., None]).astype(jnp.bfloat16)
    return lax.map(route_block, jnp.arange(blocks * REQUEST_COUNT, dtype=jnp.int32))
```

```python
import functools
import math

import jax
import jax.numpy as jnp
from jax import lax
from jax.experimental import pallas as pl
from jax.experimental.pallas import tpu as pltpu
from jax.sharding import PartitionSpec as P

CAP = 2
EPSILON = 1e-05
MESH = pl.DeviceIdType.MESH


def kernel(
    sizes,
    q_hbm,
    key_hbm,
    value_hbm,
    doc_hbm,
    residual_hbm,
    weight_hbm,
    gain_hbm,
    router_hbm,
    ids_hbm,
    keep_hbm,
    slot_in,
    scale_ref,
    q_ref,
    key_ref,
    value_ref,
    doc_ref,
    gain_ref,
    router_ref,
    ids_ref,
    keep_ref,
    kv_out,
    kv_in,
    routed,
    tally,
    logits,
    doc_in,
    attn,
    weight,
    residual,
    product,
    part_out,
    part_in,
    res_out,
    res_in,
    slot_out,
    load_sem,
    kv_send,
    kv_recv,
    doc_send,
    doc_recv,
    right_send,
    left_send,
    attn_recv,
    part_send,
    part_recv,
    res_send,
    res_recv,
    slot_send,
    slot_recv,
):
    ctx_count, exp_count, back, pieces = sizes
    heads, tokens, size = q_ref.shape
    groups = kv_out.shape[0]
    ratio = heads // groups
    half = tokens // 2
    columns = weight.shape[1]
    depth = weight.shape[0] // groups
    slots = slot_out.shape[3]
    part = columns // pieces
    width = columns * ctx_count
    aligned = part % 128 == 0
    me = lax.axis_index("ctx")
    mine = lax.axis_index("exp")
    core = lax.axis_index("tp")

    barrier = pltpu.get_barrier_semaphore()
    for shift in range(1, ctx_count):
        pl.semaphore_signal(
            barrier,
            inc=1,
            device_id={"ctx": lax.rem(me + shift, ctx_count)},
            device_id_type=MESH,
        )
    for shift in range(1, exp_count):
        pl.semaphore_signal(
            barrier,
            inc=1,
            device_id={"exp": lax.rem(mine + shift, exp_count)},
            device_id_type=MESH,
        )
    pl.semaphore_signal(barrier, inc=1, device_id={"tp": 1 - core}, device_id_type=MESH)

    loads = {}

    def load(name, source, target):
        loads[name] = pltpu.make_async_copy(source, target, load_sem.at[len(loads)])
        loads[name].start()

    load("key", key_hbm, key_ref)
    load("value", value_hbm, value_ref)
    load("doc", doc_hbm, doc_ref)
    load("query", q_hbm, q_ref)
    load("ids", ids_hbm, ids_ref)
    load("keep", keep_hbm, keep_ref)
    load("gain", gain_hbm, gain_ref)
    load("router", router_hbm, router_ref)
    load("weight", weight_hbm, weight)
    for block in range(ctx_count):
        there = slice(block * columns, (block + 1) * columns)
        load(
            block,
            residual_hbm.at[:, there] if columns % 128 == 0 else residual_hbm.at[block],
            residual.at[block],
        )

    loads["key"].wait()
    loads["value"].wait()
    for group in range(groups):
        kv_out[group, 0] = key_ref[:, group, :]
        kv_out[group, 1] = value_ref[:, group, :]
    loads["doc"].wait()

    pl.semaphore_wait(barrier, ctx_count + exp_count - 1)

    def kv_copy(group, shift):
        return pltpu.make_async_remote_copy(
            src_ref=kv_out.at[group] if shift == 1 else kv_in.at[group, shift - 2],
            dst_ref=kv_in.at[group, shift - 1],
            send_sem=kv_send.at[group, shift - 1],
            recv_sem=kv_recv.at[group, shift - 1],
            device_id={"ctx": lax.rem(me + 1, ctx_count)},
            device_id_type=MESH,
        )

    def doc_copy(shift):
        return pltpu.make_async_remote_copy(
            src_ref=doc_ref,
            dst_ref=doc_in.at[shift - 1],
            send_sem=doc_send.at[shift - 1],
            recv_sem=doc_recv.at[shift - 1],
            device_id={"ctx": lax.rem(me + shift, ctx_count)},
            device_id_type=MESH,
        )

    @pl.when(me < ctx_count - 1)
    def _():
        for group in range(groups):
            kv_copy(group, 1).start()

    for shift in range(1, back + 1):

        @pl.when(me + shift < ctx_count)
        def _(shift=shift):
            doc_copy(shift).start()

    for shift in range(1, back + 1):

        @pl.when(me < shift)
        def _(shift=shift):
            doc_in[shift - 1] = jnp.full(doc_in.shape[1:], -1, jnp.int32)
            for group in range(groups):
                kv_in[group, shift - 1] = jnp.zeros(kv_in.shape[2:], kv_in.dtype)

    def kv_arrive(group, shift):
        @pl.when(me >= shift)
        def _():
            kv_copy(group, shift).wait_recv()
            if shift < back:

                @pl.when(me < ctx_count - 1)
                def _():
                    kv_copy(group, shift + 1).start()

    loads["ids"].wait()
    loads["keep"].wait()
    row = lax.broadcasted_iota(jnp.int32, (half, half), 0)
    lane = lax.broadcasted_iota(jnp.int32, (half, half), 1)
    ids_row = ids_ref[...]
    ids_column = jnp.sum(jnp.where(row == lane, ids_row, 0), axis=1, keepdims=True)
    ranking = jnp.sum(
        jnp.where((ids_column == ids_row) & (row < lane), 1, 0), axis=0, keepdims=True
    )
    experts = keep_ref.shape[1]
    square_row = lax.broadcasted_iota(jnp.int32, (experts, experts), 0)
    square_lane = lax.broadcasted_iota(jnp.int32, (experts, experts), 1)
    keep_column = jnp.sum(
        jnp.where(square_row == square_lane, keep_ref[...], 0), axis=1, keepdims=True
    )
    expert_row = lax.broadcasted_iota(jnp.int32, (experts, half), 0)
    limits = jnp.sum(jnp.where(expert_row == ids_row, keep_column, 0), axis=0, keepdims=True)
    target = jnp.where(ranking < limits, ids_row * CAP + ranking, -1)
    slot_row = lax.broadcasted_iota(jnp.int32, (slots, half), 0)

    for shift in range(1, back):
        for group in range(groups):
            kv_arrive(group, shift)

    for shift in range(1, back + 1):

        @pl.when(me >= shift)
        def _(shift=shift):
            doc_copy(shift).wait_recv()

    square = lax.broadcasted_iota(jnp.int32, (tokens, tokens), 0)
    across = lax.broadcasted_iota(jnp.int32, (tokens, tokens), 1)
    doc_row = doc_ref[...]
    doc_column = jnp.sum(jnp.where(square == across, doc_row, 0), axis=1, keepdims=True)
    allowed = [(across <= square) & (doc_row == doc_column)]
    for shift in range(1, back + 1):
        allowed.append(doc_in[shift - 1] == doc_column)
    allowed = jnp.concatenate(
        [jnp.where(piece, 1.0, 0.0) for piece in allowed], axis=1
    )
    allowed = allowed > 0.5
    scale = 1.0 / math.sqrt(size)
    loads["query"].wait()

    def attn_copy(block, group, rightward):
        to = me + 1 if rightward else me - 1
        sends = right_send if rightward else left_send
        return pltpu.make_async_remote_copy(
            src_ref=attn.at[block, group],
            dst_ref=attn.at[block, group],
            send_sem=sends.at[block, group],
            recv_sem=attn_recv.at[block, group],
            device_id={"ctx": lax.rem(to + ctx_count, ctx_count)},
            device_id_type=MESH,
        )

    for group in range(groups):
        if back:
            kv_arrive(group, back)
        keys = jnp.concatenate(
            [kv_out[group, 0]] + [kv_in[group, shift, 0] for shift in range(back)], axis=0
        )
        vals = jnp.concatenate(
            [kv_out[group, 1]] + [kv_in[group, shift, 1] for shift in range(back)], axis=0
        )
        for head in range(ratio):
            scores = (
                lax.dot_general(
                    q_ref[group * ratio + head],
                    keys,
                    (((1,), (1,)), ((), ())),
                    preferred_element_type=jnp.float32,
                )
                * scale
            )
            masked = jnp.where(allowed, scores, -1e30)
            highest = jnp.max(masked, axis=1, keepdims=True)
            weights = jnp.where(allowed, jnp.exp(masked - highest), 0.0)
            totals = jnp.sum(weights, axis=1, keepdims=True)
            mixed = jnp.dot(weights.astype(jnp.bfloat16), vals, preferred_element_type=jnp.float32)
            attn[me, group, :, head * size : (head + 1) * size] = (mixed / totals).astype(
                jnp.bfloat16
            )

        @pl.when(me < ctx_count - 1)
        def _(group=group):
            attn_copy(me, group, True).start()

        @pl.when(me > 0)
        def _(group=group):
            attn_copy(me, group, False).start()

    def part_copy(block, piece):
        return pltpu.make_async_remote_copy(
            src_ref=part_out.at[block, piece],
            dst_ref=part_in.at[block, piece],
            send_sem=part_send.at[block, piece],
            recv_sem=part_recv.at[block, piece],
            device_id={"tp": 1 - core},
            device_id_type=MESH,
        )

    def res_copy(block, peer, piece):
        return pltpu.make_async_remote_copy(
            src_ref=res_out.at[block, piece],
            dst_ref=res_in.at[me, piece],
            send_sem=res_send.at[block, piece],
            recv_sem=res_recv.at[peer, piece],
            device_id={"ctx": block},
            device_id_type=MESH,
        )

    def slot_at(peer, block, piece):
        if aligned:
            first = pl.multiple_of(block * columns + piece * part, 128)
            return slot_in.at[peer, :, pl.ds(first, part)]
        return slot_in.at[peer, block, piece]

    def slot_copy(shift, block, peer, piece):
        return pltpu.make_async_remote_copy(
            src_ref=slot_out.at[shift - 1, block, piece],
            dst_ref=slot_at(mine, block, piece),
            send_sem=slot_send.at[shift - 1, block, piece],
            recv_sem=slot_recv.at[peer, block, piece],
            device_id={"exp": lax.rem(mine + shift, exp_count)},
            device_id_type=MESH,
        )

    def project(block, group):
        for piece in range(pieces):
            there = slice(piece * part, (piece + 1) * part)
            term = jnp.dot(
                attn[block, group],
                weight[group * depth : (group + 1) * depth, there],
                preferred_element_type=jnp.float32,
            )
            for side in range(2):
                rows = term[side * half : (side + 1) * half]
                if group:
                    rows = rows + product[block, piece, side]
                product[block, piece, side] = rows
            if group == groups - 1:
                part_out[block, piece] = product[block, piece, 1 - core].astype(jnp.bfloat16)
                part_copy(block, piece).start()

    def finish(block, piece):
        part_copy(block, piece).wait_recv()
        return (
            product[block, piece, core] + part_in[block, piece].astype(jnp.float32)
        ).astype(jnp.bfloat16)

    def send(block):
        for piece in range(pieces):
            res_copy(block, me, piece).start()

    def send_all(count, sign):
        def body(distance, carry):
            send(me + sign * distance)
            return carry

        lax.fori_loop(1, count + 1, body, 0)

    def place(block, piece):
        hidden = (
            residual[block, :, piece * part : (piece + 1) * part].astype(jnp.float32)
            + res_in[block, piece].astype(jnp.float32)
        ).astype(jnp.bfloat16)
        for shift in (*range(1, exp_count), 0):
            peer = lax.rem(mine + shift, exp_count)
            table = (slot_row + peer * slots == target).astype(jnp.bfloat16)
            chosen = jnp.dot(table, hidden, preferred_element_type=jnp.float32).astype(
                jnp.bfloat16
            )
            if shift == 0:
                slot_at(mine, block, piece)[...] = chosen
            else:
                slot_out[shift - 1, block, piece] = chosen
                slot_copy(shift, block, mine, piece).start()

    def absorb(shift, block):
        peer = lax.rem(mine + shift, exp_count)
        for piece in range(pieces):
            if shift:
                slot_copy(1, block, peer, piece).wait_recv()
            hidden = slot_at(peer, block, piece)[...]
            if aligned:
                first = pl.multiple_of(block * columns + piece * part, 128)
                columns_here = routed[:, pl.ds(first, part)]
            else:
                columns_here = routed[block, piece]
            logits[shift] += lax.dot_general(
                hidden,
                columns_here,
                (((1,), (1,)), ((), ())),
                preferred_element_type=jnp.float32,
            )
            wide = hidden.astype(jnp.float32)
            wide = wide * wide
            if aligned:
                total = wide[:, :128]
                for first in range(128, part, 128):
                    total = total + wide[:, first : first + 128]
                tally[shift] += total
            else:
                tally[shift, :, :1] += jnp.sum(wide, axis=1, keepdims=True)

    loads["weight"].wait()
    for group in range(groups):
        project(me, group)

    loads["gain"].wait()
    loads["router"].wait()
    wide = gain_ref[...].astype(jnp.float32)
    for line in range(wide.shape[0]):
        there = slice(line * 128, (line + 1) * 128)
        router_ref[:, there] = (
            router_ref[:, there].astype(jnp.float32) * wide[line : line + 1]
        ).astype(jnp.bfloat16)
    if not aligned:
        for block in range(ctx_count):
            for piece in range(pieces):
                first = block * columns + piece * part
                routed[block, piece] = router_ref[:, first : first + part]
    else:
        routed = router_ref
    tally[...] = jnp.zeros_like(tally)
    logits[...] = jnp.zeros_like(logits)
    for block in range(ctx_count):
        loads[block].wait()

    rest = ctx_count - 1 - me

    def step(distance, carry):
        left, right = me - distance, me + distance
        has_left, has_right = left >= 0, right < ctx_count

        for group in range(groups):

            @pl.when(has_left)
            def _():
                attn_copy(left, group, True).wait_recv()

                @pl.when(me < ctx_count - 1)
                def _():
                    attn_copy(left, group, True).start()

            @pl.when(has_right)
            def _():
                attn_copy(right, group, False).wait_recv()

                @pl.when(me > 0)
                def _():
                    attn_copy(right, group, False).start()

            for block, has in ((left, has_left), (right, has_right)):

                @pl.when(has)
                def _(block=block):
                    project(block, group)

        for block, has in ((left, has_left), (right, has_right)):

            @pl.when(has)
            def _(block=block):
                for piece in range(pieces):
                    res_out[block, piece] = finish(block, piece)

        @pl.when(has_right & (distance > me))
        def _():
            send(right)

        @pl.when(distance == me)
        def _():
            send_all(jnp.minimum(me, rest), 1)

        @pl.when(has_left & (distance > rest))
        def _():
            send(left)

        @pl.when(distance == rest)
        def _():
            send_all(jnp.minimum(me, rest), -1)

        @pl.when(distance == 1)
        def _():
            for piece in range(pieces):
                res_in[me, piece] = finish(me, piece)
                place(me, piece)
            absorb(0, me)

        return carry

    lax.fori_loop(1, ctx_count, step, 0)

    def settle(distance, carry):
        for block, has in (
            (me - distance, (me >= distance) & (distance < ctx_count)),
            (me + distance, me + distance < ctx_count),
        ):

            @pl.when(has)
            def _(block=block):
                for piece in range(pieces):
                    res_copy(me, block, piece).wait_recv()
                    place(block, piece)
                absorb(0, block)

        last = distance - 1
        for block, has in (
            (me - last, me >= last),
            (me + last, (me + last < ctx_count) & (last > 0)),
        ):

            @pl.when(has)
            def _(block=block):
                for shift in range(1, exp_count):
                    absorb(shift, block)

        return carry

    lax.fori_loop(1, ctx_count + 1, settle, 0)

    spread = lax.broadcasted_iota(jnp.int32, logits.shape[1:], 0) // CAP
    expert = lax.broadcasted_iota(jnp.int32, logits.shape[1:], 1)
    for shift in range(exp_count):
        peer = lax.rem(mine + shift, exp_count)
        power = tally[shift] if aligned else tally[shift, :, :1]
        power = jnp.sum(power, axis=1, keepdims=True) / width
        factor = lax.rsqrt(power + EPSILON)
        logit = jnp.sum(jnp.where(spread == expert, logits[shift], 0.0), axis=1, keepdims=True)
        gate = jax.nn.sigmoid(logit * factor)
        scale_ref[peer] = jnp.broadcast_to(gate * factor, scale_ref.shape[1:])

    @pl.when(me < ctx_count - 1)
    def _():
        for group in range(groups):
            kv_copy(group, 1).wait_send()
            for shift in range(1, back):

                @pl.when(me >= shift)
                def _(group=group, shift=shift):
                    kv_copy(group, shift + 1).wait_send()

    for shift in range(1, back + 1):

        @pl.when(me + shift < ctx_count)
        def _(shift=shift):
            doc_copy(shift).wait_send()

    def drain(block, carry):
        for piece in range(pieces):
            part_copy(block, piece).wait_send()
            for shift in range(1, exp_count):
                slot_copy(shift, block, mine, piece).wait_send()

        @pl.when(block != me)
        def _():
            for piece in range(pieces):
                res_copy(block, me, piece).wait_send()

        for group in range(groups):

            @pl.when((block <= me) & (me < ctx_count - 1))
            def _(group=group):
                attn_copy(block, group, True).wait_send()

            @pl.when((block >= me) & (me > 0))
            def _(group=group):
                attn_copy(block, group, False).wait_send()

        return carry

    lax.fori_loop(0, ctx_count, drain, 0)


def on_device(
    queries,
    key_states,
    values,
    doc_ids,
    residual,
    out_proj,
    norm_gain,
    router,
    expert_ids,
    keep_counts,
):
    tokens, heads, size = queries.shape[1:]
    groups = key_states.shape[2]
    ctx_count = lax.axis_size("ctx")
    exp_count = lax.axis_size("exp")
    features, columns = out_proj.shape
    half = residual.shape[1]
    width = residual.shape[2]
    experts = keep_counts.shape[0]
    owned = experts // exp_count
    slots = owned * CAP
    longest = tokens * ctx_count // 2
    back = min(ctx_count - 1, -(-(longest - 1) // tokens))
    pieces = columns // 256 if columns % 256 == 0 else 2
    part = columns // pieces
    aligned = part % 128 == 0
    vmem = pl.BlockSpec(memory_space=pltpu.VMEM)
    hbm = pl.BlockSpec(memory_space=pltpu.HBM)
    bf16, f32, i32 = jnp.bfloat16, jnp.float32, jnp.int32
    dma = pltpu.SemaphoreType.DMA
    n = ctx_count
    stream = residual[0]
    if columns % 128:
        stream = stream.reshape(half, ctx_count, columns).transpose(1, 0, 2)
    slot_shape = (exp_count, slots, width) if aligned else (exp_count, n, pieces, slots, part)
    chosen, scale = pl.pallas_call(
        functools.partial(kernel, (ctx_count, exp_count, back, pieces)),
        out_shape=(
            jax.ShapeDtypeStruct(slot_shape, bf16),
            jax.ShapeDtypeStruct((exp_count, slots, 128), f32),
        ),
        in_specs=[hbm] * 10,
        out_specs=(vmem, vmem),
        scratch_shapes=[
            pltpu.VMEM((heads, tokens, size), bf16),
            pltpu.VMEM((tokens, groups, size), bf16),
            pltpu.VMEM((tokens, groups, size), bf16),
            pltpu.VMEM((1, tokens), i32),
            pltpu.VMEM((width // 128, 128), bf16),
            pltpu.VMEM((owned, width), bf16),
            pltpu.VMEM((1, half), i32),
            pltpu.VMEM((1, experts), i32),
            pltpu.VMEM((groups, 2, tokens, size), bf16),
            pltpu.VMEM((groups, back, 2, tokens, size), bf16),
            pltpu.VMEM((8, 128) if aligned else (n, pieces, owned, part), bf16),
            pltpu.VMEM((exp_count, slots, 128), f32),
            pltpu.VMEM((exp_count, slots, owned), f32),
            pltpu.VMEM((back, 1, tokens), i32),
            pltpu.VMEM((n, groups, tokens, features // groups), bf16),
            pltpu.VMEM((features, columns), bf16),
            pltpu.VMEM((n, half, columns), bf16),
            pltpu.VMEM((n, pieces, 2, half, part), f32),
            pltpu.VMEM((n, pieces, half, part), bf16),
            pltpu.VMEM((n, pieces, half, part), bf16),
            pltpu.VMEM((n, pieces, half, part), bf16),
            pltpu.VMEM((n, pieces, half, part), bf16),
            pltpu.VMEM((exp_count - 1, n, pieces, slots, part), bf16),
            dma((9 + n,)),
            dma((groups, back)),
            dma((groups, back)),
            dma((back,)),
            dma((back,)),
            dma((n, groups)),
            dma((n, groups)),
            dma((n, groups)),
            dma((n, pieces)),
            dma((n, pieces)),
            dma((n, pieces)),
            dma((n, pieces)),
            dma((exp_count - 1, n, pieces)),
            dma((exp_count, n, pieces)),
        ],
        compiler_params=pltpu.CompilerParams(
            collective_id=0, has_side_effects=True, vmem_limit_bytes=40 << 20
        ),
    )(
        *(
            pltpu.with_memory_space_constraint(operand, pltpu.HBM)
            for operand in (
                queries[0].transpose(1, 0, 2),
                key_states[0],
                values[0],
                doc_ids,
                stream,
                out_proj,
                norm_gain.reshape(width // 128, 128),
                router.T,
                expert_ids.reshape(1, half),
                keep_counts.reshape(1, experts),
            )
        )
    )
    if not aligned:
        chosen = chosen.transpose(0, 3, 1, 2, 4).reshape(exp_count, slots, width)
    scaled = chosen.astype(f32) * scale[:, :, :1] * norm_gain.astype(f32)
    return scaled.astype(bf16).reshape(exp_count, owned, CAP, width)


def solution(mesh):
    placed = (
        P(("groups", "exp"), "ctx", "tp", None),
        P(("groups", "exp"), "ctx", "tp", None),
        P(("groups", "exp"), "ctx", "tp", None),
        P(("groups", "exp"), "ctx"),
        P(("groups", "exp"), ("ctx", "tp"), None),
        P("tp", "ctx"),
        P(),
        P(None, "exp"),
        P(("groups", "exp"), ("ctx", "tp"), None),
        P("groups"),
    )
    return jax.shard_map(
        on_device,
        mesh=mesh,
        in_specs=placed,
        out_specs=P(("groups", "ctx", "tp"), "exp", None, None),
        check_vma=False,
    )
```

```python
import functools
import math

import jax
import jax.numpy as jnp
from jax import lax
from jax.experimental import pallas as pl
from jax.experimental.pallas import tpu as pltpu
from jax.sharding import PartitionSpec as P

CAP = 2
EPSILON = 1e-05
LAG = 0
SLOT_LAG = 2
WIDE = 5
MESH = pl.DeviceIdType.MESH


def kernel(
    sizes,
    q_hbm,
    key_hbm,
    value_hbm,
    doc_hbm,
    residual_hbm,
    weight_hbm,
    gain_hbm,
    router_hbm,
    ids_hbm,
    keep_hbm,
    slot_in,
    scale_ref,
    gain_row,
    q_ref,
    key_ref,
    value_ref,
    doc_ref,
    gain_ref,
    router_ref,
    ids_ref,
    keep_ref,
    kv_out,
    kv_in,
    kv_next,
    q_next,
    doc_next,
    routed,
    tally,
    logits,
    doc_in,
    attn,
    weight,
    residual,
    product,
    part_out,
    part_in,
    res_out,
    res_in,
    slot_out,
    load_sem,
    kv_send,
    kv_recv,
    doc_send,
    doc_recv,
    next_send,
    next_recv,
    right_send,
    left_send,
    attn_recv,
    part_send,
    part_recv,
    res_send,
    res_recv,
    slot_send,
    slot_recv,
):
    ctx_count, exp_count, back, pieces = sizes
    heads, tokens, size = q_ref.shape
    groups = kv_out.shape[0]
    ratio = heads // groups
    half = tokens // 2
    columns = weight.shape[1]
    depth = weight.shape[0] // groups
    slots = slot_out.shape[3]
    part = columns // pieces
    width = columns * ctx_count
    aligned = part % 128 == 0
    me = lax.axis_index("ctx")
    mine = lax.axis_index("exp")
    core = lax.axis_index("tp")
    rest = ctx_count - 1 - me

    barrier = pltpu.get_barrier_semaphore()
    for shift in range(1, ctx_count):
        pl.semaphore_signal(
            barrier,
            inc=1,
            device_id={"ctx": lax.rem(me + shift, ctx_count)},
            device_id_type=MESH,
        )
    for shift in range(1, exp_count):
        pl.semaphore_signal(
            barrier,
            inc=1,
            device_id={"exp": lax.rem(mine + shift, exp_count)},
            device_id_type=MESH,
        )
    pl.semaphore_signal(barrier, inc=1, device_id={"tp": 1 - core}, device_id_type=MESH)

    loads = {}

    def load(name, source, target):
        loads[name] = pltpu.make_async_copy(source, target, load_sem.at[len(loads)])
        loads[name].start()

    load("key", key_hbm, key_ref)
    load("value", value_hbm, value_ref)
    load("doc", doc_hbm, doc_ref)
    load("query", q_hbm, q_ref)
    load("ids", ids_hbm, ids_ref)
    load("keep", keep_hbm, keep_ref)
    load("gain", gain_hbm, gain_ref)
    load("router", router_hbm, router_ref)
    load("weight", weight_hbm, weight)
    for block in range(ctx_count):
        there = slice(block * columns, (block + 1) * columns)
        load(
            block,
            residual_hbm.at[:, there] if columns % 128 == 0 else residual_hbm.at[block],
            residual.at[block],
        )

    loads["key"].wait()
    loads["value"].wait()
    for group in range(groups):
        kv_out[group, 0] = key_ref[:, group, :]
        kv_out[group, 1] = value_ref[:, group, :]
    loads["doc"].wait()

    pl.semaphore_wait(barrier, ctx_count + exp_count - 1)

    def kv_copy(group, shift):
        return pltpu.make_async_remote_copy(
            src_ref=kv_out.at[group] if shift == 1 else kv_in.at[group, shift - 2],
            dst_ref=kv_in.at[group, shift - 1],
            send_sem=kv_send.at[group, shift - 1],
            recv_sem=kv_recv.at[group, shift - 1],
            device_id={"ctx": lax.rem(me + 1, ctx_count)},
            device_id_type=MESH,
        )

    def doc_copy(shift):
        return pltpu.make_async_remote_copy(
            src_ref=doc_ref,
            dst_ref=doc_in.at[shift - 1],
            send_sem=doc_send.at[shift - 1],
            recv_sem=doc_recv.at[shift - 1],
            device_id={"ctx": lax.rem(me + shift, ctx_count)},
            device_id_type=MESH,
        )

    def next_copy(source, target, index):
        return pltpu.make_async_remote_copy(
            src_ref=source,
            dst_ref=target,
            send_sem=next_send.at[index],
            recv_sem=next_recv.at[index],
            device_id={"ctx": lax.rem(me + ctx_count - 1, ctx_count)},
            device_id_type=MESH,
        )

    def next_doc():
        return next_copy(doc_ref, doc_next, 2 * groups)

    def next_kv(group):
        return next_copy(kv_out.at[group], kv_next.at[group], 2 * group)

    def next_query(group):
        these = pl.ds(group * ratio, ratio)
        return next_copy(q_ref.at[these], q_next.at[these], 2 * group + 1)

    for shift in range(1, back + 1):

        @pl.when(me + shift < ctx_count)
        def _(shift=shift):
            doc_copy(shift).start()

    @pl.when(me < ctx_count - 1)
    def _():
        for group in range(groups):
            kv_copy(group, 1).start()

    loads["query"].wait()

    @pl.when(me > 0)
    def _():
        next_doc().start()
        for group in range(groups):
            next_kv(group).start()
            next_query(group).start()

    for shift in range(1, back + 1):

        @pl.when(me < shift)
        def _(shift=shift):
            doc_in[shift - 1] = jnp.full(doc_in.shape[1:], -1, jnp.int32)
            for group in range(groups):
                kv_in[group, shift - 1] = jnp.zeros(kv_in.shape[2:], kv_in.dtype)

    def kv_arrive(group, shift):
        @pl.when(me >= shift)
        def _():
            kv_copy(group, shift).wait_recv()
            if shift < back:

                @pl.when(me < ctx_count - 1)
                def _():
                    kv_copy(group, shift + 1).start()

    loads["ids"].wait()
    loads["keep"].wait()
    row = lax.broadcasted_iota(jnp.int32, (half, half), 0)
    lane = lax.broadcasted_iota(jnp.int32, (half, half), 1)
    ids_row = ids_ref[...]
    ids_column = jnp.sum(jnp.where(row == lane, ids_row, 0), axis=1, keepdims=True)
    ranking = jnp.sum(
        jnp.where((ids_column == ids_row) & (row < lane), 1, 0), axis=0, keepdims=True
    )
    experts = keep_ref.shape[1]
    square_row = lax.broadcasted_iota(jnp.int32, (experts, experts), 0)
    square_lane = lax.broadcasted_iota(jnp.int32, (experts, experts), 1)
    keep_column = jnp.sum(
        jnp.where(square_row == square_lane, keep_ref[...], 0), axis=1, keepdims=True
    )
    expert_row = lax.broadcasted_iota(jnp.int32, (experts, half), 0)
    limits = jnp.sum(jnp.where(expert_row == ids_row, keep_column, 0), axis=0, keepdims=True)
    target = jnp.where(ranking < limits, ids_row * CAP + ranking, -1)
    slot_row = lax.broadcasted_iota(jnp.int32, (slots, half), 0)

    for shift in range(1, back):
        for group in range(groups):
            kv_arrive(group, shift)

    for shift in range(1, back + 1):

        @pl.when(me >= shift)
        def _(shift=shift):
            doc_copy(shift).wait_recv()

    square = lax.broadcasted_iota(jnp.int32, (tokens, tokens), 0)
    across = lax.broadcasted_iota(jnp.int32, (tokens, tokens), 1)
    scale = 1.0 / math.sqrt(size)

    def visible(doc_row, earlier):
        doc_column = jnp.sum(jnp.where(square == across, doc_row, 0), axis=1, keepdims=True)
        masks = [(across <= square) & (doc_row == doc_column)]
        masks += [other == doc_column for other in earlier]
        return jnp.concatenate([jnp.where(mask, 1.0, 0.0) for mask in masks], axis=1) > 0.5

    def attend(block, group, allowed, query, pairs):
        keys = jnp.concatenate([pair[0] for pair in pairs], axis=0)
        vals = jnp.concatenate([pair[1] for pair in pairs], axis=0)
        count = keys.shape[0]
        stacked = query[group * ratio : (group + 1) * ratio].reshape(ratio * tokens, size)
        scores = lax.dot_general(
            stacked, keys, (((1,), (1,)), ((), ())), preferred_element_type=jnp.float32
        ).reshape(ratio, tokens, count)
        masked = jnp.where(allowed[None], scores * scale, -1e30)
        highest = jnp.max(masked, axis=2, keepdims=True)
        weights = jnp.exp(masked - highest)
        totals = jnp.sum(weights, axis=2, keepdims=True)
        mixed = jnp.dot(
            weights.astype(jnp.bfloat16).reshape(ratio * tokens, count),
            vals,
            preferred_element_type=jnp.float32,
        ).reshape(ratio, tokens, size)
        mixed = (mixed / totals).astype(jnp.bfloat16)
        for head in range(ratio):
            attn[block, group, :, head * size : (head + 1) * size] = mixed[head]

    def attn_copy(block, group, rightward):
        to = me + 1 if rightward else me - 1
        sends = right_send if rightward else left_send
        return pltpu.make_async_remote_copy(
            src_ref=attn.at[block, group],
            dst_ref=attn.at[block, group],
            send_sem=sends.at[block, group],
            recv_sem=attn_recv.at[block, group],
            device_id={"ctx": lax.rem(to + ctx_count, ctx_count)},
            device_id_type=MESH,
        )

    allowed = visible(doc_ref[...], [doc_in[shift] for shift in range(back)])
    for group in range(groups):
        if back:
            kv_arrive(group, back)
        attend(
            me,
            group,
            allowed,
            q_ref,
            [kv_out.at[group]] + [kv_in.at[group, shift] for shift in range(back)],
        )
        early = group < groups - 1

        @pl.when((me < ctx_count - 1) & (early | (me == 0)))
        def _(group=group):
            attn_copy(me, group, True).start()

    def item(turn, count):
        order = turn - 1
        spot = jnp.where(count > 0, lax.rem(order, jnp.maximum(count, 1)), 0)
        group = sum((order >= count * number).astype(jnp.int32) for number in range(1, groups))
        group = group if groups > 1 else jnp.int32(0)
        final = group == groups - 1
        active = (turn >= 1) & (turn <= groups * count)
        return group, jnp.where(final, count - spot, spot + 1), final, active

    beyond = jnp.maximum(rest - 1, 0)

    def from_left(turn):
        group, far, final, active = item(turn, me)
        block = me - far

        @pl.when(active)
        def _():
            attn_copy(block, group, True).wait_recv()

            @pl.when(me < ctx_count - 1)
            def _():
                attn_copy(block, group, True).start()

                @pl.when(turn == groups * me)
                def _():
                    attn_copy(me, groups - 1, True).start()

        return block, active & final

    def from_right(turn):
        group = lax.rem(turn - 1, groups)
        block = me + 2 + (turn - 1) // groups
        final, active = group == groups - 1, turn <= groups * beyond

        @pl.when(active)
        def _():
            attn_copy(block, group, False).wait_recv()

            @pl.when(me > 0)
            def _():
                attn_copy(block, group, False).start()

        return block, active & final

    from_left(1)

    @pl.when(rest > 0)
    def _():
        next_doc().wait_recv()
        allowed = visible(
            doc_next[...],
            ([doc_ref[...]] if back else []) + [doc_in[shift] for shift in range(back - 1)],
        )
        for group in range(groups):
            next_kv(group).wait_recv()
            next_query(group).wait_recv()
            attend(
                me + 1,
                group,
                allowed,
                q_next,
                [kv_next.at[group]]
                + ([kv_out.at[group]] if back else [])
                + [kv_in.at[group, shift] for shift in range(back - 1)],
            )
            @pl.when(me > 0)
            def _(group=group):
                attn_copy(me + 1, group, False).start()

    def part_copy(block, piece):
        return pltpu.make_async_remote_copy(
            src_ref=part_out.at[block, piece],
            dst_ref=part_in.at[block, piece],
            send_sem=part_send.at[block, piece],
            recv_sem=part_recv.at[block, piece],
            device_id={"tp": 1 - core},
            device_id_type=MESH,
        )

    def res_copy(block, peer, piece):
        return pltpu.make_async_remote_copy(
            src_ref=res_out.at[block, piece],
            dst_ref=res_in.at[me, piece],
            send_sem=res_send.at[block, piece],
            recv_sem=res_recv.at[peer, piece],
            device_id={"ctx": block},
            device_id_type=MESH,
        )

    def slot_at(peer, block, piece):
        if aligned:
            first = pl.multiple_of(block * columns + piece * part, 128)
            return slot_in.at[peer, :, pl.ds(first, part)]
        return slot_in.at[peer, block, piece]

    def slot_copy(shift, block, peer, piece):
        return pltpu.make_async_remote_copy(
            src_ref=slot_out.at[shift - 1, block, piece],
            dst_ref=slot_at(mine, block, piece),
            send_sem=slot_send.at[shift - 1, block, piece],
            recv_sem=slot_recv.at[peer, block, piece],
            device_id={"exp": lax.rem(mine + shift, exp_count)},
            device_id_type=MESH,
        )

    def project(block):
        for start in range(0, pieces, WIDE):
            some = range(start, min(start + WIDE, pieces))
            there = slice(start * part, (some[-1] + 1) * part)
            total = None
            for group in range(groups):
                term = jnp.dot(
                    attn[block, group],
                    weight[group * depth : (group + 1) * depth, there],
                    preferred_element_type=jnp.float32,
                )
                total = term if total is None else total + term
            for piece in some:
                here = slice((piece - start) * part, (piece - start + 1) * part)
                product[block, piece, 0] = total[:half, here]
                product[block, piece, 1] = total[half:, here]
                part_out[block, piece] = product[block, piece, 1 - core].astype(jnp.bfloat16)
                part_copy(block, piece).start()

    def finish(block, piece):
        part_copy(block, piece).wait_recv()
        return (
            product[block, piece, core] + part_in[block, piece].astype(jnp.float32)
        ).astype(jnp.bfloat16)

    def send(block):
        for piece in range(pieces):
            res_copy(block, me, piece).start()

    def place(block, piece):
        hidden = (
            residual[block, :, piece * part : (piece + 1) * part].astype(jnp.float32)
            + res_in[block, piece].astype(jnp.float32)
        ).astype(jnp.bfloat16)
        for shift in (*range(1, exp_count), 0):
            peer = lax.rem(mine + shift, exp_count)
            table = (slot_row + peer * slots == target).astype(jnp.bfloat16)
            chosen = jnp.dot(table, hidden, preferred_element_type=jnp.float32).astype(
                jnp.bfloat16
            )
            if shift == 0:
                slot_at(mine, block, piece)[...] = chosen
            else:
                slot_out[shift - 1, block, piece] = chosen
                slot_copy(shift, block, mine, piece).start()

    def absorb(shift, block):
        peer = lax.rem(mine + shift, exp_count)
        for piece in range(pieces):
            if shift:
                slot_copy(1, block, peer, piece).wait_recv()
            hidden = slot_at(peer, block, piece)[...]
            if aligned:
                first = pl.multiple_of(block * columns + piece * part, 128)
                columns_here = routed[:, pl.ds(first, part)]
            else:
                columns_here = routed[block, piece]
            logits[shift] += lax.dot_general(
                hidden,
                columns_here,
                (((1,), (1,)), ((), ())),
                preferred_element_type=jnp.float32,
            )
            wide = hidden.astype(jnp.float32)
            wide = wide * wide
            if aligned:
                total = wide[:, :128]
                for first in range(128, part, 128):
                    total = total + wide[:, first : first + 128]
                tally[shift] += total
            else:
                tally[shift, :, :1] += jnp.sum(wide, axis=1, keepdims=True)

    loads["weight"].wait()
    project(me)

    @pl.when(rest > 0)
    def _():
        project(me + 1)

    loads["gain"].wait()
    loads["router"].wait()
    wide = gain_ref[...].astype(jnp.float32)
    for line in range(wide.shape[0]):
        there = slice(line * 128, (line + 1) * 128)
        gain_row[:, there] = wide[line : line + 1]
        router_ref[:, there] = (
            router_ref[:, there].astype(jnp.float32) * wide[line : line + 1]
        ).astype(jnp.bfloat16)
    if not aligned:
        for block in range(ctx_count):
            for piece in range(pieces):
                first = block * columns + piece * part
                routed[block, piece] = router_ref[:, first : first + part]
    else:
        routed = router_ref
    tally[...] = jnp.zeros_like(tally)
    logits[...] = jnp.zeros_like(logits)
    for block in range(ctx_count):
        loads[block].wait()

    def due(source):
        apart = jnp.abs(source - me)
        base = groups * jnp.maximum(source, me) - apart + (apart + 1) // 2
        first = groups * beyond + jnp.where(
            source == ctx_count - 1, 1, jnp.where(source == 1, 2, 3)
        )
        after = jnp.where(me == 0, first, base + 1)
        before = jnp.where(apart == 1, groups * me + 1, base + 4)
        return jnp.where(source > me, after, before)

    def reply(block, now):
        for piece in range(pieces):
            res_out[block, piece] = finish(block, piece)
            if now is not None:

                @pl.when(now)
                def _(piece=piece):
                    res_copy(block, me, piece).start()

    def send(block):
        for piece in range(pieces):
            res_copy(block, me, piece).start()

    def place_all(block):
        for piece in range(pieces):
            res_copy(me, block, piece).wait_recv()
            if piece == 0:

                @pl.when(
                    ((me > 0) & (block > me + 1))
                    | ((block == 0) & (me > 1) & (rest > 0))
                )
                def _():
                    send(block)

            place(block, piece)
        absorb(0, block)

    def step(turn, carry):
        left, left_whole = from_left(turn + 1)
        right, right_whole = from_right(turn)

        @pl.when(turn == 1)
        def _():
            for piece in range(pieces):
                res_in[me, piece] = finish(me, piece)
                place(me, piece)
            absorb(0, me)

            @pl.when(rest > 0)
            def _():
                reply(me + 1, None)

        @pl.when((rest > 0) & (turn == jnp.maximum(groups * me - 1, 1)))
        def _():
            send(me + 1)

        whole = ((left, left_whole), (right, right_whole))
        for block, has in whole:

            @pl.when(has)
            def _(block=block):
                project(block)

        prompt = (left < me - 1) & ((left > 0) | (rest == 0))
        for (block, has), now in zip(whole, (prompt, None)):

            @pl.when(has)
            def _(block=block, now=now):
                reply(block, now)

        @pl.when((me > 0) & (turn == jnp.maximum(jnp.maximum(groups * me - 1, groups * beyond), 1)))
        def _():
            send(me - 1)

        @pl.when((me == 0) & (turn == groups * beyond))
        def _():
            def body(block, carry):
                send(block)
                return carry

            lax.fori_loop(2, ctx_count, body, 0)

        @pl.when(turn == 1 + SLOT_LAG)
        def _():
            for shift in range(1, exp_count):
                absorb(shift, me)

        def arrivals(source, carry):
            when = due(source) + LAG

            @pl.when((source != me) & (turn == when))
            def _():
                place_all(source)

            @pl.when((source != me) & (turn == when + SLOT_LAG))
            def _():
                for shift in range(1, exp_count):
                    absorb(shift, source)

            return carry

        lax.fori_loop(0, ctx_count, arrivals, 0)
        return carry

    lax.fori_loop(1, groups * (ctx_count - 1) + 4 + LAG + SLOT_LAG, step, 0)

    spread = lax.broadcasted_iota(jnp.int32, logits.shape[1:], 0) // CAP
    expert = lax.broadcasted_iota(jnp.int32, logits.shape[1:], 1)
    for shift in range(exp_count):
        peer = lax.rem(mine + shift, exp_count)
        power = tally[shift] if aligned else tally[shift, :, :1]
        power = jnp.sum(power, axis=1, keepdims=True) / width
        factor = lax.rsqrt(power + EPSILON)
        logit = jnp.sum(jnp.where(spread == expert, logits[shift], 0.0), axis=1, keepdims=True)
        gate = jax.nn.sigmoid(logit * factor)
        scale_ref[peer] = jnp.broadcast_to(gate * factor, scale_ref.shape[1:])

    @pl.when(me < ctx_count - 1)
    def _():
        for group in range(groups):
            kv_copy(group, 1).wait_send()
            for shift in range(1, back):

                @pl.when(me >= shift)
                def _(group=group, shift=shift):
                    kv_copy(group, shift + 1).wait_send()

    for shift in range(1, back + 1):

        @pl.when(me + shift < ctx_count)
        def _(shift=shift):
            doc_copy(shift).wait_send()

    @pl.when(me > 0)
    def _():
        next_doc().wait_send()
        for group in range(groups):
            next_kv(group).wait_send()
            next_query(group).wait_send()

    def drain(block, carry):
        for piece in range(pieces):
            part_copy(block, piece).wait_send()
            for shift in range(1, exp_count):
                slot_copy(shift, block, mine, piece).wait_send()

        @pl.when(block != me)
        def _():
            for piece in range(pieces):
                res_copy(block, me, piece).wait_send()

        for group in range(groups):

            @pl.when((block <= me) & (me < ctx_count - 1))
            def _(group=group):
                attn_copy(block, group, True).wait_send()

            @pl.when((block > me) & (me > 0))
            def _(group=group):
                attn_copy(block, group, False).wait_send()

        return carry

    lax.fori_loop(0, ctx_count, drain, 0)


def on_device(
    queries,
    key_states,
    values,
    doc_ids,
    residual,
    out_proj,
    norm_gain,
    router,
    expert_ids,
    keep_counts,
):
    tokens, heads, size = queries.shape[1:]
    groups = key_states.shape[2]
    ctx_count = lax.axis_size("ctx")
    exp_count = lax.axis_size("exp")
    features, columns = out_proj.shape
    half = residual.shape[1]
    width = residual.shape[2]
    experts = keep_counts.shape[0]
    owned = experts // exp_count
    slots = owned * CAP
    longest = tokens * ctx_count // 2
    back = min(ctx_count - 1, -(-(longest - 1) // tokens))
    pieces = columns // 256 if columns % 256 == 0 else 2
    part = columns // pieces
    aligned = part % 128 == 0
    vmem = pl.BlockSpec(memory_space=pltpu.VMEM)
    hbm = pl.BlockSpec(memory_space=pltpu.HBM)
    bf16, f32, i32 = jnp.bfloat16, jnp.float32, jnp.int32
    dma = pltpu.SemaphoreType.DMA
    n = ctx_count
    stream = residual[0]
    if columns % 128:
        stream = stream.reshape(half, ctx_count, columns).transpose(1, 0, 2)
    slot_shape = (exp_count, slots, width) if aligned else (exp_count, n, pieces, slots, part)
    chosen, scale, gain = pl.pallas_call(
        functools.partial(kernel, (ctx_count, exp_count, back, pieces)),
        out_shape=(
            jax.ShapeDtypeStruct(slot_shape, bf16),
            jax.ShapeDtypeStruct((exp_count, slots, 128), f32),
            jax.ShapeDtypeStruct((1, width), f32),
        ),
        in_specs=[hbm] * 10,
        out_specs=(vmem, vmem, vmem),
        scratch_shapes=[
            pltpu.VMEM((heads, tokens, size), bf16),
            pltpu.VMEM((tokens, groups, size), bf16),
            pltpu.VMEM((tokens, groups, size), bf16),
            pltpu.VMEM((1, tokens), i32),
            pltpu.VMEM((width // 128, 128), bf16),
            pltpu.VMEM((owned, width), bf16),
            pltpu.VMEM((1, half), i32),
            pltpu.VMEM((1, experts), i32),
            pltpu.VMEM((groups, 2, tokens, size), bf16),
            pltpu.VMEM((groups, back, 2, tokens, size), bf16),
            pltpu.VMEM((groups, 2, tokens, size), bf16),
            pltpu.VMEM((heads, tokens, size), bf16),
            pltpu.VMEM((1, tokens), i32),
            pltpu.VMEM((8, 128) if aligned else (n, pieces, owned, part), bf16),
            pltpu.VMEM((exp_count, slots, 128), f32),
            pltpu.VMEM((exp_count, slots, owned), f32),
            pltpu.VMEM((back, 1, tokens), i32),
            pltpu.VMEM((n, groups, tokens, features // groups), bf16),
            pltpu.VMEM((features, columns), bf16),
            pltpu.VMEM((n, half, columns), bf16),
            pltpu.VMEM((n, pieces, 2, half, part), f32),
            pltpu.VMEM((n, pieces, half, part), bf16),
            pltpu.VMEM((n, pieces, half, part), bf16),
            pltpu.VMEM((n, pieces, half, part), bf16),
            pltpu.VMEM((n, pieces, half, part), bf16),
            pltpu.VMEM((exp_count - 1, n, pieces, slots, part), bf16),
            dma((9 + n,)),
            dma((groups, back)),
            dma((groups, back)),
            dma((back,)),
            dma((back,)),
            dma((2 * groups + 1,)),
            dma((2 * groups + 1,)),
            dma((n, groups)),
            dma((n, groups)),
            dma((n, groups)),
            dma((n, pieces)),
            dma((n, pieces)),
            dma((n, pieces)),
            dma((n, pieces)),
            dma((exp_count - 1, n, pieces)),
            dma((exp_count, n, pieces)),
        ],
        compiler_params=pltpu.CompilerParams(
            collective_id=0, has_side_effects=True, vmem_limit_bytes=40 << 20
        ),
    )(
        *(
            pltpu.with_memory_space_constraint(operand, pltpu.HBM)
            for operand in (
                queries[0].transpose(1, 0, 2),
                key_states[0],
                values[0],
                doc_ids,
                stream,
                out_proj,
                norm_gain.reshape(width // 128, 128),
                router.T,
                expert_ids.reshape(1, half),
                keep_counts.reshape(1, experts),
            )
        )
    )
    if not aligned:
        chosen = chosen.transpose(0, 3, 1, 2, 4).reshape(exp_count, slots, width)
    scaled = chosen.astype(f32) * scale[:, :, :1] * gain
    return scaled.astype(bf16).reshape(exp_count, owned, CAP, width)


def solution(mesh):
    placed = (
        P(("groups", "exp"), "ctx", "tp", None),
        P(("groups", "exp"), "ctx", "tp", None),
        P(("groups", "exp"), "ctx", "tp", None),
        P(("groups", "exp"), "ctx"),
        P(("groups", "exp"), ("ctx", "tp"), None),
        P("tp", "ctx"),
        P(),
        P(None, "exp"),
        P(("groups", "exp"), ("ctx", "tp"), None),
        P("groups"),
    )
    return jax.shard_map(
        on_device,
        mesh=mesh,
        in_specs=placed,
        out_specs=P(("groups", "ctx", "tp"), "exp", None, None),
        check_vma=False,
    )
```

```python
import functools
import math

import jax
import jax.numpy as jnp
from jax import lax
from jax.experimental import pallas as pl
from jax.experimental.pallas import tpu as pltpu
from jax.sharding import PartitionSpec as P

CAP = 2
EPSILON = 1e-05
HOLD = 2
WIDE = 5
MESH = pl.DeviceIdType.MESH


def kernel(
    sizes,
    q_hbm,
    key_hbm,
    value_hbm,
    doc_hbm,
    residual_hbm,
    weight_hbm,
    gain_hbm,
    router_hbm,
    ids_hbm,
    keep_hbm,
    slot_in,
    scale_ref,
    gain_row,
    q_ref,
    key_ref,
    value_ref,
    doc_ref,
    gain_ref,
    router_ref,
    ids_ref,
    keep_ref,
    kv_out,
    kv_in,
    kv_next,
    q_next,
    doc_next,
    routed,
    tally,
    logits,
    doc_in,
    attn,
    weight,
    residual,
    product,
    part_out,
    part_in,
    res_out,
    res_in,
    slot_out,
    load_sem,
    kv_send,
    kv_recv,
    doc_send,
    doc_recv,
    next_send,
    next_recv,
    right_send,
    left_send,
    attn_recv,
    part_send,
    part_recv,
    res_send,
    res_recv,
    slot_send,
    slot_recv,
):
    ctx_count, exp_count, back, pieces = sizes
    heads, tokens, size = q_ref.shape
    groups = kv_out.shape[0]
    ratio = heads // groups
    half = tokens // 2
    columns = weight.shape[1]
    depth = weight.shape[0] // groups
    slots = slot_out.shape[3]
    part = columns // pieces
    width = columns * ctx_count
    aligned = part % 128 == 0
    me = lax.axis_index("ctx")
    mine = lax.axis_index("exp")
    core = lax.axis_index("tp")
    rest = ctx_count - 1 - me
    early = (rest == 0) & (me > 1)

    barrier = pltpu.get_barrier_semaphore()
    for shift in range(1, ctx_count):
        pl.semaphore_signal(
            barrier,
            inc=1,
            device_id={"ctx": lax.rem(me + shift, ctx_count)},
            device_id_type=MESH,
        )
    for shift in range(1, exp_count):
        pl.semaphore_signal(
            barrier,
            inc=1,
            device_id={"exp": lax.rem(mine + shift, exp_count)},
            device_id_type=MESH,
        )
    pl.semaphore_signal(barrier, inc=1, device_id={"tp": 1 - core}, device_id_type=MESH)

    loads = {}

    def load(name, source, target):
        loads[name] = pltpu.make_async_copy(source, target, load_sem.at[len(loads)])
        loads[name].start()

    load("key", key_hbm, key_ref)
    load("value", value_hbm, value_ref)
    load("doc", doc_hbm, doc_ref)
    load("query", q_hbm, q_ref)
    load("ids", ids_hbm, ids_ref)
    load("keep", keep_hbm, keep_ref)
    load("gain", gain_hbm, gain_ref)
    load("router", router_hbm, router_ref)
    load("weight", weight_hbm, weight)
    for block in range(ctx_count):
        there = slice(block * columns, (block + 1) * columns)
        load(
            block,
            residual_hbm.at[:, there] if columns % 128 == 0 else residual_hbm.at[block],
            residual.at[block],
        )

    loads["key"].wait()
    loads["value"].wait()
    for group in range(groups):
        kv_out[group, 0] = key_ref[:, group, :]
        kv_out[group, 1] = value_ref[:, group, :]
    loads["doc"].wait()

    pl.semaphore_wait(barrier, ctx_count + exp_count - 1)

    def kv_copy(group, shift, hops=1):
        return pltpu.make_async_remote_copy(
            src_ref=kv_out.at[group] if shift == hops else kv_in.at[group, shift - 2],
            dst_ref=kv_in.at[group, shift - 1],
            send_sem=kv_send.at[group, shift - 1],
            recv_sem=kv_recv.at[group, shift - 1],
            device_id={"ctx": lax.rem(me + hops, ctx_count)},
            device_id_type=MESH,
        )

    def doc_copy(shift):
        return pltpu.make_async_remote_copy(
            src_ref=doc_ref,
            dst_ref=doc_in.at[shift - 1],
            send_sem=doc_send.at[shift - 1],
            recv_sem=doc_recv.at[shift - 1],
            device_id={"ctx": lax.rem(me + shift, ctx_count)},
            device_id_type=MESH,
        )

    def next_copy(source, target, index):
        return pltpu.make_async_remote_copy(
            src_ref=source,
            dst_ref=target,
            send_sem=next_send.at[index],
            recv_sem=next_recv.at[index],
            device_id={"ctx": lax.rem(me + ctx_count - 1, ctx_count)},
            device_id_type=MESH,
        )

    def next_doc():
        return next_copy(doc_ref, doc_next, 2 * groups)

    def next_kv(group):
        return next_copy(kv_out.at[group], kv_next.at[group], 2 * group)

    def next_query(group):
        these = pl.ds(group * ratio, ratio)
        return next_copy(q_ref.at[these], q_next.at[these], 2 * group + 1)

    for shift in range(1, back + 1):

        @pl.when(me + shift < ctx_count)
        def _(shift=shift):
            doc_copy(shift).start()

    @pl.when(me < ctx_count - 1)
    def _():
        for group in range(groups):
            kv_copy(group, 1).start()
            if back > 1 and group < groups - 1:

                @pl.when(me == 0)
                def _(group=group):
                    kv_copy(group, 2, 2).start()

    loads["query"].wait()

    @pl.when(me > 0)
    def _():
        next_doc().start()
        for group in range(groups):
            next_kv(group).start()
            next_query(group).start()

    for shift in range(1, back + 1):

        @pl.when(me < shift)
        def _(shift=shift):
            doc_in[shift - 1] = jnp.full(doc_in.shape[1:], -1, jnp.int32)
            for group in range(groups):
                kv_in[group, shift - 1] = jnp.zeros(kv_in.shape[2:], kv_in.dtype)

    def kv_arrive(group, shift):
        @pl.when(me >= shift)
        def _():
            kv_copy(group, shift).wait_recv()
            if shift < back:

                relayed = (me > 1) | (shift > 1) | (group == groups - 1)

                @pl.when((me < ctx_count - 1) & relayed)
                def _():
                    kv_copy(group, shift + 1).start()

    loads["ids"].wait()
    loads["keep"].wait()
    row = lax.broadcasted_iota(jnp.int32, (half, half), 0)
    lane = lax.broadcasted_iota(jnp.int32, (half, half), 1)
    ids_row = ids_ref[...]
    ids_column = jnp.sum(jnp.where(row == lane, ids_row, 0), axis=1, keepdims=True)
    ranking = jnp.sum(
        jnp.where((ids_column == ids_row) & (row < lane), 1, 0), axis=0, keepdims=True
    )
    experts = keep_ref.shape[1]
    square_row = lax.broadcasted_iota(jnp.int32, (experts, experts), 0)
    square_lane = lax.broadcasted_iota(jnp.int32, (experts, experts), 1)
    keep_column = jnp.sum(
        jnp.where(square_row == square_lane, keep_ref[...], 0), axis=1, keepdims=True
    )
    expert_row = lax.broadcasted_iota(jnp.int32, (experts, half), 0)
    limits = jnp.sum(jnp.where(expert_row == ids_row, keep_column, 0), axis=0, keepdims=True)
    target = jnp.where(ranking < limits, ids_row * CAP + ranking, -1)
    slot_row = lax.broadcasted_iota(jnp.int32, (slots, half), 0)

    for shift in range(1, back + 1):

        @pl.when(me >= shift)
        def _(shift=shift):
            doc_copy(shift).wait_recv()

    square = lax.broadcasted_iota(jnp.int32, (tokens, tokens), 0)
    across = lax.broadcasted_iota(jnp.int32, (tokens, tokens), 1)
    scale = 1.0 / math.sqrt(size)

    def visible(doc_row, earlier):
        doc_column = jnp.sum(jnp.where(square == across, doc_row, 0), axis=1, keepdims=True)
        masks = [(across <= square) & (doc_row == doc_column)]
        masks += [other == doc_column for other in earlier]
        return jnp.concatenate([jnp.where(mask, 1.0, 0.0) for mask in masks], axis=1) > 0.5

    def attend(block, group, allowed, query, pairs):
        keys = jnp.concatenate([pair[0] for pair in pairs], axis=0)
        vals = jnp.concatenate([pair[1] for pair in pairs], axis=0)
        count = keys.shape[0]
        stacked = query[group * ratio : (group + 1) * ratio].reshape(ratio * tokens, size)
        scores = lax.dot_general(
            stacked, keys, (((1,), (1,)), ((), ())), preferred_element_type=jnp.float32
        ).reshape(ratio, tokens, count)
        masked = jnp.where(allowed[None], scores * scale, -1e30)
        highest = jnp.max(masked, axis=2, keepdims=True)
        weights = jnp.exp(masked - highest)
        totals = jnp.sum(weights, axis=2, keepdims=True)
        mixed = jnp.dot(
            weights.astype(jnp.bfloat16).reshape(ratio * tokens, count),
            vals,
            preferred_element_type=jnp.float32,
        ).reshape(ratio, tokens, size)
        mixed = (mixed / totals).astype(jnp.bfloat16)
        for head in range(ratio):
            attn[block, group, :, head * size : (head + 1) * size] = mixed[head]

    def attn_copy(block, group, rightward):
        to = me + 1 if rightward else me - 1
        sends = right_send if rightward else left_send
        return pltpu.make_async_remote_copy(
            src_ref=attn.at[block, group],
            dst_ref=attn.at[block, group],
            send_sem=sends.at[block, group],
            recv_sem=attn_recv.at[block, group],
            device_id={"ctx": lax.rem(to + ctx_count, ctx_count)},
            device_id_type=MESH,
        )

    allowed = visible(doc_ref[...], [doc_in[shift] for shift in range(back)])

    def attend_own(group):
        if back:
            kv_arrive(group, back)
        attend(
            me,
            group,
            allowed,
            q_ref,
            [kv_out.at[group]] + [kv_in.at[group, shift] for shift in range(back)],
        )
        soon = group < groups - 1

        @pl.when((me < ctx_count - 1) & (soon | (me == 0) | (rest == 1)))
        def _():
            attn_copy(me, group, True).start()

    for group in range(groups - 1):
        for shift in range(1, back):
            kv_arrive(group, shift)
        attend_own(group)

    @pl.when(me == 0)
    def _():
        attend_own(groups - 1)

    def item(turn, count):
        order = turn - 1
        spot = jnp.where(count > 0, lax.rem(order, jnp.maximum(count, 1)), 0)
        group = sum((order >= count * number).astype(jnp.int32) for number in range(1, groups))
        group = group if groups > 1 else jnp.int32(0)
        final = group == groups - 1
        active = (turn >= 1) & (turn <= groups * count)
        return group, jnp.where(final, count - spot, spot + 1), final, active

    beyond = jnp.maximum(rest - 1, 0)
    skipped = jnp.where(early, 1, 0)
    upstream = me - skipped

    def from_left(turn):
        group, far, final, active = item(turn, upstream)
        block = upstream - far

        @pl.when(active)
        def _():
            attn_copy(block, group, True).wait_recv()

            @pl.when(me < ctx_count - 1)
            def _():
                attn_copy(block, group, True).start()

                @pl.when((turn == groups * me) & (rest > 1))
                def _():
                    attn_copy(me, groups - 1, True).start()

        return block, active & final

    def from_right(turn):
        group = lax.rem(turn - 1, groups)
        block = me + 2 + (turn - 1) // groups
        final, active = group == groups - 1, turn <= groups * beyond

        @pl.when(active)
        def _():
            attn_copy(block, group, False).wait_recv()

            @pl.when(me > 0)
            def _():
                attn_copy(block, group, False).start()

        return block, active & final

    def attend_next(group):
        @pl.when(rest > 0)
        def _():
            next_kv(group).wait_recv()
            next_query(group).wait_recv()
            attend(
                me + 1,
                group,
                visible(
                    doc_next[...],
                    ([doc_ref[...]] if back else []) + [doc_in[shift] for shift in range(back - 1)],
                ),
                q_next,
                [kv_next.at[group]]
                + ([kv_out.at[group]] if back else [])
                + [kv_in.at[group, shift] for shift in range(back - 1)],
            )

            @pl.when(me > 0)
            def _():
                attn_copy(me + 1, group, False).start()

    @pl.when(rest > 0)
    def _():
        next_doc().wait_recv()

    for group in range(groups - 1):
        attend_next(group)
    for shift in range(1, back):
        kv_arrive(groups - 1, shift)
    from_left(1)
    attend_next(groups - 1)

    @pl.when(me > 0)
    def _():
        attend_own(groups - 1)

    def part_copy(block, piece):
        return pltpu.make_async_remote_copy(
            src_ref=part_out.at[block, piece],
            dst_ref=part_in.at[block, piece],
            send_sem=part_send.at[0],
            recv_sem=part_recv.at[block, piece],
            device_id={"tp": 1 - core},
            device_id_type=MESH,
        )

    def res_copy(block, peer, piece):
        return pltpu.make_async_remote_copy(
            src_ref=res_out.at[block, piece],
            dst_ref=res_in.at[me, piece],
            send_sem=res_send.at[0],
            recv_sem=res_recv.at[peer, piece],
            device_id={"ctx": block},
            device_id_type=MESH,
        )

    def slot_at(peer, block, piece):
        if aligned:
            first = pl.multiple_of(block * columns + piece * part, 128)
            return slot_in.at[peer, :, pl.ds(first, part)]
        return slot_in.at[peer, block, piece]

    def slot_copy(shift, block, index, piece):
        return pltpu.make_async_remote_copy(
            src_ref=slot_out.at[shift - 1, block, piece],
            dst_ref=slot_at(mine, block, piece),
            send_sem=slot_send.at[shift - 1],
            recv_sem=slot_recv.at[index, block, piece],
            device_id={"exp": lax.rem(mine + shift, exp_count)},
            device_id_type=MESH,
        )

    def project(block):
        for start in range(0, pieces, WIDE):
            some = range(start, min(start + WIDE, pieces))
            there = slice(start * part, (some[-1] + 1) * part)
            total = None
            for group in range(groups):
                term = jnp.dot(
                    attn[block, group],
                    weight[group * depth : (group + 1) * depth, there],
                    preferred_element_type=jnp.float32,
                )
                total = term if total is None else total + term
            for piece in some:
                here = slice((piece - start) * part, (piece - start + 1) * part)
                product[block, piece, 0] = total[:half, here]
                product[block, piece, 1] = total[half:, here]
                part_out[block, piece] = product[block, piece, 1 - core].astype(jnp.bfloat16)
                part_copy(block, piece).start()

    def finish(block, piece):
        part_copy(block, piece).wait_recv()
        return (
            product[block, piece, core] + part_in[block, piece].astype(jnp.float32)
        ).astype(jnp.bfloat16)

    def send(block):
        for piece in range(pieces):
            res_copy(block, me, piece).start()

    def place(block, piece):
        hidden = (
            residual[block, :, piece * part : (piece + 1) * part].astype(jnp.float32)
            + res_in[block, piece].astype(jnp.float32)
        ).astype(jnp.bfloat16)
        for shift in (*range(1, exp_count), 0):
            peer = lax.rem(mine + shift, exp_count)
            table = (slot_row + peer * slots == target).astype(jnp.bfloat16)
            chosen = jnp.dot(table, hidden, preferred_element_type=jnp.float32).astype(
                jnp.bfloat16
            )
            if shift == 0:
                slot_at(mine, block, piece)[...] = chosen
            else:
                slot_out[shift - 1, block, piece] = chosen
                slot_copy(shift, block, exp_count - shift - 1, piece).start()

    def absorb(shift, block, piece):
        peer = lax.rem(mine + shift, exp_count)
        if shift:
            slot_copy(1, block, shift - 1, piece).wait_recv()
        hidden = slot_at(peer, block, piece)[...]
        if aligned:
            first = pl.multiple_of(block * columns + piece * part, 128)
            columns_here = routed[:, pl.ds(first, part)]
        else:
            columns_here = routed[block, piece]
        logits[shift] += lax.dot_general(
            hidden,
            columns_here,
            (((1,), (1,)), ((), ())),
            preferred_element_type=jnp.float32,
        )
        wide = hidden.astype(jnp.float32)
        wide = wide * wide
        if aligned:
            total = wide[:, :128]
            for first in range(128, part, 128):
                total = total + wide[:, first : first + 128]
            tally[shift] += total
        else:
            tally[shift, :, :1] += jnp.sum(wide, axis=1, keepdims=True)

    loads["weight"].wait()
    project(me)

    @pl.when(rest > 0)
    def _():
        project(me + 1)

    loads["gain"].wait()
    loads["router"].wait()
    wide = gain_ref[...].astype(jnp.float32)
    for line in range(wide.shape[0]):
        there = slice(line * 128, (line + 1) * 128)
        gain_row[:, there] = wide[line : line + 1]
        router_ref[:, there] = (
            router_ref[:, there].astype(jnp.float32) * wide[line : line + 1]
        ).astype(jnp.bfloat16)
    if not aligned:
        for block in range(ctx_count):
            for piece in range(pieces):
                first = block * columns + piece * part
                routed[block, piece] = router_ref[:, first : first + part]
    else:
        routed = router_ref
    tally[...] = jnp.zeros_like(tally)
    logits[...] = jnp.zeros_like(logits)
    for block in range(ctx_count):
        loads[block].wait()

    def reply(block, now):
        for piece in range(pieces):
            res_out[block, piece] = finish(block, piece)
            if now is not None:

                @pl.when(now)
                def _(piece=piece):
                    res_copy(block, me, piece).start()

    def send(block):
        for piece in range(pieces):
            res_copy(block, me, piece).start()

    def order(number):
        inner = jnp.where(number <= rest, me + number, number - rest - 1)
        inner = jnp.where(number == 0, me - 1, inner)
        return jnp.where(me == 0, jnp.where(number == 0, 1, ctx_count - number), inner)

    def send_far(start):
        def body(number, carry):
            send(ctx_count - 1 - number)
            return carry

        lax.fori_loop(start, beyond, body, 0)

    def settle(number, before):
        block = order(number)
        for piece in range(pieces):
            res_copy(me, block, piece).wait_recv()
            if piece == 0:

                @pl.when((me == 0) & (number == 1))
                def _():
                    send(ctx_count - 1)

                @pl.when(early & (number == 1))
                def _():
                    def body(block, carry):
                        send(block)
                        return carry

                    lax.fori_loop(1, me - 1, body, 0)

            if piece == min(HOLD, pieces - 1):

                @pl.when((me == 0) & (number == 2))
                def _():
                    send_far(1)

            place(block, piece)
            absorb(0, block, piece)
            for shift in range(1, exp_count):
                absorb(shift, before, piece)

        @pl.when((number == 0) & (me > 1) & (rest > 0))
        def _():
            send(0)

        @pl.when((number == 1) & (me > 0))
        def _():
            send_far(0)

        return block

    last = jnp.maximum(groups * upstream - 1, groups * beyond)

    late = (rest == 1) & (me > 1)

    def own():
        for piece in range(pieces):
            res_in[me, piece] = finish(me, piece)
            place(me, piece)
            absorb(0, me, piece)

        @pl.when(rest > 0)
        def _():
            reply(me + 1, None)

        @pl.when((rest > 0) & jnp.logical_not(late))
        def _():
            send(me + 1)

    @pl.when(early)
    def _():
        for group in range(groups):
            attn_copy(me - 1, group, True).wait_recv()
        project(me - 1)

    @pl.when((me == 0) | (rest == 0))
    def _():
        own()

    @pl.when(early)
    def _():
        reply(me - 1, None)
        send(me - 1)

    def step(turn, carry):
        left, left_whole = from_left(turn + 1)
        right, right_whole = from_right(turn)

        @pl.when((turn == 1) & (me > 0) & (rest > 0))
        def _():
            own()

        whole = ((left, left_whole), (right, right_whole))
        for block, has in whole:

            @pl.when(has)
            def _(block=block):
                project(block)

        prompt = (left < me - 1) & ((left > 0) != early)
        for (block, has), now in zip(whole, (prompt, None)):

            @pl.when(has)
            def _(block=block, now=now):
                reply(block, now)

        @pl.when(late & (turn == groups * me - 2))
        def _():
            send(me + 1)

        @pl.when(early & (turn == (groups - 1) * upstream))
        def _():
            settle(0, me)

        return carry

    lax.fori_loop(1, jnp.maximum(last, 1) + 1, step, 0)

    @pl.when((me > 0) & (rest > 0) | (me == 1))
    def _():
        send(me - 1)

    block = lax.fori_loop(
        jnp.where(early, 1, 0), ctx_count - 1, settle, jnp.where(early, me - 1, me)
    )
    for piece in range(pieces):
        for shift in range(1, exp_count):
            absorb(shift, block, piece)

    spread = lax.broadcasted_iota(jnp.int32, logits.shape[1:], 0) // CAP
    expert = lax.broadcasted_iota(jnp.int32, logits.shape[1:], 1)
    for shift in range(exp_count):
        peer = lax.rem(mine + shift, exp_count)
        power = tally[shift] if aligned else tally[shift, :, :1]
        power = jnp.sum(power, axis=1, keepdims=True) / width
        factor = lax.rsqrt(power + EPSILON)
        logit = jnp.sum(jnp.where(spread == expert, logits[shift], 0.0), axis=1, keepdims=True)
        gate = jax.nn.sigmoid(logit * factor)
        scale_ref[peer] = jnp.broadcast_to(gate * factor, scale_ref.shape[1:])

    @pl.when(me < ctx_count - 1)
    def _():
        for group in range(groups):
            kv_copy(group, 1).wait_send()
            if back > 1 and group < groups - 1:

                @pl.when(me == 0)
                def _(group=group):
                    kv_copy(group, 2, 2).wait_send()

            for shift in range(1, back):
                relayed = (me > 1) | (shift > 1) | (group == groups - 1)

                @pl.when((me >= shift) & relayed)
                def _(group=group, shift=shift):
                    kv_copy(group, shift + 1).wait_send()

    for shift in range(1, back + 1):

        @pl.when(me + shift < ctx_count)
        def _(shift=shift):
            doc_copy(shift).wait_send()

    @pl.when(me > 0)
    def _():
        next_doc().wait_send()
        for group in range(groups):
            next_kv(group).wait_send()
            next_query(group).wait_send()

    def sent(source, semaphore):
        pltpu.make_async_remote_copy(
            src_ref=source,
            dst_ref=source,
            send_sem=semaphore,
            recv_sem=semaphore,
            device_id={"tp": 1 - core},
            device_id_type=MESH,
        ).wait_send()

    sent(part_out, part_send.at[0])
    sent(res_out.at[pl.ds(0, ctx_count - 1)], res_send.at[0])
    for shift in range(1, exp_count):
        sent(slot_out.at[shift - 1], slot_send.at[shift - 1])

    def drain(block, carry):
        for group in range(groups):

            @pl.when((block <= me) & (me < ctx_count - 1))
            def _(group=group):
                attn_copy(block, group, True).wait_send()

            @pl.when((block > me) & (me > 0))
            def _(group=group):
                attn_copy(block, group, False).wait_send()

        return carry

    lax.fori_loop(0, ctx_count, drain, 0)


def on_device(
    queries,
    key_states,
    values,
    doc_ids,
    residual,
    out_proj,
    norm_gain,
    router,
    expert_ids,
    keep_counts,
):
    tokens, heads, size = queries.shape[1:]
    groups = key_states.shape[2]
    ctx_count = lax.axis_size("ctx")
    exp_count = lax.axis_size("exp")
    features, columns = out_proj.shape
    half = residual.shape[1]
    width = residual.shape[2]
    experts = keep_counts.shape[0]
    owned = experts // exp_count
    slots = owned * CAP
    longest = tokens * ctx_count // 2
    back = min(ctx_count - 1, -(-(longest - 1) // tokens))
    pieces = columns // 256 if columns % 256 == 0 else 2
    part = columns // pieces
    aligned = part % 128 == 0
    vmem = pl.BlockSpec(memory_space=pltpu.VMEM)
    hbm = pl.BlockSpec(memory_space=pltpu.HBM)
    bf16, f32, i32 = jnp.bfloat16, jnp.float32, jnp.int32
    dma = pltpu.SemaphoreType.DMA
    n = ctx_count
    stream = residual[0]
    if columns % 128:
        stream = stream.reshape(half, ctx_count, columns).transpose(1, 0, 2)
    slot_shape = (exp_count, slots, width) if aligned else (exp_count, n, pieces, slots, part)
    chosen, scale, gain = pl.pallas_call(
        functools.partial(kernel, (ctx_count, exp_count, back, pieces)),
        out_shape=(
            jax.ShapeDtypeStruct(slot_shape, bf16),
            jax.ShapeDtypeStruct((exp_count, slots, 128), f32),
            jax.ShapeDtypeStruct((1, width), f32),
        ),
        in_specs=[hbm] * 10,
        out_specs=(vmem, vmem, vmem),
        scratch_shapes=[
            pltpu.VMEM((heads, tokens, size), bf16),
            pltpu.VMEM((tokens, groups, size), bf16),
            pltpu.VMEM((tokens, groups, size), bf16),
            pltpu.VMEM((1, tokens), i32),
            pltpu.VMEM((width // 128, 128), bf16),
            pltpu.VMEM((owned, width), bf16),
            pltpu.VMEM((1, half), i32),
            pltpu.VMEM((1, experts), i32),
            pltpu.VMEM((groups, 2, tokens, size), bf16),
            pltpu.VMEM((groups, back, 2, tokens, size), bf16),
            pltpu.VMEM((groups, 2, tokens, size), bf16),
            pltpu.VMEM((heads, tokens, size), bf16),
            pltpu.VMEM((1, tokens), i32),
            pltpu.VMEM((8, 128) if aligned else (n, pieces, owned, part), bf16),
            pltpu.VMEM((exp_count, slots, 128), f32),
            pltpu.VMEM((exp_count, slots, owned), f32),
            pltpu.VMEM((back, 1, tokens), i32),
            pltpu.VMEM((n, groups, tokens, features // groups), bf16),
            pltpu.VMEM((features, columns), bf16),
            pltpu.VMEM((n, half, columns), bf16),
            pltpu.VMEM((n, pieces, 2, half, part), f32),
            pltpu.VMEM((n, pieces, half, part), bf16),
            pltpu.VMEM((n, pieces, half, part), bf16),
            pltpu.VMEM((n, pieces, half, part), bf16),
            pltpu.VMEM((n, pieces, half, part), bf16),
            pltpu.VMEM((exp_count - 1, n, pieces, slots, part), bf16),
            dma((9 + n,)),
            dma((groups, back)),
            dma((groups, back)),
            dma((back,)),
            dma((back,)),
            dma((2 * groups + 1,)),
            dma((2 * groups + 1,)),
            dma((n, groups)),
            dma((n, groups)),
            dma((n, groups)),
            dma((1,)),
            dma((n, pieces)),
            dma((1,)),
            dma((n, pieces)),
            dma((exp_count - 1,)),
            dma((exp_count - 1, n, pieces)),
        ],
        compiler_params=pltpu.CompilerParams(
            collective_id=0, has_side_effects=True, vmem_limit_bytes=40 << 20
        ),
    )(
        *(
            pltpu.with_memory_space_constraint(operand, pltpu.HBM)
            for operand in (
                queries[0].transpose(1, 0, 2),
                key_states[0],
                values[0],
                doc_ids,
                stream,
                out_proj,
                norm_gain.reshape(width // 128, 128),
                router.T,
                expert_ids.reshape(1, half),
                keep_counts.reshape(1, experts),
            )
        )
    )
    if not aligned:
        chosen = chosen.transpose(0, 3, 1, 2, 4).reshape(exp_count, slots, width)
    scaled = chosen.astype(f32) * scale[:, :, :1] * gain
    return scaled.astype(bf16).reshape(exp_count, owned, CAP, width)


def solution(mesh):
    placed = (
        P(("groups", "exp"), "ctx", "tp", None),
        P(("groups", "exp"), "ctx", "tp", None),
        P(("groups", "exp"), "ctx", "tp", None),
        P(("groups", "exp"), "ctx"),
        P(("groups", "exp"), ("ctx", "tp"), None),
        P("tp", "ctx"),
        P(),
        P(None, "exp"),
        P(("groups", "exp"), ("ctx", "tp"), None),
        P("groups"),
    )
    return jax.shard_map(
        on_device,
        mesh=mesh,
        in_specs=placed,
        out_specs=P(("groups", "ctx", "tp"), "exp", None, None),
        check_vma=False,
    )
```

```python
import functools
import math

import jax
import jax.numpy as jnp
from jax import lax
from jax.experimental import pallas as pl
from jax.experimental.pallas import tpu as pltpu
from jax.sharding import PartitionSpec as P

CAP = 2
EPSILON = 1e-05
WIDE = 5
MESH = pl.DeviceIdType.MESH


def kernel(
    sizes,
    q_hbm,
    key_hbm,
    value_hbm,
    doc_hbm,
    residual_hbm,
    weight_hbm,
    gain_hbm,
    router_hbm,
    ids_hbm,
    keep_hbm,
    slot_in,
    scale_ref,
    gain_row,
    q_ref,
    key_ref,
    value_ref,
    doc_ref,
    gain_ref,
    router_ref,
    ids_ref,
    keep_ref,
    kv_out,
    kv_in,
    kv_next,
    q_next,
    doc_next,
    routed,
    tally,
    logits,
    doc_in,
    attn,
    weight,
    residual,
    product,
    part_out,
    part_in,
    res_out,
    res_in,
    passing,
    slot_out,
    load_sem,
    kv_send,
    kv_recv,
    doc_send,
    doc_recv,
    next_send,
    next_recv,
    right_send,
    left_send,
    attn_recv,
    part_send,
    part_recv,
    res_send,
    res_recv,
    pass_send,
    pass_recv,
    slot_send,
    slot_recv,
):
    ctx_count, exp_count, back, pieces = sizes
    heads, tokens, size = q_ref.shape
    groups = kv_out.shape[0]
    ratio = heads // groups
    half = tokens // 2
    columns = weight.shape[1]
    depth = weight.shape[0] // groups
    slots = slot_out.shape[3]
    part = columns // pieces
    width = columns * ctx_count
    aligned = part % 128 == 0
    me = lax.axis_index("ctx")
    mine = lax.axis_index("exp")
    core = lax.axis_index("tp")
    rest = ctx_count - 1 - me
    early = (rest == 0) & (me > 1)

    barrier = pltpu.get_barrier_semaphore()
    for shift in range(1, ctx_count):
        pl.semaphore_signal(
            barrier,
            inc=1,
            device_id={"ctx": lax.rem(me + shift, ctx_count)},
            device_id_type=MESH,
        )
    for shift in range(1, exp_count):
        pl.semaphore_signal(
            barrier,
            inc=1,
            device_id={"exp": lax.rem(mine + shift, exp_count)},
            device_id_type=MESH,
        )
    pl.semaphore_signal(barrier, inc=1, device_id={"tp": 1 - core}, device_id_type=MESH)

    loads = {}

    def load(name, source, target):
        loads[name] = pltpu.make_async_copy(source, target, load_sem.at[len(loads)])
        loads[name].start()

    load("key", key_hbm, key_ref)
    load("value", value_hbm, value_ref)
    load("doc", doc_hbm, doc_ref)
    load("query", q_hbm, q_ref)
    load("ids", ids_hbm, ids_ref)
    load("keep", keep_hbm, keep_ref)
    load("gain", gain_hbm, gain_ref)
    load("router", router_hbm, router_ref)
    load("weight", weight_hbm, weight)
    for block in range(ctx_count):
        there = slice(block * columns, (block + 1) * columns)
        load(
            block,
            residual_hbm.at[:, there] if columns % 128 == 0 else residual_hbm.at[block],
            residual.at[block],
        )

    loads["key"].wait()
    loads["value"].wait()
    for group in range(groups):
        kv_out[group, 0] = key_ref[:, group, :]
        kv_out[group, 1] = value_ref[:, group, :]
    loads["doc"].wait()

    pl.semaphore_wait(barrier, ctx_count + exp_count - 1)

    def kv_copy(group, shift, hops=1):
        return pltpu.make_async_remote_copy(
            src_ref=kv_out.at[group] if shift == hops else kv_in.at[group, shift - 2],
            dst_ref=kv_in.at[group, shift - 1],
            send_sem=kv_send.at[group, shift - 1],
            recv_sem=kv_recv.at[group, shift - 1],
            device_id={"ctx": lax.rem(me + hops, ctx_count)},
            device_id_type=MESH,
        )

    def doc_copy(shift):
        return pltpu.make_async_remote_copy(
            src_ref=doc_ref,
            dst_ref=doc_in.at[shift - 1],
            send_sem=doc_send.at[shift - 1],
            recv_sem=doc_recv.at[shift - 1],
            device_id={"ctx": lax.rem(me + shift, ctx_count)},
            device_id_type=MESH,
        )

    def next_copy(source, target, index):
        return pltpu.make_async_remote_copy(
            src_ref=source,
            dst_ref=target,
            send_sem=next_send.at[index],
            recv_sem=next_recv.at[index],
            device_id={"ctx": lax.rem(me + ctx_count - 1, ctx_count)},
            device_id_type=MESH,
        )

    def next_doc():
        return next_copy(doc_ref, doc_next, 2 * groups)

    def next_kv(group):
        return next_copy(kv_out.at[group], kv_next.at[group], 2 * group)

    def next_query(group):
        these = pl.ds(group * ratio, ratio)
        return next_copy(q_ref.at[these], q_next.at[these], 2 * group + 1)

    for shift in range(1, back + 1):

        @pl.when(me + shift < ctx_count)
        def _(shift=shift):
            doc_copy(shift).start()

    @pl.when(me < ctx_count - 1)
    def _():
        for group in range(groups):
            kv_copy(group, 1).start()
            if back > 1 and group < groups - 1:

                @pl.when(me == 0)
                def _(group=group):
                    kv_copy(group, 2, 2).start()

    loads["query"].wait()

    @pl.when(me > 0)
    def _():
        next_doc().start()
        for group in range(groups):
            next_kv(group).start()
            next_query(group).start()

    for shift in range(1, back + 1):

        @pl.when(me < shift)
        def _(shift=shift):
            doc_in[shift - 1] = jnp.full(doc_in.shape[1:], -1, jnp.int32)
            for group in range(groups):
                kv_in[group, shift - 1] = jnp.zeros(kv_in.shape[2:], kv_in.dtype)

    def kv_arrive(group, shift):
        @pl.when(me >= shift)
        def _():
            kv_copy(group, shift).wait_recv()
            if shift < back:

                relayed = (me > 1) | (shift > 1) | (group == groups - 1)

                @pl.when((me < ctx_count - 1) & relayed)
                def _():
                    kv_copy(group, shift + 1).start()

    loads["ids"].wait()
    loads["keep"].wait()
    row = lax.broadcasted_iota(jnp.int32, (half, half), 0)
    lane = lax.broadcasted_iota(jnp.int32, (half, half), 1)
    ids_row = ids_ref[...]
    ids_column = jnp.sum(jnp.where(row == lane, ids_row, 0), axis=1, keepdims=True)
    ranking = jnp.sum(
        jnp.where((ids_column == ids_row) & (row < lane), 1, 0), axis=0, keepdims=True
    )
    experts = keep_ref.shape[1]
    square_row = lax.broadcasted_iota(jnp.int32, (experts, experts), 0)
    square_lane = lax.broadcasted_iota(jnp.int32, (experts, experts), 1)
    keep_column = jnp.sum(
        jnp.where(square_row == square_lane, keep_ref[...], 0), axis=1, keepdims=True
    )
    expert_row = lax.broadcasted_iota(jnp.int32, (experts, half), 0)
    limits = jnp.sum(jnp.where(expert_row == ids_row, keep_column, 0), axis=0, keepdims=True)
    target = jnp.where(ranking < limits, ids_row * CAP + ranking, -1)
    slot_row = lax.broadcasted_iota(jnp.int32, (slots, half), 0)

    for shift in range(1, back + 1):

        @pl.when(me >= shift)
        def _(shift=shift):
            doc_copy(shift).wait_recv()

    square = lax.broadcasted_iota(jnp.int32, (tokens, tokens), 0)
    across = lax.broadcasted_iota(jnp.int32, (tokens, tokens), 1)
    scale = 1.0 / math.sqrt(size)

    def visible(doc_row, earlier):
        doc_column = jnp.sum(jnp.where(square == across, doc_row, 0), axis=1, keepdims=True)
        masks = [(across <= square) & (doc_row == doc_column)]
        masks += [other == doc_column for other in earlier]
        return jnp.concatenate([jnp.where(mask, 1.0, 0.0) for mask in masks], axis=1) > 0.5

    def attend(block, group, allowed, query, pairs):
        keys = jnp.concatenate([pair[0] for pair in pairs], axis=0)
        vals = jnp.concatenate([pair[1] for pair in pairs], axis=0)
        count = keys.shape[0]
        stacked = query[group * ratio : (group + 1) * ratio].reshape(ratio * tokens, size)
        scores = lax.dot_general(
            stacked, keys, (((1,), (1,)), ((), ())), preferred_element_type=jnp.float32
        ).reshape(ratio, tokens, count)
        masked = jnp.where(allowed[None], scores * scale, -1e30)
        highest = jnp.max(masked, axis=2, keepdims=True)
        weights = jnp.exp(masked - highest)
        totals = jnp.sum(weights, axis=2, keepdims=True)
        mixed = jnp.dot(
            weights.astype(jnp.bfloat16).reshape(ratio * tokens, count),
            vals,
            preferred_element_type=jnp.float32,
        ).reshape(ratio, tokens, size)
        mixed = (mixed / totals).astype(jnp.bfloat16)
        for head in range(ratio):
            attn[block, group, :, head * size : (head + 1) * size] = mixed[head]

    def attn_copy(block, group, rightward):
        to = me + 1 if rightward else me - 1
        sends = right_send if rightward else left_send
        return pltpu.make_async_remote_copy(
            src_ref=attn.at[block, group],
            dst_ref=attn.at[block, group],
            send_sem=sends.at[block, group],
            recv_sem=attn_recv.at[block, group],
            device_id={"ctx": lax.rem(to + ctx_count, ctx_count)},
            device_id_type=MESH,
        )

    allowed = visible(doc_ref[...], [doc_in[shift] for shift in range(back)])

    def attend_own(group):
        if back:
            kv_arrive(group, back)
        attend(
            me,
            group,
            allowed,
            q_ref,
            [kv_out.at[group]] + [kv_in.at[group, shift] for shift in range(back)],
        )
        soon = group < groups - 1

        @pl.when((me < ctx_count - 1) & (soon | (me == 0) | (rest == 1)))
        def _():
            attn_copy(me, group, True).start()

    for group in range(groups - 1):
        for shift in range(1, back):
            kv_arrive(group, shift)
        attend_own(group)

    @pl.when(me == 0)
    def _():
        attend_own(groups - 1)

    def item(turn, count):
        order = turn - 1
        spot = jnp.where(count > 0, lax.rem(order, jnp.maximum(count, 1)), 0)
        group = sum((order >= count * number).astype(jnp.int32) for number in range(1, groups))
        group = group if groups > 1 else jnp.int32(0)
        final = group == groups - 1
        active = (turn >= 1) & (turn <= groups * count)
        return group, jnp.where(final, count - spot, spot + 1), final, active

    beyond = jnp.maximum(rest - 1, 0)
    skipped = jnp.where(early, 1, 0)
    upstream = me - skipped

    def from_left(turn):
        group, far, final, active = item(turn, upstream)
        block = upstream - far

        @pl.when(active)
        def _():
            attn_copy(block, group, True).wait_recv()

            @pl.when(me < ctx_count - 1)
            def _():
                attn_copy(block, group, True).start()

                @pl.when((turn == groups * me) & (rest > 1))
                def _():
                    attn_copy(me, groups - 1, True).start()

        return block, active & final

    def from_right(turn):
        group = lax.rem(turn - 1, groups)
        block = me + 2 + (turn - 1) // groups
        final, active = group == groups - 1, turn <= groups * beyond

        @pl.when(active)
        def _():
            attn_copy(block, group, False).wait_recv()

            @pl.when(me > 0)
            def _():
                attn_copy(block, group, False).start()

        return block, active & final

    def attend_next(group):
        @pl.when(rest > 0)
        def _():
            next_kv(group).wait_recv()
            next_query(group).wait_recv()
            attend(
                me + 1,
                group,
                visible(
                    doc_next[...],
                    ([doc_ref[...]] if back else []) + [doc_in[shift] for shift in range(back - 1)],
                ),
                q_next,
                [kv_next.at[group]]
                + ([kv_out.at[group]] if back else [])
                + [kv_in.at[group, shift] for shift in range(back - 1)],
            )

            @pl.when(me > 0)
            def _():
                attn_copy(me + 1, group, False).start()

    @pl.when(rest > 0)
    def _():
        next_doc().wait_recv()

    for group in range(groups - 1):
        attend_next(group)
    for shift in range(1, back):
        kv_arrive(groups - 1, shift)
    from_left(1)
    attend_next(groups - 1)

    @pl.when(me > 0)
    def _():
        attend_own(groups - 1)

    def part_copy(block, piece):
        return pltpu.make_async_remote_copy(
            src_ref=part_out.at[block, piece],
            dst_ref=part_in.at[block, piece],
            send_sem=part_send.at[0],
            recv_sem=part_recv.at[block, piece],
            device_id={"tp": 1 - core},
            device_id_type=MESH,
        )

    def res_copy(block, peer, piece):
        return pltpu.make_async_remote_copy(
            src_ref=res_out.at[block, piece],
            dst_ref=res_in.at[me, piece],
            send_sem=res_send.at[0],
            recv_sem=res_recv.at[peer, piece],
            device_id={"ctx": block},
            device_id_type=MESH,
        )

    routes = ((1, ctx_count - 3), (-1, 2)) if ctx_count > 3 else ()

    def pass_copy(side):
        sign, source = routes[side]
        return pltpu.make_async_remote_copy(
            src_ref=res_out.at[source + 2 * sign],
            dst_ref=passing.at[side],
            send_sem=res_send.at[0],
            recv_sem=pass_recv.at[side],
            device_id={"ctx": source + sign},
            device_id_type=MESH,
        )

    def onward_copy(side, piece):
        sign, source = routes[side]
        return pltpu.make_async_remote_copy(
            src_ref=passing.at[side, piece],
            dst_ref=res_in.at[source, piece],
            send_sem=pass_send.at[side],
            recv_sem=res_recv.at[source, piece],
            device_id={"ctx": source + 2 * sign},
            device_id_type=MESH,
        )

    def pass_on():
        for side, (sign, source) in enumerate(routes):

            @pl.when(me == source + sign)
            def _(side=side):
                pass_copy(side).wait_recv()
                for piece in range(pieces):
                    onward_copy(side, piece).start()

    def slot_at(peer, block, piece):
        if aligned:
            first = pl.multiple_of(block * columns + piece * part, 128)
            return slot_in.at[peer, :, pl.ds(first, part)]
        return slot_in.at[peer, block, piece]

    def slot_copy(shift, block, index, piece):
        return pltpu.make_async_remote_copy(
            src_ref=slot_out.at[shift - 1, block, piece],
            dst_ref=slot_at(mine, block, piece),
            send_sem=slot_send.at[shift - 1],
            recv_sem=slot_recv.at[index, block, piece],
            device_id={"exp": lax.rem(mine + shift, exp_count)},
            device_id_type=MESH,
        )

    def project(block):
        for start in range(0, pieces, WIDE):
            some = range(start, min(start + WIDE, pieces))
            there = slice(start * part, (some[-1] + 1) * part)
            total = None
            for group in range(groups):
                term = jnp.dot(
                    attn[block, group],
                    weight[group * depth : (group + 1) * depth, there],
                    preferred_element_type=jnp.float32,
                )
                total = term if total is None else total + term
            for piece in some:
                here = slice((piece - start) * part, (piece - start + 1) * part)
                product[block, piece, 0] = total[:half, here]
                product[block, piece, 1] = total[half:, here]
                part_out[block, piece] = product[block, piece, 1 - core].astype(jnp.bfloat16)
                part_copy(block, piece).start()

    def finish(block, piece):
        part_copy(block, piece).wait_recv()
        return (
            product[block, piece, core] + part_in[block, piece].astype(jnp.float32)
        ).astype(jnp.bfloat16)

    def send(block):
        for piece in range(pieces):
            res_copy(block, me, piece).start()

    def place(block, piece):
        hidden = (
            residual[block, :, piece * part : (piece + 1) * part].astype(jnp.float32)
            + res_in[block, piece].astype(jnp.float32)
        ).astype(jnp.bfloat16)
        for shift in (*range(1, exp_count), 0):
            peer = lax.rem(mine + shift, exp_count)
            table = (slot_row + peer * slots == target).astype(jnp.bfloat16)
            chosen = jnp.dot(table, hidden, preferred_element_type=jnp.float32).astype(
                jnp.bfloat16
            )
            if shift == 0:
                slot_at(mine, block, piece)[...] = chosen
            else:
                slot_out[shift - 1, block, piece] = chosen
                slot_copy(shift, block, exp_count - shift - 1, piece).start()

    def absorb(shift, block, piece):
        peer = lax.rem(mine + shift, exp_count)
        if shift:
            slot_copy(1, block, shift - 1, piece).wait_recv()
        hidden = slot_at(peer, block, piece)[...]
        if aligned:
            first = pl.multiple_of(block * columns + piece * part, 128)
            columns_here = routed[:, pl.ds(first, part)]
        else:
            columns_here = routed[block, piece]
        logits[shift] += lax.dot_general(
            hidden,
            columns_here,
            (((1,), (1,)), ((), ())),
            preferred_element_type=jnp.float32,
        )
        wide = hidden.astype(jnp.float32)
        wide = wide * wide
        if aligned:
            total = wide[:, :128]
            for first in range(128, part, 128):
                total = total + wide[:, first : first + 128]
            tally[shift] += total
        else:
            tally[shift, :, :1] += jnp.sum(wide, axis=1, keepdims=True)

    loads["weight"].wait()
    project(me)

    @pl.when(rest > 0)
    def _():
        project(me + 1)

    loads["gain"].wait()
    loads["router"].wait()
    wide = gain_ref[...].astype(jnp.float32)
    for line in range(wide.shape[0]):
        there = slice(line * 128, (line + 1) * 128)
        gain_row[:, there] = wide[line : line + 1]
        router_ref[:, there] = (
            router_ref[:, there].astype(jnp.float32) * wide[line : line + 1]
        ).astype(jnp.bfloat16)
    if not aligned:
        for block in range(ctx_count):
            for piece in range(pieces):
                first = block * columns + piece * part
                routed[block, piece] = router_ref[:, first : first + part]
    else:
        routed = router_ref
    tally[...] = jnp.zeros_like(tally)
    logits[...] = jnp.zeros_like(logits)
    for block in range(ctx_count):
        loads[block].wait()

    def reply(block, now):
        for piece in range(pieces):
            res_out[block, piece] = finish(block, piece)
            if now is not None:

                @pl.when(now)
                def _(piece=piece):
                    res_copy(block, me, piece).start()

        for side, (sign, source) in enumerate(routes):

            @pl.when((me == source) & (block == source + 2 * sign))
            def _(side=side):
                pass_copy(side).start()

    def send(block):
        for piece in range(pieces):
            res_copy(block, me, piece).start()

    def order(number):
        inner = jnp.where(number <= rest, me + number, number - rest - 1)
        inner = jnp.where(number == 0, me - 1, inner)
        return jnp.where(me == 0, jnp.where(number == 0, 1, ctx_count - number), inner)

    def send_far():
        def body(number, carry):
            send(ctx_count - 1 - number)
            return carry

        lax.fori_loop(0, beyond, body, 0)

    def settle(number, before):
        block = order(number)
        for piece in range(pieces):
            res_copy(me, block, piece).wait_recv()
            if piece == 0:

                @pl.when((me == 0) & (number == 1))
                def _():
                    send_far()

            place(block, piece)
            absorb(0, block, piece)
            for shift in range(1, exp_count):
                absorb(shift, before, piece)

        direct = me > (2 if routes else 1)

        @pl.when((number == 0) & direct & (rest > 0))
        def _():
            send(0)

        @pl.when((number == 1) & (me > 0) & (rest > (2 if routes else 1)))
        def _():
            send_far()

        @pl.when(number == 0)
        def _():
            pass_on()

        return block

    last = jnp.maximum(groups * upstream - 1, groups * beyond)

    late = (rest == 1) & (me > 1)

    def own():
        for piece in range(pieces):
            res_in[me, piece] = finish(me, piece)
            place(me, piece)
            absorb(0, me, piece)

        @pl.when(rest > 0)
        def _():
            reply(me + 1, None)

        @pl.when((rest > 0) & jnp.logical_not(late))
        def _():
            send(me + 1)

    @pl.when(early)
    def _():
        for group in range(groups):
            attn_copy(me - 1, group, True).wait_recv()
        project(me - 1)

    @pl.when((me == 0) | (rest == 0))
    def _():
        own()

    @pl.when(early)
    def _():
        reply(me - 1, None)
        send(me - 1)

    def step(turn, carry):
        left, left_whole = from_left(turn + 1)
        right, right_whole = from_right(turn)

        @pl.when((turn == 1) & (me > 0) & (rest > 0))
        def _():
            own()

        whole = ((left, left_whole), (right, right_whole))
        for block, has in whole:

            @pl.when(has)
            def _(block=block):
                project(block)

        prompt = (left < me - 1) & (early | (left > 0))
        for (block, has), now in zip(whole, (prompt, None)):

            @pl.when(has)
            def _(block=block, now=now):
                reply(block, now)

        @pl.when(late & (turn == groups * me - 2))
        def _():
            send(me + 1)

        @pl.when(early & (turn == (groups - 1) * upstream))
        def _():
            settle(0, me)

        return carry

    lax.fori_loop(1, jnp.maximum(last, 1) + 1, step, 0)

    @pl.when((me > 0) & (rest > 0) | (me == 1))
    def _():
        send(me - 1)

    block = lax.fori_loop(
        jnp.where(early, 1, 0), ctx_count - 1, settle, jnp.where(early, me - 1, me)
    )
    for piece in range(pieces):
        for shift in range(1, exp_count):
            absorb(shift, block, piece)

    spread = lax.broadcasted_iota(jnp.int32, logits.shape[1:], 0) // CAP
    expert = lax.broadcasted_iota(jnp.int32, logits.shape[1:], 1)
    for shift in range(exp_count):
        peer = lax.rem(mine + shift, exp_count)
        power = tally[shift] if aligned else tally[shift, :, :1]
        power = jnp.sum(power, axis=1, keepdims=True) / width
        factor = lax.rsqrt(power + EPSILON)
        logit = jnp.sum(jnp.where(spread == expert, logits[shift], 0.0), axis=1, keepdims=True)
        gate = jax.nn.sigmoid(logit * factor)
        scale_ref[peer] = jnp.broadcast_to(gate * factor, scale_ref.shape[1:])

    @pl.when(me < ctx_count - 1)
    def _():
        for group in range(groups):
            kv_copy(group, 1).wait_send()
            if back > 1 and group < groups - 1:

                @pl.when(me == 0)
                def _(group=group):
                    kv_copy(group, 2, 2).wait_send()

            for shift in range(1, back):
                relayed = (me > 1) | (shift > 1) | (group == groups - 1)

                @pl.when((me >= shift) & relayed)
                def _(group=group, shift=shift):
                    kv_copy(group, shift + 1).wait_send()

    for shift in range(1, back + 1):

        @pl.when(me + shift < ctx_count)
        def _(shift=shift):
            doc_copy(shift).wait_send()

    @pl.when(me > 0)
    def _():
        next_doc().wait_send()
        for group in range(groups):
            next_kv(group).wait_send()
            next_query(group).wait_send()

    def sent(source, semaphore):
        pltpu.make_async_remote_copy(
            src_ref=source,
            dst_ref=source,
            send_sem=semaphore,
            recv_sem=semaphore,
            device_id={"tp": 1 - core},
            device_id_type=MESH,
        ).wait_send()

    sent(part_out, part_send.at[0])
    sent(res_out.at[pl.ds(0, ctx_count - 1)], res_send.at[0])
    for side, (sign, source) in enumerate(routes):

        @pl.when(me == source + sign)
        def _(side=side):
            sent(passing.at[side], pass_send.at[side])

    for shift in range(1, exp_count):
        sent(slot_out.at[shift - 1], slot_send.at[shift - 1])

    def drain(block, carry):
        for group in range(groups):

            @pl.when((block <= me) & (me < ctx_count - 1))
            def _(group=group):
                attn_copy(block, group, True).wait_send()

            @pl.when((block > me) & (me > 0))
            def _(group=group):
                attn_copy(block, group, False).wait_send()

        return carry

    lax.fori_loop(0, ctx_count, drain, 0)


def on_device(
    queries,
    key_states,
    values,
    doc_ids,
    residual,
    out_proj,
    norm_gain,
    router,
    expert_ids,
    keep_counts,
):
    tokens, heads, size = queries.shape[1:]
    groups = key_states.shape[2]
    ctx_count = lax.axis_size("ctx")
    exp_count = lax.axis_size("exp")
    features, columns = out_proj.shape
    half = residual.shape[1]
    width = residual.shape[2]
    experts = keep_counts.shape[0]
    owned = experts // exp_count
    slots = owned * CAP
    longest = tokens * ctx_count // 2
    back = min(ctx_count - 1, -(-(longest - 1) // tokens))
    pieces = columns // 256 if columns % 256 == 0 else 2
    part = columns // pieces
    aligned = part % 128 == 0
    vmem = pl.BlockSpec(memory_space=pltpu.VMEM)
    hbm = pl.BlockSpec(memory_space=pltpu.HBM)
    bf16, f32, i32 = jnp.bfloat16, jnp.float32, jnp.int32
    dma = pltpu.SemaphoreType.DMA
    n = ctx_count
    stream = residual[0]
    if columns % 128:
        stream = stream.reshape(half, ctx_count, columns).transpose(1, 0, 2)
    slot_shape = (exp_count, slots, width) if aligned else (exp_count, n, pieces, slots, part)
    chosen, scale, gain = pl.pallas_call(
        functools.partial(kernel, (ctx_count, exp_count, back, pieces)),
        out_shape=(
            jax.ShapeDtypeStruct(slot_shape, bf16),
            jax.ShapeDtypeStruct((exp_count, slots, 128), f32),
            jax.ShapeDtypeStruct((1, width), f32),
        ),
        in_specs=[hbm] * 10,
        out_specs=(vmem, vmem, vmem),
        scratch_shapes=[
            pltpu.VMEM((heads, tokens, size), bf16),
            pltpu.VMEM((tokens, groups, size), bf16),
            pltpu.VMEM((tokens, groups, size), bf16),
            pltpu.VMEM((1, tokens), i32),
            pltpu.VMEM((width // 128, 128), bf16),
            pltpu.VMEM((owned, width), bf16),
            pltpu.VMEM((1, half), i32),
            pltpu.VMEM((1, experts), i32),
            pltpu.VMEM((groups, 2, tokens, size), bf16),
            pltpu.VMEM((groups, back, 2, tokens, size), bf16),
            pltpu.VMEM((groups, 2, tokens, size), bf16),
            pltpu.VMEM((heads, tokens, size), bf16),
            pltpu.VMEM((1, tokens), i32),
            pltpu.VMEM((8, 128) if aligned else (n, pieces, owned, part), bf16),
            pltpu.VMEM((exp_count, slots, 128), f32),
            pltpu.VMEM((exp_count, slots, owned), f32),
            pltpu.VMEM((back, 1, tokens), i32),
            pltpu.VMEM((n, groups, tokens, features // groups), bf16),
            pltpu.VMEM((features, columns), bf16),
            pltpu.VMEM((n, half, columns), bf16),
            pltpu.VMEM((n, pieces, 2, half, part), f32),
            pltpu.VMEM((n, pieces, half, part), bf16),
            pltpu.VMEM((n, pieces, half, part), bf16),
            pltpu.VMEM((n, pieces, half, part), bf16),
            pltpu.VMEM((n, pieces, half, part), bf16),
            pltpu.VMEM((2, pieces, half, part), bf16),
            pltpu.VMEM((exp_count - 1, n, pieces, slots, part), bf16),
            dma((9 + n,)),
            dma((groups, back)),
            dma((groups, back)),
            dma((back,)),
            dma((back,)),
            dma((2 * groups + 1,)),
            dma((2 * groups + 1,)),
            dma((n, groups)),
            dma((n, groups)),
            dma((n, groups)),
            dma((1,)),
            dma((n, pieces)),
            dma((1,)),
            dma((n, pieces)),
            dma((2,)),
            dma((2,)),
            dma((exp_count - 1,)),
            dma((exp_count - 1, n, pieces)),
        ],
        compiler_params=pltpu.CompilerParams(
            collective_id=0, has_side_effects=True, vmem_limit_bytes=40 << 20
        ),
    )(
        *(
            pltpu.with_memory_space_constraint(operand, pltpu.HBM)
            for operand in (
                queries[0].transpose(1, 0, 2),
                key_states[0],
                values[0],
                doc_ids,
                stream,
                out_proj,
                norm_gain.reshape(width // 128, 128),
                router.T,
                expert_ids.reshape(1, half),
                keep_counts.reshape(1, experts),
            )
        )
    )
    if not aligned:
        chosen = chosen.transpose(0, 3, 1, 2, 4).reshape(exp_count, slots, width)
    scaled = chosen.astype(f32) * scale[:, :, :1] * gain
    return scaled.astype(bf16).reshape(exp_count, owned, CAP, width)


def solution(mesh):
    placed = (
        P(("groups", "exp"), "ctx", "tp", None),
        P(("groups", "exp"), "ctx", "tp", None),
        P(("groups", "exp"), "ctx", "tp", None),
        P(("groups", "exp"), "ctx"),
        P(("groups", "exp"), ("ctx", "tp"), None),
        P("tp", "ctx"),
        P(),
        P(None, "exp"),
        P(("groups", "exp"), ("ctx", "tp"), None),
        P("groups"),
    )
    return jax.shard_map(
        on_device,
        mesh=mesh,
        in_specs=placed,
        out_specs=P(("groups", "ctx", "tp"), "exp", None, None),
        check_vma=False,
    )
```

```python
import functools
import math

import jax
import jax.numpy as jnp
from jax import lax
from jax.experimental import pallas as pl
from jax.experimental.pallas import tpu as pltpu
from jax.sharding import PartitionSpec as P

CAP = 2
EPSILON = 1e-05
WIDE = 5
MESH = pl.DeviceIdType.MESH


def kernel(
    sizes,
    q_hbm,
    key_hbm,
    value_hbm,
    doc_hbm,
    residual_hbm,
    weight_hbm,
    gain_hbm,
    router_hbm,
    ids_hbm,
    keep_hbm,
    slot_in,
    scale_ref,
    gain_row,
    q_ref,
    key_ref,
    value_ref,
    doc_ref,
    gain_ref,
    router_ref,
    ids_ref,
    keep_ref,
    kv_out,
    kv_in,
    kv_next,
    q_next,
    doc_next,
    routed,
    tally,
    logits,
    doc_in,
    attn,
    weight,
    residual,
    product,
    part_out,
    part_in,
    res_out,
    res_in,
    passing,
    slot_out,
    load_sem,
    kv_send,
    kv_recv,
    doc_send,
    doc_recv,
    next_send,
    next_recv,
    right_send,
    left_send,
    attn_recv,
    part_send,
    part_recv,
    res_send,
    res_recv,
    pass_send,
    pass_recv,
    slot_send,
    slot_recv,
):
    ctx_count, exp_count, back, pieces = sizes
    heads, tokens, size = q_ref.shape
    groups = kv_out.shape[0]
    ratio = heads // groups
    half = tokens // 2
    columns = weight.shape[1]
    depth = weight.shape[0] // groups
    slots = slot_out.shape[3]
    part = columns // pieces
    width = columns * ctx_count
    aligned = part % 128 == 0
    me = lax.axis_index("ctx")
    mine = lax.axis_index("exp")
    core = lax.axis_index("tp")
    rest = ctx_count - 1 - me
    early = (rest == 0) & (me > 1)

    barrier = pltpu.get_barrier_semaphore()
    for shift in range(1, ctx_count):
        pl.semaphore_signal(
            barrier,
            inc=1,
            device_id={"ctx": lax.rem(me + shift, ctx_count)},
            device_id_type=MESH,
        )
    for shift in range(1, exp_count):
        pl.semaphore_signal(
            barrier,
            inc=1,
            device_id={"exp": lax.rem(mine + shift, exp_count)},
            device_id_type=MESH,
        )
    pl.semaphore_signal(barrier, inc=1, device_id={"tp": 1 - core}, device_id_type=MESH)

    loads = {}

    def load(name, source, target):
        loads[name] = pltpu.make_async_copy(source, target, load_sem.at[len(loads)])
        loads[name].start()

    load("key", key_hbm, key_ref)
    load("value", value_hbm, value_ref)
    load("doc", doc_hbm, doc_ref)
    load("query", q_hbm, q_ref)
    load("ids", ids_hbm, ids_ref)
    load("keep", keep_hbm, keep_ref)
    load("gain", gain_hbm, gain_ref)
    load("router", router_hbm, router_ref)
    load("weight", weight_hbm, weight)
    for block in range(ctx_count):
        there = slice(block * columns, (block + 1) * columns)
        load(
            block,
            residual_hbm.at[:, there] if columns % 128 == 0 else residual_hbm.at[block],
            residual.at[block],
        )

    loads["key"].wait()
    loads["value"].wait()
    for group in range(groups):
        kv_out[group, 0] = key_ref[:, group, :]
        kv_out[group, 1] = value_ref[:, group, :]
    loads["doc"].wait()

    pl.semaphore_wait(barrier, ctx_count + exp_count - 1)

    def kv_copy(group, shift, hops=1):
        return pltpu.make_async_remote_copy(
            src_ref=kv_out.at[group] if shift == hops else kv_in.at[group, shift - 2],
            dst_ref=kv_in.at[group, shift - 1],
            send_sem=kv_send.at[group, shift - 1],
            recv_sem=kv_recv.at[group, shift - 1],
            device_id={"ctx": lax.rem(me + hops, ctx_count)},
            device_id_type=MESH,
        )

    def doc_copy(shift):
        return pltpu.make_async_remote_copy(
            src_ref=doc_ref,
            dst_ref=doc_in.at[shift - 1],
            send_sem=doc_send.at[shift - 1],
            recv_sem=doc_recv.at[shift - 1],
            device_id={"ctx": lax.rem(me + shift, ctx_count)},
            device_id_type=MESH,
        )

    def next_copy(source, target, index):
        return pltpu.make_async_remote_copy(
            src_ref=source,
            dst_ref=target,
            send_sem=next_send.at[index],
            recv_sem=next_recv.at[index],
            device_id={"ctx": lax.rem(me + ctx_count - 1, ctx_count)},
            device_id_type=MESH,
        )

    def next_doc():
        return next_copy(doc_ref, doc_next, 2 * groups)

    def next_kv(group):
        return next_copy(kv_out.at[group], kv_next.at[group], 2 * group)

    def next_query(group):
        these = pl.ds(group * ratio, ratio)
        return next_copy(q_ref.at[these], q_next.at[these], 2 * group + 1)

    for shift in range(1, back + 1):

        @pl.when(me + shift < ctx_count)
        def _(shift=shift):
            doc_copy(shift).start()

    @pl.when(me < ctx_count - 1)
    def _():
        for group in range(groups):
            kv_copy(group, 1).start()
            if back > 1 and group < groups - 1:

                @pl.when(me == 0)
                def _(group=group):
                    kv_copy(group, 2, 2).start()

    loads["query"].wait()

    @pl.when(me > 0)
    def _():
        next_doc().start()
        for group in range(groups):
            next_kv(group).start()
            next_query(group).start()

    for shift in range(1, back + 1):

        @pl.when(me < shift)
        def _(shift=shift):
            doc_in[shift - 1] = jnp.full(doc_in.shape[1:], -1, jnp.int32)
            for group in range(groups):
                kv_in[group, shift - 1] = jnp.zeros(kv_in.shape[2:], kv_in.dtype)

    def kv_arrive(group, shift):
        @pl.when(me >= shift)
        def _():
            kv_copy(group, shift).wait_recv()
            if shift < back:

                relayed = (me > 1) | (shift > 1) | (group == groups - 1)

                @pl.when((me < ctx_count - 1) & relayed)
                def _():
                    kv_copy(group, shift + 1).start()

    loads["ids"].wait()
    loads["keep"].wait()
    row = lax.broadcasted_iota(jnp.int32, (half, half), 0)
    lane = lax.broadcasted_iota(jnp.int32, (half, half), 1)
    ids_row = ids_ref[...]
    ids_column = jnp.sum(jnp.where(row == lane, ids_row, 0), axis=1, keepdims=True)
    ranking = jnp.sum(
        jnp.where((ids_column == ids_row) & (row < lane), 1, 0), axis=0, keepdims=True
    )
    experts = keep_ref.shape[1]
    square_row = lax.broadcasted_iota(jnp.int32, (experts, experts), 0)
    square_lane = lax.broadcasted_iota(jnp.int32, (experts, experts), 1)
    keep_column = jnp.sum(
        jnp.where(square_row == square_lane, keep_ref[...], 0), axis=1, keepdims=True
    )
    expert_row = lax.broadcasted_iota(jnp.int32, (experts, half), 0)
    limits = jnp.sum(jnp.where(expert_row == ids_row, keep_column, 0), axis=0, keepdims=True)
    target = jnp.where(ranking < limits, ids_row * CAP + ranking, -1)
    slot_row = lax.broadcasted_iota(jnp.int32, (slots, half), 0)

    for shift in range(1, back + 1):

        @pl.when(me >= shift)
        def _(shift=shift):
            doc_copy(shift).wait_recv()

    square = lax.broadcasted_iota(jnp.int32, (tokens, tokens), 0)
    across = lax.broadcasted_iota(jnp.int32, (tokens, tokens), 1)
    scale = 1.0 / math.sqrt(size)

    def visible(doc_row, earlier):
        doc_column = jnp.sum(jnp.where(square == across, doc_row, 0), axis=1, keepdims=True)
        masks = [(across <= square) & (doc_row == doc_column)]
        masks += [other == doc_column for other in earlier]
        return jnp.concatenate([jnp.where(mask, 1.0, 0.0) for mask in masks], axis=1) > 0.5

    def attend(block, group, allowed, query, pairs):
        keys = jnp.concatenate([pair[0] for pair in pairs], axis=0)
        vals = jnp.concatenate([pair[1] for pair in pairs], axis=0)
        count = keys.shape[0]
        stacked = query[group * ratio : (group + 1) * ratio].reshape(ratio * tokens, size)
        scores = lax.dot_general(
            stacked, keys, (((1,), (1,)), ((), ())), preferred_element_type=jnp.float32
        ).reshape(ratio, tokens, count)
        masked = jnp.where(allowed[None], scores * scale, -1e30)
        highest = jnp.max(masked, axis=2, keepdims=True)
        weights = jnp.exp(masked - highest)
        totals = jnp.sum(weights, axis=2, keepdims=True)
        mixed = jnp.dot(
            weights.astype(jnp.bfloat16).reshape(ratio * tokens, count),
            vals,
            preferred_element_type=jnp.float32,
        ).reshape(ratio, tokens, size)
        mixed = (mixed / totals).astype(jnp.bfloat16)
        for head in range(ratio):
            attn[block, group, :, head * size : (head + 1) * size] = mixed[head]

    def attn_copy(block, group, rightward):
        to = me + 1 if rightward else me - 1
        sends = right_send if rightward else left_send
        return pltpu.make_async_remote_copy(
            src_ref=attn.at[block, group],
            dst_ref=attn.at[block, group],
            send_sem=sends.at[block, group],
            recv_sem=attn_recv.at[block, group],
            device_id={"ctx": lax.rem(to + ctx_count, ctx_count)},
            device_id_type=MESH,
        )

    allowed = visible(doc_ref[...], [doc_in[shift] for shift in range(back)])

    def attend_own(group):
        if back:
            kv_arrive(group, back)
        attend(
            me,
            group,
            allowed,
            q_ref,
            [kv_out.at[group]] + [kv_in.at[group, shift] for shift in range(back)],
        )
        soon = group < groups - 1

        @pl.when((me < ctx_count - 1) & (soon | (me == 0) | (rest == 1)))
        def _():
            attn_copy(me, group, True).start()

    def kv_last():
        for shift in range(1, back):
            kv_arrive(groups - 1, shift)

    for group in range(groups - 1):
        for shift in range(1, back):
            kv_arrive(group, shift)
        if group == 0:

            @pl.when(me >= back)
            def _():
                kv_last()

        attend_own(group)

    @pl.when(me == 0)
    def _():
        attend_own(groups - 1)

    def item(turn, count):
        order = turn - 1
        spot = jnp.where(count > 0, lax.rem(order, jnp.maximum(count, 1)), 0)
        group = sum((order >= count * number).astype(jnp.int32) for number in range(1, groups))
        group = group if groups > 1 else jnp.int32(0)
        final = group == groups - 1
        active = (turn >= 1) & (turn <= groups * count)
        return group, jnp.where(final, count - spot, spot + 1), final, active

    beyond = jnp.maximum(rest - 1, 0)
    skipped = jnp.where(early, 1, 0)
    upstream = me - skipped

    def from_left(turn):
        group, far, final, active = item(turn, upstream)
        block = upstream - far

        @pl.when(active)
        def _():
            attn_copy(block, group, True).wait_recv()

            @pl.when(me < ctx_count - 1)
            def _():
                attn_copy(block, group, True).start()

                @pl.when((turn == groups * me) & (rest > 1))
                def _():
                    attn_copy(me, groups - 1, True).start()

        return block, active & final

    def from_right(turn):
        group = lax.rem(turn - 1, groups)
        block = me + 2 + (turn - 1) // groups
        final, active = group == groups - 1, turn <= groups * beyond

        @pl.when(active)
        def _():
            attn_copy(block, group, False).wait_recv()

            @pl.when(me > 0)
            def _():
                attn_copy(block, group, False).start()

        return block, active & final

    def attend_next(group):
        @pl.when(rest > 0)
        def _():
            next_kv(group).wait_recv()
            next_query(group).wait_recv()
            attend(
                me + 1,
                group,
                visible(
                    doc_next[...],
                    ([doc_ref[...]] if back else []) + [doc_in[shift] for shift in range(back - 1)],
                ),
                q_next,
                [kv_next.at[group]]
                + ([kv_out.at[group]] if back else [])
                + [kv_in.at[group, shift] for shift in range(back - 1)],
            )

            @pl.when(me > 0)
            def _():
                attn_copy(me + 1, group, False).start()

    @pl.when(rest > 0)
    def _():
        next_doc().wait_recv()

    for group in range(groups - 1):
        attend_next(group)

    @pl.when((me < back) | (groups == 1))
    def _():
        kv_last()

    from_left(1)
    attend_next(groups - 1)

    @pl.when(me > 0)
    def _():
        attend_own(groups - 1)

    def part_copy(block, piece):
        return pltpu.make_async_remote_copy(
            src_ref=part_out.at[block, piece],
            dst_ref=part_in.at[block, piece],
            send_sem=part_send.at[0],
            recv_sem=part_recv.at[block, piece],
            device_id={"tp": 1 - core},
            device_id_type=MESH,
        )

    def res_copy(block, peer, piece):
        return pltpu.make_async_remote_copy(
            src_ref=res_out.at[block, piece],
            dst_ref=res_in.at[me, piece],
            send_sem=res_send.at[0],
            recv_sem=res_recv.at[peer, piece],
            device_id={"ctx": block},
            device_id_type=MESH,
        )

    routes = ((1, ctx_count - 3), (-1, 2)) if ctx_count > 3 else ()

    def pass_copy(side):
        sign, source = routes[side]
        return pltpu.make_async_remote_copy(
            src_ref=res_out.at[source + 2 * sign],
            dst_ref=passing.at[side],
            send_sem=res_send.at[0],
            recv_sem=pass_recv.at[side],
            device_id={"ctx": source + sign},
            device_id_type=MESH,
        )

    def onward_copy(side, piece):
        sign, source = routes[side]
        return pltpu.make_async_remote_copy(
            src_ref=passing.at[side, piece],
            dst_ref=res_in.at[source, piece],
            send_sem=pass_send.at[side],
            recv_sem=res_recv.at[source, piece],
            device_id={"ctx": source + 2 * sign},
            device_id_type=MESH,
        )

    def pass_on():
        for side, (sign, source) in enumerate(routes):

            @pl.when(me == source + sign)
            def _(side=side):
                pass_copy(side).wait_recv()
                for piece in range(pieces):
                    onward_copy(side, piece).start()

    def slot_at(peer, block, piece):
        if aligned:
            first = pl.multiple_of(block * columns + piece * part, 128)
            return slot_in.at[peer, :, pl.ds(first, part)]
        return slot_in.at[peer, block, piece]

    def slot_copy(shift, block, index, piece):
        return pltpu.make_async_remote_copy(
            src_ref=slot_out.at[shift - 1, block, piece],
            dst_ref=slot_at(mine, block, piece),
            send_sem=slot_send.at[shift - 1],
            recv_sem=slot_recv.at[index, block, piece],
            device_id={"exp": lax.rem(mine + shift, exp_count)},
            device_id_type=MESH,
        )

    def project(block):
        for start in range(0, pieces, WIDE):
            some = range(start, min(start + WIDE, pieces))
            there = slice(start * part, (some[-1] + 1) * part)
            total = None
            for group in range(groups):
                term = jnp.dot(
                    attn[block, group],
                    weight[group * depth : (group + 1) * depth, there],
                    preferred_element_type=jnp.float32,
                )
                total = term if total is None else total + term
            for piece in some:
                here = slice((piece - start) * part, (piece - start + 1) * part)
                product[block, piece, 0] = total[:half, here]
                product[block, piece, 1] = total[half:, here]
                part_out[block, piece] = product[block, piece, 1 - core].astype(jnp.bfloat16)
                part_copy(block, piece).start()

    def finish(block, piece):
        part_copy(block, piece).wait_recv()
        return (
            product[block, piece, core] + part_in[block, piece].astype(jnp.float32)
        ).astype(jnp.bfloat16)

    def send(block):
        for piece in range(pieces):
            res_copy(block, me, piece).start()

    def place(block, piece):
        hidden = (
            residual[block, :, piece * part : (piece + 1) * part].astype(jnp.float32)
            + res_in[block, piece].astype(jnp.float32)
        ).astype(jnp.bfloat16)
        for shift in (*range(1, exp_count), 0):
            peer = lax.rem(mine + shift, exp_count)
            table = (slot_row + peer * slots == target).astype(jnp.bfloat16)
            chosen = jnp.dot(table, hidden, preferred_element_type=jnp.float32).astype(
                jnp.bfloat16
            )
            if shift == 0:
                slot_at(mine, block, piece)[...] = chosen
            else:
                slot_out[shift - 1, block, piece] = chosen
                slot_copy(shift, block, exp_count - shift - 1, piece).start()

    def absorb(shift, block, piece):
        peer = lax.rem(mine + shift, exp_count)
        if shift:
            slot_copy(1, block, shift - 1, piece).wait_recv()
        hidden = slot_at(peer, block, piece)[...]
        if aligned:
            first = pl.multiple_of(block * columns + piece * part, 128)
            columns_here = routed[:, pl.ds(first, part)]
        else:
            columns_here = routed[block, piece]
        logits[shift] += lax.dot_general(
            hidden,
            columns_here,
            (((1,), (1,)), ((), ())),
            preferred_element_type=jnp.float32,
        )
        wide = hidden.astype(jnp.float32)
        wide = wide * wide
        if aligned:
            total = wide[:, :128]
            for first in range(128, part, 128):
                total = total + wide[:, first : first + 128]
            tally[shift] += total
        else:
            tally[shift, :, :1] += jnp.sum(wide, axis=1, keepdims=True)

    loads["weight"].wait()
    project(me)

    @pl.when(rest > 0)
    def _():
        project(me + 1)

    loads["gain"].wait()
    loads["router"].wait()
    wide = gain_ref[...].astype(jnp.float32)
    for line in range(wide.shape[0]):
        there = slice(line * 128, (line + 1) * 128)
        gain_row[:, there] = wide[line : line + 1]
        router_ref[:, there] = (
            router_ref[:, there].astype(jnp.float32) * wide[line : line + 1]
        ).astype(jnp.bfloat16)
    if not aligned:
        for block in range(ctx_count):
            for piece in range(pieces):
                first = block * columns + piece * part
                routed[block, piece] = router_ref[:, first : first + part]
    else:
        routed = router_ref
    tally[...] = jnp.zeros_like(tally)
    logits[...] = jnp.zeros_like(logits)
    for block in range(ctx_count):
        loads[block].wait()

    def reply(block, now):
        for piece in range(pieces):
            res_out[block, piece] = finish(block, piece)
            if now is not None:

                @pl.when(now)
                def _(piece=piece):
                    res_copy(block, me, piece).start()

        for side, (sign, source) in enumerate(routes):

            @pl.when((me == source) & (block == source + 2 * sign))
            def _(side=side):
                pass_copy(side).start()

    def send(block):
        for piece in range(pieces):
            res_copy(block, me, piece).start()

    def order(number):
        inner = jnp.where(number <= rest, me + number, number - rest - 1)
        inner = jnp.where(number == 0, me - 1, inner)
        return jnp.where(me == 0, jnp.where(number == 0, 1, ctx_count - number), inner)

    def send_far():
        def body(number, carry):
            send(ctx_count - 1 - number)
            return carry

        lax.fori_loop(0, beyond, body, 0)

    def settle(number, before):
        block = order(number)
        for piece in range(pieces):
            res_copy(me, block, piece).wait_recv()
            if piece == 0:

                @pl.when((me == 0) & (number == 1))
                def _():
                    send_far()

            place(block, piece)
            absorb(0, block, piece)
            for shift in range(1, exp_count):
                absorb(shift, before, piece)

        direct = me > (2 if routes else 1)

        @pl.when((number == 0) & direct & (rest > 0))
        def _():
            send(0)

        @pl.when((number == 1) & (me > 0) & (rest > (2 if routes else 1)))
        def _():
            send_far()

        @pl.when(number == 0)
        def _():
            pass_on()

        return block

    last = jnp.maximum(groups * upstream - 1, groups * beyond)

    late = (rest == 1) & (me > 1)

    def own():
        for piece in range(pieces):
            res_in[me, piece] = finish(me, piece)
            place(me, piece)
            absorb(0, me, piece)

        @pl.when(rest > 0)
        def _():
            reply(me + 1, None)

        @pl.when((rest > 0) & jnp.logical_not(late))
        def _():
            send(me + 1)

    @pl.when(early)
    def _():
        for group in range(groups):
            attn_copy(me - 1, group, True).wait_recv()
        project(me - 1)

    @pl.when((me == 0) | (rest == 0))
    def _():
        own()

    @pl.when(early)
    def _():
        reply(me - 1, None)
        send(me - 1)

    def step(turn, carry):
        left, left_whole = from_left(turn + 1)
        right, right_whole = from_right(turn)

        @pl.when((turn == 1) & (me > 0) & (rest > 0))
        def _():
            own()

        whole = ((left, left_whole), (right, right_whole))
        for block, has in whole:

            @pl.when(has)
            def _(block=block):
                project(block)

        prompt = (left < me - 1) & (early | (left > 0))
        for (block, has), now in zip(whole, (prompt, None)):

            @pl.when(has)
            def _(block=block, now=now):
                reply(block, now)

        @pl.when(late & (turn == groups * me - 2))
        def _():
            send(me + 1)

        @pl.when(early & (turn == (groups - 1) * upstream))
        def _():
            settle(0, me)

        return carry

    lax.fori_loop(1, jnp.maximum(last, 1) + 1, step, 0)

    @pl.when((me > 0) & (rest > 0) | (me == 1))
    def _():
        send(me - 1)

    block = lax.fori_loop(
        jnp.where(early, 1, 0), ctx_count - 1, settle, jnp.where(early, me - 1, me)
    )
    for piece in range(pieces):
        for shift in range(1, exp_count):
            absorb(shift, block, piece)

    spread = lax.broadcasted_iota(jnp.int32, logits.shape[1:], 0) // CAP
    expert = lax.broadcasted_iota(jnp.int32, logits.shape[1:], 1)
    for shift in range(exp_count):
        peer = lax.rem(mine + shift, exp_count)
        power = tally[shift] if aligned else tally[shift, :, :1]
        power = jnp.sum(power, axis=1, keepdims=True) / width
        factor = lax.rsqrt(power + EPSILON)
        logit = jnp.sum(jnp.where(spread == expert, logits[shift], 0.0), axis=1, keepdims=True)
        gate = jax.nn.sigmoid(logit * factor)
        scale_ref[peer] = jnp.broadcast_to(gate * factor, scale_ref.shape[1:])

    @pl.when(me < ctx_count - 1)
    def _():
        for group in range(groups):
            kv_copy(group, 1).wait_send()
            if back > 1 and group < groups - 1:

                @pl.when(me == 0)
                def _(group=group):
                    kv_copy(group, 2, 2).wait_send()

            for shift in range(1, back):
                relayed = (me > 1) | (shift > 1) | (group == groups - 1)

                @pl.when((me >= shift) & relayed)
                def _(group=group, shift=shift):
                    kv_copy(group, shift + 1).wait_send()

    for shift in range(1, back + 1):

        @pl.when(me + shift < ctx_count)
        def _(shift=shift):
            doc_copy(shift).wait_send()

    @pl.when(me > 0)
    def _():
        next_doc().wait_send()
        for group in range(groups):
            next_kv(group).wait_send()
            next_query(group).wait_send()

    def sent(source, semaphore):
        pltpu.make_async_remote_copy(
            src_ref=source,
            dst_ref=source,
            send_sem=semaphore,
            recv_sem=semaphore,
            device_id={"tp": 1 - core},
            device_id_type=MESH,
        ).wait_send()

    sent(part_out, part_send.at[0])
    sent(res_out.at[pl.ds(0, ctx_count - 1)], res_send.at[0])
    for side, (sign, source) in enumerate(routes):

        @pl.when(me == source + sign)
        def _(side=side):
            sent(passing.at[side], pass_send.at[side])

    for shift in range(1, exp_count):
        sent(slot_out.at[shift - 1], slot_send.at[shift - 1])

    def drain(block, carry):
        for group in range(groups):

            @pl.when((block <= me) & (me < ctx_count - 1))
            def _(group=group):
                attn_copy(block, group, True).wait_send()

            @pl.when((block > me) & (me > 0))
            def _(group=group):
                attn_copy(block, group, False).wait_send()

        return carry

    lax.fori_loop(0, ctx_count, drain, 0)


def on_device(
    queries,
    key_states,
    values,
    doc_ids,
    residual,
    out_proj,
    norm_gain,
    router,
    expert_ids,
    keep_counts,
):
    tokens, heads, size = queries.shape[1:]
    groups = key_states.shape[2]
    ctx_count = lax.axis_size("ctx")
    exp_count = lax.axis_size("exp")
    features, columns = out_proj.shape
    half = residual.shape[1]
    width = residual.shape[2]
    experts = keep_counts.shape[0]
    owned = experts // exp_count
    slots = owned * CAP
    longest = tokens * ctx_count // 2
    back = min(ctx_count - 1, -(-(longest - 1) // tokens))
    pieces = columns // 256 if columns % 256 == 0 else 2
    part = columns // pieces
    aligned = part % 128 == 0
    vmem = pl.BlockSpec(memory_space=pltpu.VMEM)
    hbm = pl.BlockSpec(memory_space=pltpu.HBM)
    bf16, f32, i32 = jnp.bfloat16, jnp.float32, jnp.int32
    dma = pltpu.SemaphoreType.DMA
    n = ctx_count
    stream = residual[0]
    if columns % 128:
        stream = stream.reshape(half, ctx_count, columns).transpose(1, 0, 2)
    slot_shape = (exp_count, slots, width) if aligned else (exp_count, n, pieces, slots, part)
    chosen, scale, gain = pl.pallas_call(
        functools.partial(kernel, (ctx_count, exp_count, back, pieces)),
        out_shape=(
            jax.ShapeDtypeStruct(slot_shape, bf16),
            jax.ShapeDtypeStruct((exp_count, slots, 128), f32),
            jax.ShapeDtypeStruct((1, width), f32),
        ),
        in_specs=[hbm] * 10,
        out_specs=(vmem, vmem, vmem),
        scratch_shapes=[
            pltpu.VMEM((heads, tokens, size), bf16),
            pltpu.VMEM((tokens, groups, size), bf16),
            pltpu.VMEM((tokens, groups, size), bf16),
            pltpu.VMEM((1, tokens), i32),
            pltpu.VMEM((width // 128, 128), bf16),
            pltpu.VMEM((owned, width), bf16),
            pltpu.VMEM((1, half), i32),
            pltpu.VMEM((1, experts), i32),
            pltpu.VMEM((groups, 2, tokens, size), bf16),
            pltpu.VMEM((groups, back, 2, tokens, size), bf16),
            pltpu.VMEM((groups, 2, tokens, size), bf16),
            pltpu.VMEM((heads, tokens, size), bf16),
            pltpu.VMEM((1, tokens), i32),
            pltpu.VMEM((8, 128) if aligned else (n, pieces, owned, part), bf16),
            pltpu.VMEM((exp_count, slots, 128), f32),
            pltpu.VMEM((exp_count, slots, owned), f32),
            pltpu.VMEM((back, 1, tokens), i32),
            pltpu.VMEM((n, groups, tokens, features // groups), bf16),
            pltpu.VMEM((features, columns), bf16),
            pltpu.VMEM((n, half, columns), bf16),
            pltpu.VMEM((n, pieces, 2, half, part), f32),
            pltpu.VMEM((n, pieces, half, part), bf16),
            pltpu.VMEM((n, pieces, half, part), bf16),
            pltpu.VMEM((n, pieces, half, part), bf16),
            pltpu.VMEM((n, pieces, half, part), bf16),
            pltpu.VMEM((2, pieces, half, part), bf16),
            pltpu.VMEM((exp_count - 1, n, pieces, slots, part), bf16),
            dma((9 + n,)),
            dma((groups, back)),
            dma((groups, back)),
            dma((back,)),
            dma((back,)),
            dma((2 * groups + 1,)),
            dma((2 * groups + 1,)),
            dma((n, groups)),
            dma((n, groups)),
            dma((n, groups)),
            dma((1,)),
            dma((n, pieces)),
            dma((1,)),
            dma((n, pieces)),
            dma((2,)),
            dma((2,)),
            dma((exp_count - 1,)),
            dma((exp_count - 1, n, pieces)),
        ],
        compiler_params=pltpu.CompilerParams(
            collective_id=0, has_side_effects=True, vmem_limit_bytes=40 << 20
        ),
    )(
        *(
            pltpu.with_memory_space_constraint(operand, pltpu.HBM)
            for operand in (
                queries[0].transpose(1, 0, 2),
                key_states[0],
                values[0],
                doc_ids,
                stream,
                out_proj,
                norm_gain.reshape(width // 128, 128),
                router.T,
                expert_ids.reshape(1, half),
                keep_counts.reshape(1, experts),
            )
        )
    )
    if not aligned:
        chosen = chosen.transpose(0, 3, 1, 2, 4).reshape(exp_count, slots, width)
    scaled = chosen.astype(f32) * scale[:, :, :1] * gain
    return scaled.astype(bf16).reshape(exp_count, owned, CAP, width)


def solution(mesh):
    placed = (
        P(("groups", "exp"), "ctx", "tp", None),
        P(("groups", "exp"), "ctx", "tp", None),
        P(("groups", "exp"), "ctx", "tp", None),
        P(("groups", "exp"), "ctx"),
        P(("groups", "exp"), ("ctx", "tp"), None),
        P("tp", "ctx"),
        P(),
        P(None, "exp"),
        P(("groups", "exp"), ("ctx", "tp"), None),
        P("groups"),
    )
    return jax.shard_map(
        on_device,
        mesh=mesh,
        in_specs=placed,
        out_specs=P(("groups", "ctx", "tp"), "exp", None, None),
        check_vma=False,
    )
```

```python
import functools
import math

import jax
import jax.numpy as jnp
from jax import lax
from jax.experimental import pallas as pl
from jax.experimental.pallas import tpu as pltpu
from jax.sharding import PartitionSpec as P

CAP = 2
EPSILON = 1e-05
WIDE = 5
MESH = pl.DeviceIdType.MESH


def kernel(
    sizes,
    q_hbm,
    key_hbm,
    value_hbm,
    doc_hbm,
    residual_hbm,
    weight_hbm,
    gain_hbm,
    router_hbm,
    ids_hbm,
    keep_hbm,
    slot_in,
    scale_ref,
    gain_row,
    q_ref,
    key_ref,
    value_ref,
    doc_ref,
    gain_ref,
    router_ref,
    ids_ref,
    keep_ref,
    kv_out,
    kv_in,
    kv_next,
    q_next,
    doc_next,
    routed,
    tally,
    logits,
    doc_in,
    attn,
    weight,
    residual,
    product,
    part_out,
    part_in,
    res_out,
    res_in,
    passing,
    slot_out,
    load_sem,
    kv_send,
    kv_recv,
    doc_send,
    doc_recv,
    next_send,
    next_recv,
    right_send,
    left_send,
    attn_recv,
    part_send,
    part_recv,
    res_send,
    res_recv,
    pass_send,
    pass_recv,
    slot_send,
    slot_recv,
):
    ctx_count, exp_count, back, pieces = sizes
    heads, tokens, size = q_ref.shape
    groups = kv_out.shape[0]
    ratio = heads // groups
    half = tokens // 2
    columns = weight.shape[1]
    depth = weight.shape[0] // groups
    slots = slot_out.shape[3]
    part = columns // pieces
    width = columns * ctx_count
    aligned = part % 128 == 0
    me = lax.axis_index("ctx")
    mine = lax.axis_index("exp")
    core = lax.axis_index("tp")
    rest = ctx_count - 1 - me
    early = (rest == 0) & (me > 1)

    barrier = pltpu.get_barrier_semaphore()
    for shift in range(1, ctx_count):
        pl.semaphore_signal(
            barrier,
            inc=1,
            device_id={"ctx": lax.rem(me + shift, ctx_count)},
            device_id_type=MESH,
        )
    for shift in range(1, exp_count):
        pl.semaphore_signal(
            barrier,
            inc=1,
            device_id={"exp": lax.rem(mine + shift, exp_count)},
            device_id_type=MESH,
        )
    pl.semaphore_signal(barrier, inc=1, device_id={"tp": 1 - core}, device_id_type=MESH)

    loads = {}

    def load(name, source, target):
        loads[name] = pltpu.make_async_copy(source, target, load_sem.at[len(loads)])
        loads[name].start()

    load("key", key_hbm, key_ref)
    load("value", value_hbm, value_ref)
    load("doc", doc_hbm, doc_ref)
    load("query", q_hbm, q_ref)
    load("ids", ids_hbm, ids_ref)
    load("keep", keep_hbm, keep_ref)
    load("gain", gain_hbm, gain_ref)
    load("router", router_hbm, router_ref)
    load("weight", weight_hbm, weight)
    for block in range(ctx_count):
        there = slice(block * columns, (block + 1) * columns)
        pltpu.make_async_copy(
            residual_hbm.at[:, there] if columns % 128 == 0 else residual_hbm.at[block],
            residual.at[block],
            load_sem.at[len(loads)],
        ).start()

    loads["key"].wait()
    loads["value"].wait()
    for group in range(groups):
        kv_out[group, 0] = key_ref[:, group, :]
        kv_out[group, 1] = value_ref[:, group, :]
    loads["doc"].wait()

    pl.semaphore_wait(barrier, ctx_count + exp_count - 1)

    def kv_copy(group, shift, hops=1):
        return pltpu.make_async_remote_copy(
            src_ref=kv_out.at[group] if shift == hops else kv_in.at[group, shift - 2],
            dst_ref=kv_in.at[group, shift - 1],
            send_sem=kv_send.at[group, shift - 1],
            recv_sem=kv_recv.at[group, shift - 1],
            device_id={"ctx": lax.rem(me + hops, ctx_count)},
            device_id_type=MESH,
        )

    def doc_copy(shift):
        return pltpu.make_async_remote_copy(
            src_ref=doc_ref,
            dst_ref=doc_in.at[shift - 1],
            send_sem=doc_send.at[shift - 1],
            recv_sem=doc_recv.at[shift - 1],
            device_id={"ctx": lax.rem(me + shift, ctx_count)},
            device_id_type=MESH,
        )

    def next_copy(source, target, index):
        return pltpu.make_async_remote_copy(
            src_ref=source,
            dst_ref=target,
            send_sem=next_send.at[index],
            recv_sem=next_recv.at[index],
            device_id={"ctx": lax.rem(me + ctx_count - 1, ctx_count)},
            device_id_type=MESH,
        )

    def next_doc():
        return next_copy(doc_ref, doc_next, 2 * groups)

    def next_kv(group):
        return next_copy(kv_out.at[group], kv_next.at[group], 2 * group)

    def next_query(group):
        these = pl.ds(group * ratio, ratio)
        return next_copy(q_ref.at[these], q_next.at[these], 2 * group + 1)

    for shift in range(1, back + 1):

        @pl.when(me + shift < ctx_count)
        def _(shift=shift):
            doc_copy(shift).start()

    @pl.when(me < ctx_count - 1)
    def _():
        for group in range(groups):
            kv_copy(group, 1).start()
            if back > 1 and group < groups - 1:

                @pl.when(me == 0)
                def _(group=group):
                    kv_copy(group, 2, 2).start()

    loads["query"].wait()

    @pl.when(me > 0)
    def _():
        next_doc().start()
        for group in range(groups):
            next_kv(group).start()
            next_query(group).start()

    for shift in range(1, back + 1):

        @pl.when(me < shift)
        def _(shift=shift):
            doc_in[shift - 1] = jnp.full(doc_in.shape[1:], -1, jnp.int32)
            for group in range(groups):
                kv_in[group, shift - 1] = jnp.zeros(kv_in.shape[2:], kv_in.dtype)

    def kv_arrive(group, shift):
        @pl.when(me >= shift)
        def _():
            kv_copy(group, shift).wait_recv()
            if shift < back:

                relayed = (me > 1) | (shift > 1) | (group == groups - 1)

                @pl.when((me < ctx_count - 1) & relayed)
                def _():
                    kv_copy(group, shift + 1).start()

    loads["ids"].wait()
    loads["keep"].wait()
    row = lax.broadcasted_iota(jnp.int32, (half, half), 0)
    lane = lax.broadcasted_iota(jnp.int32, (half, half), 1)
    ids_row = ids_ref[...]
    ids_column = jnp.sum(jnp.where(row == lane, ids_row, 0), axis=1, keepdims=True)
    ranking = jnp.sum(
        jnp.where((ids_column == ids_row) & (row < lane), 1, 0), axis=0, keepdims=True
    )
    experts = keep_ref.shape[1]
    square_row = lax.broadcasted_iota(jnp.int32, (experts, experts), 0)
    square_lane = lax.broadcasted_iota(jnp.int32, (experts, experts), 1)
    keep_column = jnp.sum(
        jnp.where(square_row == square_lane, keep_ref[...], 0), axis=1, keepdims=True
    )
    expert_row = lax.broadcasted_iota(jnp.int32, (experts, half), 0)
    limits = jnp.sum(jnp.where(expert_row == ids_row, keep_column, 0), axis=0, keepdims=True)
    target = jnp.where(ranking < limits, ids_row * CAP + ranking, -1)
    slot_row = lax.broadcasted_iota(jnp.int32, (slots, half), 0)

    for shift in range(1, back + 1):

        @pl.when(me >= shift)
        def _(shift=shift):
            doc_copy(shift).wait_recv()

    square = lax.broadcasted_iota(jnp.int32, (tokens, tokens), 0)
    across = lax.broadcasted_iota(jnp.int32, (tokens, tokens), 1)
    scale = 1.0 / math.sqrt(size)

    def visible(doc_row, earlier):
        doc_column = jnp.sum(jnp.where(square == across, doc_row, 0), axis=1, keepdims=True)
        masks = [(across <= square) & (doc_row == doc_column)]
        masks += [other == doc_column for other in earlier]
        return jnp.concatenate([jnp.where(mask, 1.0, 0.0) for mask in masks], axis=1) > 0.5

    def attend(block, group, allowed, query, pairs):
        keys = jnp.concatenate([pair[0] for pair in pairs], axis=0)
        vals = jnp.concatenate([pair[1] for pair in pairs], axis=0)
        count = keys.shape[0]
        stacked = query[group * ratio : (group + 1) * ratio].reshape(ratio * tokens, size)
        scores = lax.dot_general(
            stacked, keys, (((1,), (1,)), ((), ())), preferred_element_type=jnp.float32
        ).reshape(ratio, tokens, count)
        masked = jnp.where(allowed[None], scores * scale, -1e30)
        highest = jnp.max(masked, axis=2, keepdims=True)
        weights = jnp.exp(masked - highest)
        totals = jnp.sum(weights, axis=2, keepdims=True)
        mixed = jnp.dot(
            weights.astype(jnp.bfloat16).reshape(ratio * tokens, count),
            vals,
            preferred_element_type=jnp.float32,
        ).reshape(ratio, tokens, size)
        mixed = (mixed / totals).astype(jnp.bfloat16)
        for head in range(ratio):
            attn[block, group, :, head * size : (head + 1) * size] = mixed[head]

    def attn_copy(block, group, rightward):
        to = me + 1 if rightward else me - 1
        sends = right_send if rightward else left_send
        return pltpu.make_async_remote_copy(
            src_ref=attn.at[block, group],
            dst_ref=attn.at[block, group],
            send_sem=sends.at[0],
            recv_sem=attn_recv.at[block, group],
            device_id={"ctx": lax.rem(to + ctx_count, ctx_count)},
            device_id_type=MESH,
        )

    allowed = visible(doc_ref[...], [doc_in[shift] for shift in range(back)])

    def attend_own(group):
        if back:
            kv_arrive(group, back)
        attend(
            me,
            group,
            allowed,
            q_ref,
            [kv_out.at[group]] + [kv_in.at[group, shift] for shift in range(back)],
        )
        soon = group < groups - 1

        @pl.when((me < ctx_count - 1) & (soon | (me == 0) | (rest == 1)))
        def _():
            attn_copy(me, group, True).start()

    def kv_last():
        for shift in range(1, back):
            kv_arrive(groups - 1, shift)

    for group in range(groups - 1):
        for shift in range(1, back):
            kv_arrive(group, shift)
        if group == 0:

            @pl.when(me >= back)
            def _():
                kv_last()

        attend_own(group)

    @pl.when(me == 0)
    def _():
        attend_own(groups - 1)

    def item(turn, count):
        order = turn - 1
        spot = jnp.where(count > 0, lax.rem(order, jnp.maximum(count, 1)), 0)
        group = sum((order >= count * number).astype(jnp.int32) for number in range(1, groups))
        group = group if groups > 1 else jnp.int32(0)
        final = group == groups - 1
        active = (turn >= 1) & (turn <= groups * count)
        return group, jnp.where(final, count - spot, spot + 1), final, active

    beyond = jnp.maximum(rest - 1, 0)
    skipped = jnp.where(early, 1, 0)
    upstream = me - skipped

    def from_left(turn):
        group, far, final, active = item(turn, upstream)
        block = upstream - far

        @pl.when(active)
        def _():
            attn_copy(block, group, True).wait_recv()

            @pl.when(me < ctx_count - 1)
            def _():
                attn_copy(block, group, True).start()

                @pl.when((turn == groups * me) & (rest > 1))
                def _():
                    attn_copy(me, groups - 1, True).start()

        return block, active & final

    def from_right(turn):
        group = lax.rem(turn - 1, groups)
        block = me + 2 + (turn - 1) // groups
        final, active = group == groups - 1, turn <= groups * beyond

        @pl.when(active)
        def _():
            attn_copy(block, group, False).wait_recv()

            @pl.when(me > 0)
            def _():
                attn_copy(block, group, False).start()

        return block, active & final

    def attend_next(group):
        @pl.when(rest > 0)
        def _():
            next_kv(group).wait_recv()
            next_query(group).wait_recv()
            attend(
                me + 1,
                group,
                visible(
                    doc_next[...],
                    ([doc_ref[...]] if back else []) + [doc_in[shift] for shift in range(back - 1)],
                ),
                q_next,
                [kv_next.at[group]]
                + ([kv_out.at[group]] if back else [])
                + [kv_in.at[group, shift] for shift in range(back - 1)],
            )

            @pl.when(me > 0)
            def _():
                attn_copy(me + 1, group, False).start()

    @pl.when(rest > 0)
    def _():
        next_doc().wait_recv()

    for group in range(groups - 1):
        attend_next(group)

    @pl.when((me < back) | (groups == 1))
    def _():
        kv_last()

    from_left(1)
    attend_next(groups - 1)

    @pl.when(me > 0)
    def _():
        attend_own(groups - 1)

    def part_copy(block, piece):
        return pltpu.make_async_remote_copy(
            src_ref=part_out.at[block, piece],
            dst_ref=part_in.at[block, piece],
            send_sem=part_send.at[0],
            recv_sem=part_recv.at[block],
            device_id={"tp": 1 - core},
            device_id_type=MESH,
        )

    def res_copy(block, peer, piece):
        return pltpu.make_async_remote_copy(
            src_ref=res_out.at[block, piece],
            dst_ref=res_in.at[me, piece],
            send_sem=res_send.at[0],
            recv_sem=res_recv.at[peer, piece],
            device_id={"ctx": block},
            device_id_type=MESH,
        )

    routes = ((1, ctx_count - 3), (-1, 2)) if ctx_count > 3 else ()

    def pass_copy(side):
        sign, source = routes[side]
        return pltpu.make_async_remote_copy(
            src_ref=res_out.at[source + 2 * sign],
            dst_ref=passing.at[side],
            send_sem=res_send.at[0],
            recv_sem=pass_recv.at[side],
            device_id={"ctx": source + sign},
            device_id_type=MESH,
        )

    def onward_copy(side, piece):
        sign, source = routes[side]
        return pltpu.make_async_remote_copy(
            src_ref=passing.at[side, piece],
            dst_ref=res_in.at[source, piece],
            send_sem=pass_send.at[side],
            recv_sem=res_recv.at[source, piece],
            device_id={"ctx": source + 2 * sign},
            device_id_type=MESH,
        )

    def pass_on():
        for side, (sign, source) in enumerate(routes):

            @pl.when(me == source + sign)
            def _(side=side):
                pass_copy(side).wait_recv()
                for piece in range(pieces):
                    onward_copy(side, piece).start()

    def slot_at(peer, block, piece):
        if aligned:
            first = pl.multiple_of(block * columns + piece * part, 128)
            return slot_in.at[peer, :, pl.ds(first, part)]
        return slot_in.at[peer, block, piece]

    def slot_copy(shift, block, index, piece):
        return pltpu.make_async_remote_copy(
            src_ref=slot_out.at[shift - 1, block, piece],
            dst_ref=slot_at(mine, block, piece),
            send_sem=slot_send.at[shift - 1],
            recv_sem=slot_recv.at[index, block, piece],
            device_id={"exp": lax.rem(mine + shift, exp_count)},
            device_id_type=MESH,
        )

    def project(block):
        for start in range(0, pieces, WIDE):
            some = range(start, min(start + WIDE, pieces))
            there = slice(start * part, (some[-1] + 1) * part)
            total = None
            for group in range(groups):
                term = jnp.dot(
                    attn[block, group],
                    weight[group * depth : (group + 1) * depth, there],
                    preferred_element_type=jnp.float32,
                )
                total = term if total is None else total + term
            for piece in some:
                here = slice((piece - start) * part, (piece - start + 1) * part)
                product[block, piece, 0] = total[:half, here]
                product[block, piece, 1] = total[half:, here]
                part_out[block, piece] = product[block, piece, 1 - core].astype(jnp.bfloat16)
                part_copy(block, piece).start()

    def parts_arrive(block):
        pltpu.make_async_remote_copy(
            src_ref=part_out.at[block],
            dst_ref=part_in.at[block],
            send_sem=part_send.at[0],
            recv_sem=part_recv.at[block],
            device_id={"tp": 1 - core},
            device_id_type=MESH,
        ).wait_recv()

    def finish(block, piece):
        return (
            product[block, piece, core] + part_in[block, piece].astype(jnp.float32)
        ).astype(jnp.bfloat16)

    def send(block):
        for piece in range(pieces):
            res_copy(block, me, piece).start()

    def place(block, piece):
        hidden = (
            residual[block, :, piece * part : (piece + 1) * part].astype(jnp.float32)
            + res_in[block, piece].astype(jnp.float32)
        ).astype(jnp.bfloat16)
        for shift in (*range(1, exp_count), 0):
            peer = lax.rem(mine + shift, exp_count)
            table = (slot_row + peer * slots == target).astype(jnp.bfloat16)
            chosen = jnp.dot(table, hidden, preferred_element_type=jnp.float32).astype(
                jnp.bfloat16
            )
            if shift == 0:
                slot_at(mine, block, piece)[...] = chosen
            else:
                slot_out[shift - 1, block, piece] = chosen
                slot_copy(shift, block, exp_count - shift - 1, piece).start()

    def absorb(shift, block, piece):
        peer = lax.rem(mine + shift, exp_count)
        if shift:
            slot_copy(1, block, shift - 1, piece).wait_recv()
        hidden = slot_at(peer, block, piece)[...]
        if aligned:
            first = pl.multiple_of(block * columns + piece * part, 128)
            columns_here = routed[:, pl.ds(first, part)]
        else:
            columns_here = routed[block, piece]
        logits[shift] += lax.dot_general(
            hidden,
            columns_here,
            (((1,), (1,)), ((), ())),
            preferred_element_type=jnp.float32,
        )
        wide = hidden.astype(jnp.float32)
        wide = wide * wide
        if aligned:
            total = wide[:, :128]
            for first in range(128, part, 128):
                total = total + wide[:, first : first + 128]
            tally[shift] += total
        else:
            tally[shift, :, :1] += jnp.sum(wide, axis=1, keepdims=True)

    loads["weight"].wait()
    project(me)

    @pl.when(rest > 0)
    def _():
        project(me + 1)

    loads["gain"].wait()
    loads["router"].wait()
    wide = gain_ref[...].astype(jnp.float32)
    for line in range(wide.shape[0]):
        there = slice(line * 128, (line + 1) * 128)
        gain_row[:, there] = wide[line : line + 1]
        router_ref[:, there] = (
            router_ref[:, there].astype(jnp.float32) * wide[line : line + 1]
        ).astype(jnp.bfloat16)
    if not aligned:
        for block in range(ctx_count):
            for piece in range(pieces):
                first = block * columns + piece * part
                routed[block, piece] = router_ref[:, first : first + part]
    else:
        routed = router_ref
    tally[...] = jnp.zeros_like(tally)
    logits[...] = jnp.zeros_like(logits)
    pltpu.make_async_copy(residual, residual, load_sem.at[len(loads)]).wait()

    def reply(block, now):
        parts_arrive(block)
        for piece in range(pieces):
            res_out[block, piece] = finish(block, piece)
            if now is not None:

                @pl.when(now)
                def _(piece=piece):
                    res_copy(block, me, piece).start()

        for side, (sign, source) in enumerate(routes):

            @pl.when((me == source) & (block == source + 2 * sign))
            def _(side=side):
                pass_copy(side).start()

    def send(block):
        for piece in range(pieces):
            res_copy(block, me, piece).start()

    def order(number):
        inner = jnp.where(number <= rest, me + number, number - rest - 1)
        inner = jnp.where(number == 0, me - 1, inner)
        return jnp.where(me == 0, jnp.where(number == 0, 1, ctx_count - number), inner)

    def send_far():
        def body(number, carry):
            send(ctx_count - 1 - number)
            return carry

        lax.fori_loop(0, beyond, body, 0)

    def settle(number, before):
        block = order(number)
        for piece in range(pieces):
            res_copy(me, block, piece).wait_recv()
            if piece == 0:

                @pl.when((me == 0) & (number == 1))
                def _():
                    send_far()

            place(block, piece)
            absorb(0, block, piece)
            for shift in range(1, exp_count):
                absorb(shift, before, piece)

        direct = me > (2 if routes else 1)

        @pl.when((number == 0) & direct & (rest > 0))
        def _():
            send(0)

        @pl.when((number == 1) & (me > 0) & (rest > (2 if routes else 1)))
        def _():
            send_far()

        @pl.when(number == 0)
        def _():
            pass_on()

        return block

    last = jnp.maximum(groups * upstream - 1, groups * beyond)

    late = (rest == 1) & (me > 1)

    def own():
        parts_arrive(me)
        for piece in range(pieces):
            res_in[me, piece] = finish(me, piece)
            place(me, piece)
            absorb(0, me, piece)

        @pl.when(rest > 0)
        def _():
            reply(me + 1, None)

        @pl.when((rest > 0) & jnp.logical_not(late))
        def _():
            send(me + 1)

    @pl.when(early)
    def _():
        for group in range(groups):
            attn_copy(me - 1, group, True).wait_recv()
        project(me - 1)

    @pl.when((me == 0) | (rest == 0))
    def _():
        own()

    @pl.when(early)
    def _():
        reply(me - 1, None)
        send(me - 1)

    def step(turn, carry):
        left, left_whole = from_left(turn + 1)
        right, right_whole = from_right(turn)

        @pl.when((turn == 1) & (me > 0) & (rest > 0))
        def _():
            own()

        whole = ((left, left_whole), (right, right_whole))
        for block, has in whole:

            @pl.when(has)
            def _(block=block):
                project(block)

        prompt = (left < me - 1) & (early | (left > 0))
        for (block, has), now in zip(whole, (prompt, None)):

            @pl.when(has)
            def _(block=block, now=now):
                reply(block, now)

        @pl.when(late & (turn == groups * me - 2))
        def _():
            send(me + 1)

        @pl.when(early & (turn == (groups - 1) * upstream))
        def _():
            settle(0, me)

        return carry

    lax.fori_loop(1, jnp.maximum(last, 1) + 1, step, 0)

    @pl.when((me > 0) & (rest > 0) | (me == 1))
    def _():
        send(me - 1)

    block = lax.fori_loop(
        jnp.where(early, 1, 0), ctx_count - 1, settle, jnp.where(early, me - 1, me)
    )
    for piece in range(pieces):
        for shift in range(1, exp_count):
            absorb(shift, block, piece)

    spread = lax.broadcasted_iota(jnp.int32, logits.shape[1:], 0) // CAP
    expert = lax.broadcasted_iota(jnp.int32, logits.shape[1:], 1)
    slot_across = lax.broadcasted_iota(jnp.int32, (slots, slots), 0) == (
        lax.broadcasted_iota(jnp.int32, (slots, slots), 1)
    )
    for shift in range(exp_count):
        peer = lax.rem(mine + shift, exp_count)
        power = tally[shift] if aligned else tally[shift, :, :1]
        power = jnp.sum(power, axis=1, keepdims=True) / width
        factor = lax.rsqrt(power + EPSILON)
        logit = jnp.sum(jnp.where(spread == expert, logits[shift], 0.0), axis=1, keepdims=True)
        gate = jax.nn.sigmoid(logit * factor)
        column = gate * factor
        scale_ref[pl.ds(peer, 1)] = jnp.sum(
            jnp.where(slot_across, column, 0.0), axis=0, keepdims=True
        )

    @pl.when(me < ctx_count - 1)
    def _():
        for group in range(groups):
            kv_copy(group, 1).wait_send()
            if back > 1 and group < groups - 1:

                @pl.when(me == 0)
                def _(group=group):
                    kv_copy(group, 2, 2).wait_send()

            for shift in range(1, back):
                relayed = (me > 1) | (shift > 1) | (group == groups - 1)

                @pl.when((me >= shift) & relayed)
                def _(group=group, shift=shift):
                    kv_copy(group, shift + 1).wait_send()

    for shift in range(1, back + 1):

        @pl.when(me + shift < ctx_count)
        def _(shift=shift):
            doc_copy(shift).wait_send()

    @pl.when(me > 0)
    def _():
        next_doc().wait_send()
        for group in range(groups):
            next_kv(group).wait_send()
            next_query(group).wait_send()

    def sent(source, semaphore):
        pltpu.make_async_remote_copy(
            src_ref=source,
            dst_ref=source,
            send_sem=semaphore,
            recv_sem=semaphore,
            device_id={"tp": 1 - core},
            device_id_type=MESH,
        ).wait_send()

    sent(part_out, part_send.at[0])
    sent(res_out.at[pl.ds(0, ctx_count - 1)], res_send.at[0])
    for side, (sign, source) in enumerate(routes):

        @pl.when(me == source + sign)
        def _(side=side):
            sent(passing.at[side], pass_send.at[side])

    for shift in range(1, exp_count):
        sent(slot_out.at[shift - 1], slot_send.at[shift - 1])

    for count in range(1, ctx_count):

        @pl.when((me + 1 == count) & (rest > 0))
        def _(count=count):
            sent(attn.at[pl.ds(0, count)], right_send.at[0])

        @pl.when((rest == count) & (me > 0))
        def _(count=count):
            sent(attn.at[pl.ds(0, count)], left_send.at[0])


def on_device(
    queries,
    key_states,
    values,
    doc_ids,
    residual,
    out_proj,
    norm_gain,
    router,
    expert_ids,
    keep_counts,
):
    tokens, heads, size = queries.shape[1:]
    groups = key_states.shape[2]
    ctx_count = lax.axis_size("ctx")
    exp_count = lax.axis_size("exp")
    features, columns = out_proj.shape
    half = residual.shape[1]
    width = residual.shape[2]
    experts = keep_counts.shape[0]
    owned = experts // exp_count
    slots = owned * CAP
    longest = tokens * ctx_count // 2
    back = min(ctx_count - 1, -(-(longest - 1) // tokens))
    pieces = columns // 256 if columns % 256 == 0 else 2
    part = columns // pieces
    aligned = part % 128 == 0
    vmem = pl.BlockSpec(memory_space=pltpu.VMEM)
    hbm = pl.BlockSpec(memory_space=pltpu.HBM)
    bf16, f32, i32 = jnp.bfloat16, jnp.float32, jnp.int32
    dma = pltpu.SemaphoreType.DMA
    n = ctx_count
    stream = residual[0]
    if columns % 128:
        stream = stream.reshape(half, ctx_count, columns).transpose(1, 0, 2)
    slot_shape = (exp_count, slots, width) if aligned else (exp_count, n, pieces, slots, part)
    chosen, scale, gain = pl.pallas_call(
        functools.partial(kernel, (ctx_count, exp_count, back, pieces)),
        out_shape=(
            jax.ShapeDtypeStruct(slot_shape, bf16),
            jax.ShapeDtypeStruct((exp_count, slots), f32),
            jax.ShapeDtypeStruct((1, width), f32),
        ),
        in_specs=[hbm] * 10,
        out_specs=(vmem, vmem, vmem),
        scratch_shapes=[
            pltpu.VMEM((heads, tokens, size), bf16),
            pltpu.VMEM((tokens, groups, size), bf16),
            pltpu.VMEM((tokens, groups, size), bf16),
            pltpu.VMEM((1, tokens), i32),
            pltpu.VMEM((width // 128, 128), bf16),
            pltpu.VMEM((owned, width), bf16),
            pltpu.VMEM((1, half), i32),
            pltpu.VMEM((1, experts), i32),
            pltpu.VMEM((groups, 2, tokens, size), bf16),
            pltpu.VMEM((groups, back, 2, tokens, size), bf16),
            pltpu.VMEM((groups, 2, tokens, size), bf16),
            pltpu.VMEM((heads, tokens, size), bf16),
            pltpu.VMEM((1, tokens), i32),
            pltpu.VMEM((8, 128) if aligned else (n, pieces, owned, part), bf16),
            pltpu.VMEM((exp_count, slots, 128), f32),
            pltpu.VMEM((exp_count, slots, owned), f32),
            pltpu.VMEM((back, 1, tokens), i32),
            pltpu.VMEM((n, groups, tokens, features // groups), bf16),
            pltpu.VMEM((features, columns), bf16),
            pltpu.VMEM((n, half, columns), bf16),
            pltpu.VMEM((n, pieces, 2, half, part), f32),
            pltpu.VMEM((n, pieces, half, part), bf16),
            pltpu.VMEM((n, pieces, half, part), bf16),
            pltpu.VMEM((n, pieces, half, part), bf16),
            pltpu.VMEM((n, pieces, half, part), bf16),
            pltpu.VMEM((2, pieces, half, part), bf16),
            pltpu.VMEM((exp_count - 1, n, pieces, slots, part), bf16),
            dma((10,)),
            dma((groups, back)),
            dma((groups, back)),
            dma((back,)),
            dma((back,)),
            dma((2 * groups + 1,)),
            dma((2 * groups + 1,)),
            dma((1,)),
            dma((1,)),
            dma((n, groups)),
            dma((1,)),
            dma((n,)),
            dma((1,)),
            dma((n, pieces)),
            dma((2,)),
            dma((2,)),
            dma((exp_count - 1,)),
            dma((exp_count - 1, n, pieces)),
        ],
        compiler_params=pltpu.CompilerParams(
            collective_id=0, has_side_effects=True, vmem_limit_bytes=40 << 20
        ),
    )(
        *(
            pltpu.with_memory_space_constraint(operand, pltpu.HBM)
            for operand in (
                queries[0].transpose(1, 0, 2),
                key_states[0],
                values[0],
                doc_ids,
                stream,
                out_proj,
                norm_gain.reshape(width // 128, 128),
                router.T,
                expert_ids.reshape(1, half),
                keep_counts.reshape(1, experts),
            )
        )
    )
    if not aligned:
        chosen = chosen.transpose(0, 3, 1, 2, 4).reshape(exp_count, slots, width)
    scaled = chosen.astype(f32) * scale[:, :, None] * gain
    return scaled.astype(bf16).reshape(exp_count, owned, CAP, width)


def solution(mesh):
    placed = (
        P(("groups", "exp"), "ctx", "tp", None),
        P(("groups", "exp"), "ctx", "tp", None),
        P(("groups", "exp"), "ctx", "tp", None),
        P(("groups", "exp"), "ctx"),
        P(("groups", "exp"), ("ctx", "tp"), None),
        P("tp", "ctx"),
        P(),
        P(None, "exp"),
        P(("groups", "exp"), ("ctx", "tp"), None),
        P("groups"),
    )
    return jax.shard_map(
        on_device,
        mesh=mesh,
        in_specs=placed,
        out_specs=P(("groups", "ctx", "tp"), "exp", None, None),
        check_vma=False,
    )
```

```python
import functools
import math

import jax
import jax.numpy as jnp
from jax import lax
from jax.experimental import pallas as pl
from jax.experimental.pallas import tpu as pltpu
from jax.sharding import PartitionSpec as P

CAP = 2
EPSILON = 1e-05
WIDE = 5
MESH = pl.DeviceIdType.MESH


def kernel(
    sizes,
    q_hbm,
    key_hbm,
    value_hbm,
    doc_hbm,
    residual_hbm,
    weight_hbm,
    gain_hbm,
    router_hbm,
    ids_hbm,
    keep_hbm,
    slot_in,
    scale_ref,
    gain_row,
    q_ref,
    key_ref,
    value_ref,
    doc_ref,
    gain_ref,
    router_ref,
    ids_ref,
    keep_ref,
    kv_out,
    kv_in,
    kv_next,
    q_next,
    doc_next,
    routed,
    tally,
    logits,
    doc_in,
    attn,
    weight,
    residual,
    product,
    part_out,
    part_in,
    res_out,
    res_in,
    passing,
    tables,
    slot_out,
    load_sem,
    kv_send,
    kv_recv,
    doc_send,
    doc_recv,
    next_send,
    next_recv,
    right_send,
    left_send,
    attn_recv,
    part_send,
    part_recv,
    res_send,
    res_recv,
    pass_send,
    pass_recv,
    slot_send,
    slot_recv,
):
    ctx_count, exp_count, back, pieces = sizes
    heads, tokens, size = q_ref.shape
    groups = kv_out.shape[0]
    ratio = heads // groups
    half = tokens // 2
    columns = weight.shape[1]
    depth = weight.shape[0] // groups
    slots = slot_out.shape[3]
    part = columns // pieces
    width = columns * ctx_count
    aligned = part % 128 == 0
    me = lax.axis_index("ctx")
    mine = lax.axis_index("exp")
    core = lax.axis_index("tp")
    rest = ctx_count - 1 - me
    early = (rest == 0) & (me > 1)

    barrier = pltpu.get_barrier_semaphore()
    for shift in range(1, ctx_count):
        pl.semaphore_signal(
            barrier,
            inc=1,
            device_id={"ctx": lax.rem(me + shift, ctx_count)},
            device_id_type=MESH,
        )
    for shift in range(1, exp_count):
        pl.semaphore_signal(
            barrier,
            inc=1,
            device_id={"exp": lax.rem(mine + shift, exp_count)},
            device_id_type=MESH,
        )
    pl.semaphore_signal(barrier, inc=1, device_id={"tp": 1 - core}, device_id_type=MESH)

    loads = {}

    def load(name, source, target):
        loads[name] = pltpu.make_async_copy(source, target, load_sem.at[len(loads)])
        loads[name].start()

    load("key", key_hbm, key_ref)
    load("value", value_hbm, value_ref)
    load("doc", doc_hbm, doc_ref)
    load("query", q_hbm, q_ref)
    load("ids", ids_hbm, ids_ref)
    load("keep", keep_hbm, keep_ref)
    load("gain", gain_hbm, gain_ref)
    load("router", router_hbm, router_ref)
    load("weight", weight_hbm, weight)
    for block in range(ctx_count):
        there = slice(block * columns, (block + 1) * columns)
        pltpu.make_async_copy(
            residual_hbm.at[:, there] if columns % 128 == 0 else residual_hbm.at[block],
            residual.at[block],
            load_sem.at[len(loads)],
        ).start()

    loads["key"].wait()
    loads["value"].wait()
    for group in range(groups):
        kv_out[group, 0] = key_ref[:, group, :]
        kv_out[group, 1] = value_ref[:, group, :]
    loads["doc"].wait()

    pl.semaphore_wait(barrier, ctx_count + exp_count - 1)

    def kv_copy(group, shift, hops=1):
        return pltpu.make_async_remote_copy(
            src_ref=kv_out.at[group] if shift == hops else kv_in.at[group, shift - 2],
            dst_ref=kv_in.at[group, shift - 1],
            send_sem=kv_send.at[group, shift - 1],
            recv_sem=kv_recv.at[group, shift - 1],
            device_id={"ctx": lax.rem(me + hops, ctx_count)},
            device_id_type=MESH,
        )

    def doc_copy(shift):
        return pltpu.make_async_remote_copy(
            src_ref=doc_ref,
            dst_ref=doc_in.at[shift - 1],
            send_sem=doc_send.at[shift - 1],
            recv_sem=doc_recv.at[shift - 1],
            device_id={"ctx": lax.rem(me + shift, ctx_count)},
            device_id_type=MESH,
        )

    def next_copy(source, target, index):
        return pltpu.make_async_remote_copy(
            src_ref=source,
            dst_ref=target,
            send_sem=next_send.at[index],
            recv_sem=next_recv.at[index],
            device_id={"ctx": lax.rem(me + ctx_count - 1, ctx_count)},
            device_id_type=MESH,
        )

    def next_doc():
        return next_copy(doc_ref, doc_next, 2 * groups)

    def next_kv(group):
        return next_copy(kv_out.at[group], kv_next.at[group], 2 * group)

    def next_query(group):
        these = pl.ds(group * ratio, ratio)
        return next_copy(q_ref.at[these], q_next.at[these], 2 * group + 1)

    for shift in range(1, back + 1):

        @pl.when(me + shift < ctx_count)
        def _(shift=shift):
            doc_copy(shift).start()

    @pl.when(me < ctx_count - 1)
    def _():
        for group in range(groups):
            kv_copy(group, 1).start()
            if back > 1 and group < groups - 1:

                @pl.when(me == 0)
                def _(group=group):
                    kv_copy(group, 2, 2).start()

    loads["query"].wait()

    @pl.when(me > 0)
    def _():
        next_doc().start()
        for group in range(groups):
            next_kv(group).start()
            next_query(group).start()

    for shift in range(1, back + 1):

        @pl.when(me < shift)
        def _(shift=shift):
            doc_in[shift - 1] = jnp.full(doc_in.shape[1:], -1, jnp.int32)
            for group in range(groups):
                kv_in[group, shift - 1] = jnp.zeros(kv_in.shape[2:], kv_in.dtype)

    def kv_arrive(group, shift):
        @pl.when(me >= shift)
        def _():
            kv_copy(group, shift).wait_recv()
            if shift < back:

                relayed = (me > 1) | (shift > 1) | (group == groups - 1)

                @pl.when((me < ctx_count - 1) & relayed)
                def _():
                    kv_copy(group, shift + 1).start()

    loads["ids"].wait()
    loads["keep"].wait()
    row = lax.broadcasted_iota(jnp.int32, (half, half), 0)
    lane = lax.broadcasted_iota(jnp.int32, (half, half), 1)
    ids_row = ids_ref[...]
    ids_column = jnp.sum(jnp.where(row == lane, ids_row, 0), axis=1, keepdims=True)
    ranking = jnp.sum(
        jnp.where((ids_column == ids_row) & (row < lane), 1, 0), axis=0, keepdims=True
    )
    experts = keep_ref.shape[1]
    square_row = lax.broadcasted_iota(jnp.int32, (experts, experts), 0)
    square_lane = lax.broadcasted_iota(jnp.int32, (experts, experts), 1)
    keep_column = jnp.sum(
        jnp.where(square_row == square_lane, keep_ref[...], 0), axis=1, keepdims=True
    )
    expert_row = lax.broadcasted_iota(jnp.int32, (experts, half), 0)
    limits = jnp.sum(jnp.where(expert_row == ids_row, keep_column, 0), axis=0, keepdims=True)
    target = jnp.where(ranking < limits, ids_row * CAP + ranking, -1)
    slot_row = lax.broadcasted_iota(jnp.int32, (slots, half), 0)
    for shift in range(exp_count):
        peer = lax.rem(mine + shift, exp_count)
        tables[shift * slots : (shift + 1) * slots] = jnp.where(
            slot_row + peer * slots == target, 1.0, 0.0
        ).astype(jnp.bfloat16)

    for shift in range(1, back + 1):

        @pl.when(me >= shift)
        def _(shift=shift):
            doc_copy(shift).wait_recv()

    square = lax.broadcasted_iota(jnp.int32, (tokens, tokens), 0)
    across = lax.broadcasted_iota(jnp.int32, (tokens, tokens), 1)
    scale = 1.0 / math.sqrt(size)

    def visible(doc_row, earlier):
        doc_column = jnp.sum(jnp.where(square == across, doc_row, 0), axis=1, keepdims=True)
        masks = [(across <= square) & (doc_row == doc_column)]
        masks += [other == doc_column for other in earlier]
        return jnp.concatenate([jnp.where(mask, 1.0, 0.0) for mask in masks], axis=1) > 0.5

    def attend(block, group, allowed, query, pairs):
        keys = jnp.concatenate([pair[0] for pair in pairs], axis=0)
        vals = jnp.concatenate([pair[1] for pair in pairs], axis=0)
        count = keys.shape[0]
        stacked = query[group * ratio : (group + 1) * ratio].reshape(ratio * tokens, size)
        scores = lax.dot_general(
            stacked, keys, (((1,), (1,)), ((), ())), preferred_element_type=jnp.float32
        ).reshape(ratio, tokens, count)
        masked = jnp.where(allowed[None], scores * scale, -1e30)
        highest = jnp.max(masked, axis=2, keepdims=True)
        weights = jnp.exp(masked - highest)
        totals = jnp.sum(weights, axis=2, keepdims=True)
        mixed = jnp.dot(
            weights.astype(jnp.bfloat16).reshape(ratio * tokens, count),
            vals,
            preferred_element_type=jnp.float32,
        ).reshape(ratio, tokens, size)
        mixed = (mixed / totals).astype(jnp.bfloat16)
        for head in range(ratio):
            attn[block, group, :, head * size : (head + 1) * size] = mixed[head]

    def attn_copy(block, group, rightward):
        to = me + 1 if rightward else me - 1
        sends = right_send if rightward else left_send
        return pltpu.make_async_remote_copy(
            src_ref=attn.at[block, group],
            dst_ref=attn.at[block, group],
            send_sem=sends.at[0],
            recv_sem=attn_recv.at[block, group],
            device_id={"ctx": lax.rem(to + ctx_count, ctx_count)},
            device_id_type=MESH,
        )

    allowed = visible(doc_ref[...], [doc_in[shift] for shift in range(back)])

    def attend_own(group):
        if back:
            kv_arrive(group, back)
        attend(
            me,
            group,
            allowed,
            q_ref,
            [kv_out.at[group]] + [kv_in.at[group, shift] for shift in range(back)],
        )
        soon = group < groups - 1

        @pl.when((me < ctx_count - 1) & (soon | (me == 0) | (rest == 1)))
        def _():
            attn_copy(me, group, True).start()

    def kv_last():
        for shift in range(1, back):
            kv_arrive(groups - 1, shift)

    for group in range(groups - 1):
        for shift in range(1, back):
            kv_arrive(group, shift)
        if group == 0:

            @pl.when(me >= back)
            def _():
                kv_last()

        attend_own(group)

    @pl.when(me == 0)
    def _():
        attend_own(groups - 1)

    def item(turn, count):
        order = turn - 1
        spot = jnp.where(count > 0, lax.rem(order, jnp.maximum(count, 1)), 0)
        group = sum((order >= count * number).astype(jnp.int32) for number in range(1, groups))
        group = group if groups > 1 else jnp.int32(0)
        final = group == groups - 1
        active = (turn >= 1) & (turn <= groups * count)
        return group, jnp.where(final, count - spot, spot + 1), final, active

    beyond = jnp.maximum(rest - 1, 0)
    skipped = jnp.where(early, 1, 0)
    upstream = me - skipped

    def from_left(turn):
        group, far, final, active = item(turn, upstream)
        block = upstream - far

        @pl.when(active)
        def _():
            attn_copy(block, group, True).wait_recv()

            @pl.when(me < ctx_count - 1)
            def _():
                attn_copy(block, group, True).start()

                @pl.when((turn == groups * me) & (rest > 1))
                def _():
                    attn_copy(me, groups - 1, True).start()

        return block, active & final

    def from_right(turn):
        group = lax.rem(turn - 1, groups)
        block = me + 2 + (turn - 1) // groups
        final, active = group == groups - 1, turn <= groups * beyond

        @pl.when(active)
        def _():
            attn_copy(block, group, False).wait_recv()

            @pl.when(me > 0)
            def _():
                attn_copy(block, group, False).start()

        return block, active & final

    def attend_next(group):
        @pl.when(rest > 0)
        def _():
            next_kv(group).wait_recv()
            next_query(group).wait_recv()
            attend(
                me + 1,
                group,
                visible(
                    doc_next[...],
                    ([doc_ref[...]] if back else []) + [doc_in[shift] for shift in range(back - 1)],
                ),
                q_next,
                [kv_next.at[group]]
                + ([kv_out.at[group]] if back else [])
                + [kv_in.at[group, shift] for shift in range(back - 1)],
            )

            @pl.when(me > 0)
            def _():
                attn_copy(me + 1, group, False).start()

    @pl.when(rest > 0)
    def _():
        next_doc().wait_recv()

    for group in range(groups - 1):
        attend_next(group)

    @pl.when((me < back) | (groups == 1))
    def _():
        kv_last()

    from_left(1)
    attend_next(groups - 1)

    @pl.when(me > 0)
    def _():
        attend_own(groups - 1)

    def part_copy(block, piece):
        return pltpu.make_async_remote_copy(
            src_ref=part_out.at[block, piece],
            dst_ref=part_in.at[block, piece],
            send_sem=part_send.at[0],
            recv_sem=part_recv.at[block],
            device_id={"tp": 1 - core},
            device_id_type=MESH,
        )

    def res_copy(block, peer, piece):
        return pltpu.make_async_remote_copy(
            src_ref=res_out.at[block, piece],
            dst_ref=res_in.at[me, piece],
            send_sem=res_send.at[0],
            recv_sem=res_recv.at[peer, piece],
            device_id={"ctx": block},
            device_id_type=MESH,
        )

    routes = ((1, ctx_count - 3), (-1, 2)) if ctx_count > 3 else ()

    def pass_copy(side):
        sign, source = routes[side]
        return pltpu.make_async_remote_copy(
            src_ref=res_out.at[source + 2 * sign],
            dst_ref=passing.at[side],
            send_sem=res_send.at[0],
            recv_sem=pass_recv.at[side],
            device_id={"ctx": source + sign},
            device_id_type=MESH,
        )

    def onward_copy(side, piece):
        sign, source = routes[side]
        return pltpu.make_async_remote_copy(
            src_ref=passing.at[side, piece],
            dst_ref=res_in.at[source, piece],
            send_sem=pass_send.at[side],
            recv_sem=res_recv.at[source, piece],
            device_id={"ctx": source + 2 * sign},
            device_id_type=MESH,
        )

    def pass_on():
        for side, (sign, source) in enumerate(routes):

            @pl.when(me == source + sign)
            def _(side=side):
                pass_copy(side).wait_recv()
                for piece in range(pieces):
                    onward_copy(side, piece).start()

    def slot_at(peer, block, piece):
        if aligned:
            first = pl.multiple_of(block * columns + piece * part, 128)
            return slot_in.at[peer, :, pl.ds(first, part)]
        return slot_in.at[peer, block, piece]

    def slot_copy(shift, block, index, piece):
        return pltpu.make_async_remote_copy(
            src_ref=slot_out.at[shift - 1, block, piece],
            dst_ref=slot_at(mine, block, piece),
            send_sem=slot_send.at[shift - 1],
            recv_sem=slot_recv.at[index, block, piece],
            device_id={"exp": lax.rem(mine + shift, exp_count)},
            device_id_type=MESH,
        )

    def project(block):
        for start in range(0, pieces, WIDE):
            some = range(start, min(start + WIDE, pieces))
            there = slice(start * part, (some[-1] + 1) * part)
            total = None
            for group in range(groups):
                term = jnp.dot(
                    attn[block, group],
                    weight[group * depth : (group + 1) * depth, there],
                    preferred_element_type=jnp.float32,
                )
                total = term if total is None else total + term
            for piece in some:
                here = slice((piece - start) * part, (piece - start + 1) * part)
                product[block, piece, 0] = total[:half, here]
                product[block, piece, 1] = total[half:, here]
                part_out[block, piece] = product[block, piece, 1 - core].astype(jnp.bfloat16)
                part_copy(block, piece).start()

    def parts_arrive(block):
        pltpu.make_async_remote_copy(
            src_ref=part_out.at[block],
            dst_ref=part_in.at[block],
            send_sem=part_send.at[0],
            recv_sem=part_recv.at[block],
            device_id={"tp": 1 - core},
            device_id_type=MESH,
        ).wait_recv()

    def finish(block, piece):
        return (
            product[block, piece, core] + part_in[block, piece].astype(jnp.float32)
        ).astype(jnp.bfloat16)

    def send(block):
        for piece in range(pieces):
            res_copy(block, me, piece).start()

    def place(block, piece):
        hidden = (
            residual[block, :, piece * part : (piece + 1) * part].astype(jnp.float32)
            + res_in[block, piece].astype(jnp.float32)
        ).astype(jnp.bfloat16)
        rows = jnp.dot(tables[...], hidden, preferred_element_type=jnp.float32)
        rows = rows.astype(jnp.bfloat16)
        for shift in (*range(1, exp_count), 0):
            chosen = rows[shift * slots : (shift + 1) * slots]
            if shift == 0:
                slot_at(mine, block, piece)[...] = chosen
            else:
                slot_out[shift - 1, block, piece] = chosen
                slot_copy(shift, block, exp_count - shift - 1, piece).start()

    def absorb(shift, block, piece):
        peer = lax.rem(mine + shift, exp_count)
        if shift:
            slot_copy(1, block, shift - 1, piece).wait_recv()
        hidden = slot_at(peer, block, piece)[...]
        if aligned:
            first = pl.multiple_of(block * columns + piece * part, 128)
            columns_here = routed[:, pl.ds(first, part)]
        else:
            columns_here = routed[block, piece]
        logits[shift] += lax.dot_general(
            hidden,
            columns_here,
            (((1,), (1,)), ((), ())),
            preferred_element_type=jnp.float32,
        )
        wide = hidden.astype(jnp.float32)
        wide = wide * wide
        if aligned:
            total = wide[:, :128]
            for first in range(128, part, 128):
                total = total + wide[:, first : first + 128]
            tally[shift] += total
        else:
            tally[shift, :, :1] += jnp.sum(wide, axis=1, keepdims=True)

    loads["weight"].wait()
    project(me)

    @pl.when(rest > 0)
    def _():
        project(me + 1)

    loads["gain"].wait()
    loads["router"].wait()
    wide = gain_ref[...].astype(jnp.float32)
    for line in range(wide.shape[0]):
        there = slice(line * 128, (line + 1) * 128)
        gain_row[:, there] = wide[line : line + 1]
        router_ref[:, there] = (
            router_ref[:, there].astype(jnp.float32) * wide[line : line + 1]
        ).astype(jnp.bfloat16)
    if not aligned:
        for block in range(ctx_count):
            for piece in range(pieces):
                first = block * columns + piece * part
                routed[block, piece] = router_ref[:, first : first + part]
    else:
        routed = router_ref
    tally[...] = jnp.zeros_like(tally)
    logits[...] = jnp.zeros_like(logits)
    pltpu.make_async_copy(residual, residual, load_sem.at[len(loads)]).wait()

    def reply(block, now):
        parts_arrive(block)
        for piece in range(pieces):
            res_out[block, piece] = finish(block, piece)
            if now is not None:

                @pl.when(now)
                def _(piece=piece):
                    res_copy(block, me, piece).start()

        for side, (sign, source) in enumerate(routes):

            @pl.when((me == source) & (block == source + 2 * sign))
            def _(side=side):
                pass_copy(side).start()

    def send(block):
        for piece in range(pieces):
            res_copy(block, me, piece).start()

    def order(number):
        inner = jnp.where(number <= rest, me + number, number - rest - 1)
        inner = jnp.where(number == 0, me - 1, inner)
        return jnp.where(me == 0, jnp.where(number == 0, 1, ctx_count - number), inner)

    def send_far():
        def body(number, carry):
            send(ctx_count - 1 - number)
            return carry

        lax.fori_loop(0, beyond, body, 0)

    def settle(number, before):
        block = order(number)
        for piece in range(pieces):
            res_copy(me, block, piece).wait_recv()
            if piece == 0:

                @pl.when((me == 0) & (number == 1))
                def _():
                    send_far()

            place(block, piece)
            absorb(0, block, piece)
            for shift in range(1, exp_count):
                absorb(shift, before, piece)

        direct = me > (2 if routes else 1)

        @pl.when((number == 0) & direct & (rest > 0))
        def _():
            send(0)

        @pl.when((number == 1) & (me > 0) & (rest > (2 if routes else 1)))
        def _():
            send_far()

        @pl.when(number == 0)
        def _():
            pass_on()

        return block

    last = jnp.maximum(groups * upstream - 1, groups * beyond)

    late = (rest == 1) & (me > 1)

    def own():
        parts_arrive(me)
        for piece in range(pieces):
            res_in[me, piece] = finish(me, piece)
            place(me, piece)
            absorb(0, me, piece)

        @pl.when(rest > 0)
        def _():
            reply(me + 1, None)

        @pl.when((rest > 0) & jnp.logical_not(late))
        def _():
            send(me + 1)

    @pl.when(early)
    def _():
        for group in range(groups):
            attn_copy(me - 1, group, True).wait_recv()
        project(me - 1)

    @pl.when((me == 0) | (rest == 0))
    def _():
        own()

    @pl.when(early)
    def _():
        reply(me - 1, None)
        send(me - 1)

    def step(turn, carry):
        left, left_whole = from_left(turn + 1)
        right, right_whole = from_right(turn)

        @pl.when((turn == 1) & (me > 0) & (rest > 0))
        def _():
            own()

        whole = ((left, left_whole), (right, right_whole))
        for block, has in whole:

            @pl.when(has)
            def _(block=block):
                project(block)

        prompt = (left < me - 1) & (early | (left > 0))
        for (block, has), now in zip(whole, (prompt, None)):

            @pl.when(has)
            def _(block=block, now=now):
                reply(block, now)

        @pl.when(late & (turn == groups * me - 2))
        def _():
            send(me + 1)

        @pl.when(early & (turn == (groups - 1) * upstream))
        def _():
            settle(0, me)

        return carry

    lax.fori_loop(1, jnp.maximum(last, 1) + 1, step, 0)

    @pl.when((me > 0) & (rest > 0) | (me == 1))
    def _():
        send(me - 1)

    block = lax.fori_loop(
        jnp.where(early, 1, 0), ctx_count - 1, settle, jnp.where(early, me - 1, me)
    )
    for piece in range(pieces):
        for shift in range(1, exp_count):
            absorb(shift, block, piece)

    spread = lax.broadcasted_iota(jnp.int32, logits.shape[1:], 0) // CAP
    expert = lax.broadcasted_iota(jnp.int32, logits.shape[1:], 1)
    slot_across = lax.broadcasted_iota(jnp.int32, (slots, slots), 0) == (
        lax.broadcasted_iota(jnp.int32, (slots, slots), 1)
    )
    for shift in range(exp_count):
        peer = lax.rem(mine + shift, exp_count)
        power = tally[shift] if aligned else tally[shift, :, :1]
        power = jnp.sum(power, axis=1, keepdims=True) / width
        factor = lax.rsqrt(power + EPSILON)
        logit = jnp.sum(jnp.where(spread == expert, logits[shift], 0.0), axis=1, keepdims=True)
        gate = jax.nn.sigmoid(logit * factor)
        column = gate * factor
        scale_ref[pl.ds(peer, 1)] = jnp.sum(
            jnp.where(slot_across, column, 0.0), axis=0, keepdims=True
        )

    @pl.when(me < ctx_count - 1)
    def _():
        for group in range(groups):
            kv_copy(group, 1).wait_send()
            if back > 1 and group < groups - 1:

                @pl.when(me == 0)
                def _(group=group):
                    kv_copy(group, 2, 2).wait_send()

            for shift in range(1, back):
                relayed = (me > 1) | (shift > 1) | (group == groups - 1)

                @pl.when((me >= shift) & relayed)
                def _(group=group, shift=shift):
                    kv_copy(group, shift + 1).wait_send()

    for shift in range(1, back + 1):

        @pl.when(me + shift < ctx_count)
        def _(shift=shift):
            doc_copy(shift).wait_send()

    @pl.when(me > 0)
    def _():
        next_doc().wait_send()
        for group in range(groups):
            next_kv(group).wait_send()
            next_query(group).wait_send()

    def sent(source, semaphore):
        pltpu.make_async_remote_copy(
            src_ref=source,
            dst_ref=source,
            send_sem=semaphore,
            recv_sem=semaphore,
            device_id={"tp": 1 - core},
            device_id_type=MESH,
        ).wait_send()

    sent(part_out, part_send.at[0])
    sent(res_out.at[pl.ds(0, ctx_count - 1)], res_send.at[0])
    for side, (sign, source) in enumerate(routes):

        @pl.when(me == source + sign)
        def _(side=side):
            sent(passing.at[side], pass_send.at[side])

    for shift in range(1, exp_count):
        sent(slot_out.at[shift - 1], slot_send.at[shift - 1])

    for count in range(1, ctx_count):

        @pl.when((me + 1 == count) & (rest > 0))
        def _(count=count):
            sent(attn.at[pl.ds(0, count)], right_send.at[0])

        @pl.when((rest == count) & (me > 0))
        def _(count=count):
            sent(attn.at[pl.ds(0, count)], left_send.at[0])


def on_device(
    queries,
    key_states,
    values,
    doc_ids,
    residual,
    out_proj,
    norm_gain,
    router,
    expert_ids,
    keep_counts,
):
    tokens, heads, size = queries.shape[1:]
    groups = key_states.shape[2]
    ctx_count = lax.axis_size("ctx")
    exp_count = lax.axis_size("exp")
    features, columns = out_proj.shape
    half = residual.shape[1]
    width = residual.shape[2]
    experts = keep_counts.shape[0]
    owned = experts // exp_count
    slots = owned * CAP
    longest = tokens * ctx_count // 2
    back = min(ctx_count - 1, -(-(longest - 1) // tokens))
    pieces = columns // 256 if columns % 256 == 0 else 2
    part = columns // pieces
    aligned = part % 128 == 0
    vmem = pl.BlockSpec(memory_space=pltpu.VMEM)
    hbm = pl.BlockSpec(memory_space=pltpu.HBM)
    bf16, f32, i32 = jnp.bfloat16, jnp.float32, jnp.int32
    dma = pltpu.SemaphoreType.DMA
    n = ctx_count
    stream = residual[0]
    if columns % 128:
        stream = stream.reshape(half, ctx_count, columns).transpose(1, 0, 2)
    slot_shape = (exp_count, slots, width) if aligned else (exp_count, n, pieces, slots, part)
    chosen, scale, gain = pl.pallas_call(
        functools.partial(kernel, (ctx_count, exp_count, back, pieces)),
        out_shape=(
            jax.ShapeDtypeStruct(slot_shape, bf16),
            jax.ShapeDtypeStruct((exp_count, slots), f32),
            jax.ShapeDtypeStruct((1, width), f32),
        ),
        in_specs=[hbm] * 10,
        out_specs=(vmem, vmem, vmem),
        scratch_shapes=[
            pltpu.VMEM((heads, tokens, size), bf16),
            pltpu.VMEM((tokens, groups, size), bf16),
            pltpu.VMEM((tokens, groups, size), bf16),
            pltpu.VMEM((1, tokens), i32),
            pltpu.VMEM((width // 128, 128), bf16),
            pltpu.VMEM((owned, width), bf16),
            pltpu.VMEM((1, half), i32),
            pltpu.VMEM((1, experts), i32),
            pltpu.VMEM((groups, 2, tokens, size), bf16),
            pltpu.VMEM((groups, back, 2, tokens, size), bf16),
            pltpu.VMEM((groups, 2, tokens, size), bf16),
            pltpu.VMEM((heads, tokens, size), bf16),
            pltpu.VMEM((1, tokens), i32),
            pltpu.VMEM((8, 128) if aligned else (n, pieces, owned, part), bf16),
            pltpu.VMEM((exp_count, slots, 128), f32),
            pltpu.VMEM((exp_count, slots, owned), f32),
            pltpu.VMEM((back, 1, tokens), i32),
            pltpu.VMEM((n, groups, tokens, features // groups), bf16),
            pltpu.VMEM((features, columns), bf16),
            pltpu.VMEM((n, half, columns), bf16),
            pltpu.VMEM((n, pieces, 2, half, part), f32),
            pltpu.VMEM((n, pieces, half, part), bf16),
            pltpu.VMEM((n, pieces, half, part), bf16),
            pltpu.VMEM((n, pieces, half, part), bf16),
            pltpu.VMEM((n, pieces, half, part), bf16),
            pltpu.VMEM((2, pieces, half, part), bf16),
            pltpu.VMEM((exp_count * slots, half), bf16),
            pltpu.VMEM((exp_count - 1, n, pieces, slots, part), bf16),
            dma((10,)),
            dma((groups, back)),
            dma((groups, back)),
            dma((back,)),
            dma((back,)),
            dma((2 * groups + 1,)),
            dma((2 * groups + 1,)),
            dma((1,)),
            dma((1,)),
            dma((n, groups)),
            dma((1,)),
            dma((n,)),
            dma((1,)),
            dma((n, pieces)),
            dma((2,)),
            dma((2,)),
            dma((exp_count - 1,)),
            dma((exp_count - 1, n, pieces)),
        ],
        compiler_params=pltpu.CompilerParams(
            collective_id=0, has_side_effects=True, vmem_limit_bytes=40 << 20
        ),
    )(
        *(
            pltpu.with_memory_space_constraint(operand, pltpu.HBM)
            for operand in (
                queries[0].transpose(1, 0, 2),
                key_states[0],
                values[0],
                doc_ids,
                stream,
                out_proj,
                norm_gain.reshape(width // 128, 128),
                router.T,
                expert_ids.reshape(1, half),
                keep_counts.reshape(1, experts),
            )
        )
    )
    if not aligned:
        chosen = chosen.transpose(0, 3, 1, 2, 4).reshape(exp_count, slots, width)
    scaled = chosen.astype(f32) * scale[:, :, None] * gain
    return scaled.astype(bf16).reshape(exp_count, owned, CAP, width)


def solution(mesh):
    placed = (
        P(("groups", "exp"), "ctx", "tp", None),
        P(("groups", "exp"), "ctx", "tp", None),
        P(("groups", "exp"), "ctx", "tp", None),
        P(("groups", "exp"), "ctx"),
        P(("groups", "exp"), ("ctx", "tp"), None),
        P("tp", "ctx"),
        P(),
        P(None, "exp"),
        P(("groups", "exp"), ("ctx", "tp"), None),
        P("groups"),
    )
    return jax.shard_map(
        on_device,
        mesh=mesh,
        in_specs=placed,
        out_specs=P(("groups", "ctx", "tp"), "exp", None, None),
        check_vma=False,
    )
```

```python
import functools
import math

import jax
import jax.numpy as jnp
from jax import lax
from jax.experimental import pallas as pl
from jax.experimental.pallas import tpu as pltpu
from jax.sharding import PartitionSpec as P

CAP = 2
EPSILON = 1e-05
WIDE = 5
MESH = pl.DeviceIdType.MESH


def kernel(
    sizes,
    q_hbm,
    key_hbm,
    value_hbm,
    doc_hbm,
    residual_hbm,
    weight_hbm,
    gain_hbm,
    router_hbm,
    ids_hbm,
    keep_hbm,
    slot_in,
    scale_ref,
    gain_row,
    q_ref,
    key_ref,
    value_ref,
    doc_ref,
    gain_ref,
    router_ref,
    ids_ref,
    keep_ref,
    kv_out,
    kv_in,
    kv_next,
    q_next,
    doc_next,
    routed,
    tally,
    logits,
    doc_in,
    attn,
    weight,
    residual,
    product,
    part_out,
    part_in,
    res_out,
    res_in,
    passing,
    tables,
    slot_out,
    begun,
    load_sem,
    kv_send,
    kv_recv,
    doc_send,
    doc_recv,
    next_send,
    next_recv,
    right_send,
    left_send,
    attn_recv,
    part_send,
    part_recv,
    res_send,
    res_recv,
    pass_send,
    pass_recv,
    slot_send,
    slot_recv,
):
    ctx_count, exp_count, back, pieces = sizes
    heads, tokens, size = q_ref.shape
    groups = kv_out.shape[0]
    ratio = heads // groups
    half = tokens // 2
    columns = weight.shape[1]
    depth = weight.shape[0] // groups
    slots = slot_out.shape[3]
    part = columns // pieces
    width = columns * ctx_count
    aligned = part % 128 == 0
    me = lax.axis_index("ctx")
    mine = lax.axis_index("exp")
    core = lax.axis_index("tp")
    rest = ctx_count - 1 - me
    early = (rest == 0) & (me > 1)

    barrier = pltpu.get_barrier_semaphore()
    for ok, step in ((rest > 0, 1), (me > 0, -1)):

        @pl.when(ok)
        def _(step=step):
            pl.semaphore_signal(
                barrier, inc=1, device_id={"ctx": me + step}, device_id_type=MESH
            )

    for shift in range(1, exp_count):
        pl.semaphore_signal(
            barrier,
            inc=1,
            device_id={"exp": lax.rem(mine + shift, exp_count)},
            device_id_type=MESH,
        )
    pl.semaphore_signal(barrier, inc=1, device_id={"tp": 1 - core}, device_id_type=MESH)

    loads = {}

    def load(name, source, target):
        loads[name] = pltpu.make_async_copy(source, target, load_sem.at[len(loads)])
        loads[name].start()

    load("key", key_hbm, key_ref)
    load("value", value_hbm, value_ref)
    load("doc", doc_hbm, doc_ref)
    load("query", q_hbm, q_ref)
    load("ids", ids_hbm, ids_ref)
    load("keep", keep_hbm, keep_ref)
    load("gain", gain_hbm, gain_ref)
    load("router", router_hbm, router_ref)
    load("weight", weight_hbm, weight)
    for block in range(ctx_count):
        there = slice(block * columns, (block + 1) * columns)
        pltpu.make_async_copy(
            residual_hbm.at[:, there] if columns % 128 == 0 else residual_hbm.at[block],
            residual.at[block],
            load_sem.at[len(loads)],
        ).start()

    loads["key"].wait()
    loads["value"].wait()
    for group in range(groups):
        kv_out[group, 0] = key_ref[:, group, :]
        kv_out[group, 1] = value_ref[:, group, :]
    loads["doc"].wait()

    both = (me > 0) & (rest > 0)
    pl.semaphore_wait(barrier, exp_count + jnp.where(both, 2, 1))

    def kv_copy(group, shift, hops=1):
        return pltpu.make_async_remote_copy(
            src_ref=kv_out.at[group] if shift == hops else kv_in.at[group, shift - 2],
            dst_ref=kv_in.at[group, shift - 1],
            send_sem=kv_send.at[group, shift - 1],
            recv_sem=kv_recv.at[group, shift - 1],
            device_id={"ctx": lax.rem(me + hops, ctx_count)},
            device_id_type=MESH,
        )

    def doc_copy(shift):
        return pltpu.make_async_remote_copy(
            src_ref=doc_ref if shift == 1 else doc_in.at[shift - 2],
            dst_ref=doc_in.at[shift - 1],
            send_sem=doc_send.at[shift - 1],
            recv_sem=doc_recv.at[shift - 1],
            device_id={"ctx": lax.rem(me + 1, ctx_count)},
            device_id_type=MESH,
        )

    def next_copy(source, target, index):
        return pltpu.make_async_remote_copy(
            src_ref=source,
            dst_ref=target,
            send_sem=next_send.at[index],
            recv_sem=next_recv.at[index],
            device_id={"ctx": lax.rem(me + ctx_count - 1, ctx_count)},
            device_id_type=MESH,
        )

    def next_doc():
        return next_copy(doc_ref, doc_next, 2 * groups)

    def next_kv(group):
        return next_copy(kv_out.at[group], kv_next.at[group], 2 * group)

    def next_query(group):
        these = pl.ds(group * ratio, ratio)
        return next_copy(q_ref.at[these], q_next.at[these], 2 * group + 1)

    def kv_direct():
        for group in range(groups - 1):
            kv_copy(group, 2, 2).start()

    if back > 1:

        @pl.when(me == 1)
        def _():
            pl.semaphore_signal(
                begun.at[2], inc=1, device_id={"ctx": me - 1}, device_id_type=MESH
            )

    @pl.when(me < ctx_count - 1)
    def _():
        doc_copy(1).start()
        for group in range(groups):
            if back > 1 and group == groups - 1:

                @pl.when(me == 0)
                def _():
                    pl.semaphore_wait(begun.at[2], 1)
                    kv_direct()

            kv_copy(group, 1).start()

    loads["query"].wait()

    @pl.when(me > 0)
    def _():
        next_doc().start()
        for group in range(groups):
            next_kv(group).start()
            next_query(group).start()

    def tell(side):
        pl.semaphore_signal(
            begun.at[side],
            inc=1,
            device_id={"ctx": me + (-1, 1)[side]},
            device_id_type=MESH,
        )

    def pass_word(side, ok):
        inward, outward = ((rest > 0, me > 0), (me > 0, rest > 0))[side]

        @pl.when(inward & ok)
        def _():
            pl.semaphore_wait(begun.at[side], 1)

        @pl.when(outward & ok)
        def _():
            tell(side)

    @pl.when(me == 0)
    def _():
        tell(1)

    @pl.when(rest == 0)
    def _():
        tell(0)

    for shift in range(1, back + 1):

        @pl.when(me < shift)
        def _(shift=shift):
            doc_in[shift - 1] = jnp.full(doc_in.shape[1:], -1, jnp.int32)
            for group in range(groups):
                kv_in[group, shift - 1] = jnp.zeros(kv_in.shape[2:], kv_in.dtype)

    def kv_arrive(group, shift):
        @pl.when(me >= shift)
        def _():
            kv_copy(group, shift).wait_recv()
            if shift < back:
                relayed = (me > 1) | (shift > 1) | (group == groups - 1)

                @pl.when((me < ctx_count - 1) & relayed)
                def _():
                    kv_copy(group, shift + 1).start()

    loads["ids"].wait()
    loads["keep"].wait()
    row = lax.broadcasted_iota(jnp.int32, (half, half), 0)
    lane = lax.broadcasted_iota(jnp.int32, (half, half), 1)
    ids_row = ids_ref[...]
    ids_column = jnp.sum(jnp.where(row == lane, ids_row, 0), axis=1, keepdims=True)
    ranking = jnp.sum(
        jnp.where((ids_column == ids_row) & (row < lane), 1, 0), axis=0, keepdims=True
    )
    experts = keep_ref.shape[1]
    square_row = lax.broadcasted_iota(jnp.int32, (experts, experts), 0)
    square_lane = lax.broadcasted_iota(jnp.int32, (experts, experts), 1)
    keep_column = jnp.sum(
        jnp.where(square_row == square_lane, keep_ref[...], 0), axis=1, keepdims=True
    )
    expert_row = lax.broadcasted_iota(jnp.int32, (experts, half), 0)
    limits = jnp.sum(jnp.where(expert_row == ids_row, keep_column, 0), axis=0, keepdims=True)
    target = jnp.where(ranking < limits, ids_row * CAP + ranking, -1)
    slot_row = lax.broadcasted_iota(jnp.int32, (slots, half), 0)
    for shift in range(exp_count):
        peer = lax.rem(mine + shift, exp_count)
        tables[shift * slots : (shift + 1) * slots] = jnp.where(
            slot_row + peer * slots == target, 1.0, 0.0
        ).astype(jnp.bfloat16)

    square = lax.broadcasted_iota(jnp.int32, (tokens, tokens), 0)
    across = lax.broadcasted_iota(jnp.int32, (tokens, tokens), 1)
    scale = 1.0 / math.sqrt(size)

    def visible(doc_row, earlier):
        doc_column = jnp.sum(jnp.where(square == across, doc_row, 0), axis=1, keepdims=True)
        masks = [(across <= square) & (doc_row == doc_column)]
        masks += [other == doc_column for other in earlier]
        return jnp.concatenate([jnp.where(mask, 1.0, 0.0) for mask in masks], axis=1) > 0.5

    def attend(block, group, allowed, query, pairs):
        keys = jnp.concatenate([pair[0] for pair in pairs], axis=0)
        vals = jnp.concatenate([pair[1] for pair in pairs], axis=0)
        count = keys.shape[0]
        stacked = query[group * ratio : (group + 1) * ratio].reshape(ratio * tokens, size)
        scores = lax.dot_general(
            stacked, keys, (((1,), (1,)), ((), ())), preferred_element_type=jnp.float32
        ).reshape(ratio, tokens, count)
        masked = jnp.where(allowed[None], scores * scale, -1e30)
        highest = jnp.max(masked, axis=2, keepdims=True)
        weights = jnp.exp(masked - highest)
        totals = jnp.sum(weights, axis=2, keepdims=True)
        mixed = jnp.dot(
            weights.astype(jnp.bfloat16).reshape(ratio * tokens, count),
            vals,
            preferred_element_type=jnp.float32,
        ).reshape(ratio, tokens, size)
        mixed = (mixed / totals).astype(jnp.bfloat16)
        for head in range(ratio):
            attn[block, group, :, head * size : (head + 1) * size] = mixed[head]

    def attn_copy(block, group, rightward):
        to = me + 1 if rightward else me - 1
        sends = right_send if rightward else left_send
        return pltpu.make_async_remote_copy(
            src_ref=attn.at[block, group],
            dst_ref=attn.at[block, group],
            send_sem=sends.at[0],
            recv_sem=attn_recv.at[block, group],
            device_id={"ctx": lax.rem(to + ctx_count, ctx_count)},
            device_id_type=MESH,
        )


    def attend_own(group):
        if back:
            kv_arrive(group, back)
        attend(
            me,
            group,
            allowed,
            q_ref,
            [kv_out.at[group]] + [kv_in.at[group, shift] for shift in range(back)],
        )
        soon = group < groups - 1

        @pl.when((me < ctx_count - 1) & (soon | (me == 0) | (rest == 1)))
        def _():
            attn_copy(me, group, True).start()

    def kv_last():
        for shift in range(1, back):
            kv_arrive(groups - 1, shift)

    for group in range(groups - 1):
        for shift in range(1, back):
            kv_arrive(group, shift)
    if groups > 1:

        @pl.when(me >= back)
        def _():
            kv_last()

    for shift in range(1, back + 1):

        @pl.when(me >= shift)
        def _(shift=shift):
            doc_copy(shift).wait_recv()
            if shift < back:

                @pl.when(me < ctx_count - 1)
                def _():
                    doc_copy(shift + 1).start()

    allowed = visible(doc_ref[...], [doc_in[shift] for shift in range(back)])
    for group in range(groups - 1):
        attend_own(group)

    @pl.when(me == 0)
    def _():
        attend_own(groups - 1)

    lower = me < ctx_count // 2
    inside = (me > 0) & (rest > 0)
    pass_word(1, lower & inside)
    pass_word(0, jnp.logical_not(lower) & inside)

    def item(turn, count):
        order = turn - 1
        spot = jnp.where(count > 0, lax.rem(order, jnp.maximum(count, 1)), 0)
        group = sum((order >= count * number).astype(jnp.int32) for number in range(1, groups))
        group = group if groups > 1 else jnp.int32(0)
        final = group == groups - 1
        active = (turn >= 1) & (turn <= groups * count)
        return group, jnp.where(final, count - spot, spot + 1), final, active

    beyond = jnp.maximum(rest - 1, 0)
    skipped = jnp.where(early, 1, 0)
    upstream = me - skipped

    def from_left(turn):
        group, far, final, active = item(turn, upstream)
        block = upstream - far

        @pl.when(active)
        def _():
            attn_copy(block, group, True).wait_recv()

            @pl.when(me < ctx_count - 1)
            def _():
                attn_copy(block, group, True).start()

                @pl.when((turn == groups * me) & (rest > 1))
                def _():
                    attn_copy(me, groups - 1, True).start()

        return block, active & final

    def from_right(turn):
        group = lax.rem(turn - 1, groups)
        block = me + 2 + (turn - 1) // groups
        final, active = group == groups - 1, turn <= groups * beyond

        @pl.when(active)
        def _():
            attn_copy(block, group, False).wait_recv()

            @pl.when(me > 0)
            def _():
                attn_copy(block, group, False).start()

        return block, active & final

    def attend_next(group):
        @pl.when(rest > 0)
        def _():
            next_kv(group).wait_recv()
            next_query(group).wait_recv()
            attend(
                me + 1,
                group,
                visible(
                    doc_next[...],
                    ([doc_ref[...]] if back else []) + [doc_in[shift] for shift in range(back - 1)],
                ),
                q_next,
                [kv_next.at[group]]
                + ([kv_out.at[group]] if back else [])
                + [kv_in.at[group, shift] for shift in range(back - 1)],
            )

            @pl.when(me > 0)
            def _():
                attn_copy(me + 1, group, False).start()

    @pl.when(rest > 0)
    def _():
        next_doc().wait_recv()

    for group in range(groups - 1):
        attend_next(group)

    @pl.when((me < back) | (groups == 1))
    def _():
        kv_last()

    from_left(1)
    pass_word(0, lower & inside)
    pass_word(1, jnp.logical_not(lower) & inside)
    attend_next(groups - 1)

    @pl.when(me > 0)
    def _():
        attend_own(groups - 1)

    def part_copy(block, piece):
        return pltpu.make_async_remote_copy(
            src_ref=part_out.at[block, piece],
            dst_ref=part_in.at[block, piece],
            send_sem=part_send.at[0],
            recv_sem=part_recv.at[block],
            device_id={"tp": 1 - core},
            device_id_type=MESH,
        )

    def res_copy(block, peer, piece):
        return pltpu.make_async_remote_copy(
            src_ref=res_out.at[block, piece],
            dst_ref=res_in.at[me, piece],
            send_sem=res_send.at[0],
            recv_sem=res_recv.at[peer, piece],
            device_id={"ctx": block},
            device_id_type=MESH,
        )

    routes = ((1, ctx_count - 3), (-1, 2)) if ctx_count > 3 else ()

    def pass_copy(side):
        sign, source = routes[side]
        return pltpu.make_async_remote_copy(
            src_ref=res_out.at[source + 2 * sign],
            dst_ref=passing.at[side],
            send_sem=res_send.at[0],
            recv_sem=pass_recv.at[side],
            device_id={"ctx": source + sign},
            device_id_type=MESH,
        )

    def onward_copy(side, piece):
        sign, source = routes[side]
        return pltpu.make_async_remote_copy(
            src_ref=passing.at[side, piece],
            dst_ref=res_in.at[source, piece],
            send_sem=pass_send.at[side],
            recv_sem=res_recv.at[source, piece],
            device_id={"ctx": source + 2 * sign},
            device_id_type=MESH,
        )

    def pass_on():
        for side, (sign, source) in enumerate(routes):

            @pl.when(me == source + sign)
            def _(side=side):
                pass_copy(side).wait_recv()
                for piece in range(pieces):
                    onward_copy(side, piece).start()

    def slot_at(peer, block, piece):
        if aligned:
            first = pl.multiple_of(block * columns + piece * part, 128)
            return slot_in.at[peer, :, pl.ds(first, part)]
        return slot_in.at[peer, block, piece]

    def slot_copy(shift, block, index, piece):
        return pltpu.make_async_remote_copy(
            src_ref=slot_out.at[shift - 1, block, piece],
            dst_ref=slot_at(mine, block, piece),
            send_sem=slot_send.at[shift - 1],
            recv_sem=slot_recv.at[index, block, piece],
            device_id={"exp": lax.rem(mine + shift, exp_count)},
            device_id_type=MESH,
        )

    def project(block):
        for start in range(0, pieces, WIDE):
            some = range(start, min(start + WIDE, pieces))
            there = slice(start * part, (some[-1] + 1) * part)
            total = None
            for group in range(groups):
                term = jnp.dot(
                    attn[block, group],
                    weight[group * depth : (group + 1) * depth, there],
                    preferred_element_type=jnp.float32,
                )
                total = term if total is None else total + term
            for piece in some:
                here = slice((piece - start) * part, (piece - start + 1) * part)
                product[block, piece, 0] = total[:half, here]
                product[block, piece, 1] = total[half:, here]
                part_out[block, piece] = product[block, piece, 1 - core].astype(jnp.bfloat16)
                part_copy(block, piece).start()

    def parts_arrive(block):
        pltpu.make_async_remote_copy(
            src_ref=part_out.at[block],
            dst_ref=part_in.at[block],
            send_sem=part_send.at[0],
            recv_sem=part_recv.at[block],
            device_id={"tp": 1 - core},
            device_id_type=MESH,
        ).wait_recv()

    def finish(block, piece):
        return (
            product[block, piece, core] + part_in[block, piece].astype(jnp.float32)
        ).astype(jnp.bfloat16)

    def send(block):
        for piece in range(pieces):
            res_copy(block, me, piece).start()

    def place(block, piece):
        hidden = (
            residual[block, :, piece * part : (piece + 1) * part].astype(jnp.float32)
            + res_in[block, piece].astype(jnp.float32)
        ).astype(jnp.bfloat16)
        rows = jnp.dot(tables[...], hidden, preferred_element_type=jnp.float32)
        rows = rows.astype(jnp.bfloat16)
        for shift in (*range(1, exp_count), 0):
            chosen = rows[shift * slots : (shift + 1) * slots]
            if shift == 0:
                slot_at(mine, block, piece)[...] = chosen
            else:
                slot_out[shift - 1, block, piece] = chosen
                slot_copy(shift, block, exp_count - shift - 1, piece).start()

    def absorb(shift, block, piece):
        peer = lax.rem(mine + shift, exp_count)
        if shift:
            slot_copy(1, block, shift - 1, piece).wait_recv()
        hidden = slot_at(peer, block, piece)[...]
        if aligned:
            first = pl.multiple_of(block * columns + piece * part, 128)
            columns_here = routed[:, pl.ds(first, part)]
        else:
            columns_here = routed[block, piece]
        logits[shift] += lax.dot_general(
            hidden,
            columns_here,
            (((1,), (1,)), ((), ())),
            preferred_element_type=jnp.float32,
        )
        wide = hidden.astype(jnp.float32)
        wide = wide * wide
        if aligned:
            total = wide[:, :128]
            for first in range(128, part, 128):
                total = total + wide[:, first : first + 128]
            tally[shift] += total
        else:
            tally[shift, :, :1] += jnp.sum(wide, axis=1, keepdims=True)

    loads["weight"].wait()
    project(me)

    @pl.when(rest > 0)
    def _():
        project(me + 1)

    loads["gain"].wait()
    loads["router"].wait()
    wide = gain_ref[...].astype(jnp.float32)
    for line in range(wide.shape[0]):
        there = slice(line * 128, (line + 1) * 128)
        gain_row[:, there] = wide[line : line + 1]
        router_ref[:, there] = (
            router_ref[:, there].astype(jnp.float32) * wide[line : line + 1]
        ).astype(jnp.bfloat16)
    if not aligned:
        for block in range(ctx_count):
            for piece in range(pieces):
                first = block * columns + piece * part
                routed[block, piece] = router_ref[:, first : first + part]
    else:
        routed = router_ref
    tally[...] = jnp.zeros_like(tally)
    logits[...] = jnp.zeros_like(logits)
    pltpu.make_async_copy(residual, residual, load_sem.at[len(loads)]).wait()

    def reply(block, now):
        parts_arrive(block)
        for piece in range(pieces):
            res_out[block, piece] = finish(block, piece)
            if now is not None:

                @pl.when(now)
                def _(piece=piece):
                    res_copy(block, me, piece).start()

        for side, (sign, source) in enumerate(routes):

            @pl.when((me == source) & (block == source + 2 * sign))
            def _(side=side):
                pass_copy(side).start()

    def send(block):
        for piece in range(pieces):
            res_copy(block, me, piece).start()

    def order(number):
        inner = jnp.where(number <= rest, me + number, number - rest - 1)
        inner = jnp.where(number == 0, me - 1, inner)
        return jnp.where(me == 0, jnp.where(number == 0, 1, ctx_count - number), inner)

    def send_far():
        def body(number, carry):
            send(ctx_count - 1 - number)
            return carry

        lax.fori_loop(0, beyond, body, 0)

    def settle(number, before):
        block = order(number)
        for piece in range(pieces):
            res_copy(me, block, piece).wait_recv()
            if piece == 0:

                @pl.when((me == 0) & (number == 1))
                def _():
                    send_far()

            place(block, piece)
            absorb(0, block, piece)
            for shift in range(1, exp_count):
                absorb(shift, before, piece)

        direct = me > (2 if routes else 1)

        @pl.when((number == 0) & direct & (rest > 0))
        def _():
            send(0)

        @pl.when((number == 1) & (me > 0) & (rest > (2 if routes else 1)))
        def _():
            send_far()

        @pl.when(number == 0)
        def _():
            pass_on()

        return block

    last = jnp.maximum(groups * upstream - 1, groups * beyond)

    late = (rest == 1) & (me > 1)

    def own():
        parts_arrive(me)
        for piece in range(pieces):
            res_in[me, piece] = finish(me, piece)
            place(me, piece)
            absorb(0, me, piece)

        @pl.when(rest > 0)
        def _():
            reply(me + 1, None)

        @pl.when((rest > 0) & jnp.logical_not(late))
        def _():
            send(me + 1)

    @pl.when(early)
    def _():
        for group in range(groups):
            attn_copy(me - 1, group, True).wait_recv()
        project(me - 1)

    @pl.when((me == 0) | (rest == 0))
    def _():
        own()

    pass_word(0, me == 0)
    pass_word(1, rest == 0)

    @pl.when(early)
    def _():
        reply(me - 1, None)
        send(me - 1)

    def step(turn, carry):
        left, left_whole = from_left(turn + 1)
        right, right_whole = from_right(turn)

        @pl.when((turn == 1) & (me > 0) & (rest > 0))
        def _():
            own()

        whole = ((left, left_whole), (right, right_whole))
        for block, has in whole:

            @pl.when(has)
            def _(block=block):
                project(block)

        prompt = (left < me - 1) & (early | (left > 0))
        for (block, has), now in zip(whole, (prompt, None)):

            @pl.when(has)
            def _(block=block, now=now):
                reply(block, now)

        @pl.when(late & (turn == groups * me - 2))
        def _():
            send(me + 1)

        @pl.when(early & (turn == (groups - 1) * upstream))
        def _():
            settle(0, me)

        return carry

    lax.fori_loop(1, jnp.maximum(last, 1) + 1, step, 0)

    @pl.when((me > 0) & (rest > 0) | (me == 1))
    def _():
        send(me - 1)

    block = lax.fori_loop(
        jnp.where(early, 1, 0), ctx_count - 1, settle, jnp.where(early, me - 1, me)
    )
    for piece in range(pieces):
        for shift in range(1, exp_count):
            absorb(shift, block, piece)

    spread = lax.broadcasted_iota(jnp.int32, logits.shape[1:], 0) // CAP
    expert = lax.broadcasted_iota(jnp.int32, logits.shape[1:], 1)
    slot_across = lax.broadcasted_iota(jnp.int32, (slots, slots), 0) == (
        lax.broadcasted_iota(jnp.int32, (slots, slots), 1)
    )
    for shift in range(exp_count):
        peer = lax.rem(mine + shift, exp_count)
        power = tally[shift] if aligned else tally[shift, :, :1]
        power = jnp.sum(power, axis=1, keepdims=True) / width
        factor = lax.rsqrt(power + EPSILON)
        logit = jnp.sum(jnp.where(spread == expert, logits[shift], 0.0), axis=1, keepdims=True)
        gate = jax.nn.sigmoid(logit * factor)
        column = gate * factor
        scale_ref[pl.ds(peer, 1)] = jnp.sum(
            jnp.where(slot_across, column, 0.0), axis=0, keepdims=True
        )

    @pl.when(me < ctx_count - 1)
    def _():
        for group in range(groups):
            kv_copy(group, 1).wait_send()
            if back > 1 and group < groups - 1:

                @pl.when(me == 0)
                def _(group=group):
                    kv_copy(group, 2, 2).wait_send()

            for shift in range(1, back):
                relayed = (me > 1) | (shift > 1) | (group == groups - 1)

                @pl.when((me >= shift) & relayed)
                def _(group=group, shift=shift):
                    kv_copy(group, shift + 1).wait_send()

    for shift in range(1, back + 1):

        @pl.when((me >= shift - 1) & (me < ctx_count - 1))
        def _(shift=shift):
            doc_copy(shift).wait_send()

    @pl.when(me > 0)
    def _():
        next_doc().wait_send()
        for group in range(groups):
            next_kv(group).wait_send()
            next_query(group).wait_send()

    def sent(source, semaphore):
        pltpu.make_async_remote_copy(
            src_ref=source,
            dst_ref=source,
            send_sem=semaphore,
            recv_sem=semaphore,
            device_id={"tp": 1 - core},
            device_id_type=MESH,
        ).wait_send()

    sent(part_out, part_send.at[0])
    sent(res_out.at[pl.ds(0, ctx_count - 1)], res_send.at[0])
    for side, (sign, source) in enumerate(routes):

        @pl.when(me == source + sign)
        def _(side=side):
            sent(passing.at[side], pass_send.at[side])

    for shift in range(1, exp_count):
        sent(slot_out.at[shift - 1], slot_send.at[shift - 1])

    for count in range(1, ctx_count):

        @pl.when((me + 1 == count) & (rest > 0))
        def _(count=count):
            sent(attn.at[pl.ds(0, count)], right_send.at[0])

        @pl.when((rest == count) & (me > 0))
        def _(count=count):
            sent(attn.at[pl.ds(0, count)], left_send.at[0])


def on_device(
    queries,
    key_states,
    values,
    doc_ids,
    residual,
    out_proj,
    norm_gain,
    router,
    expert_ids,
    keep_counts,
):
    tokens, heads, size = queries.shape[1:]
    groups = key_states.shape[2]
    ctx_count = lax.axis_size("ctx")
    exp_count = lax.axis_size("exp")
    features, columns = out_proj.shape
    half = residual.shape[1]
    width = residual.shape[2]
    experts = keep_counts.shape[0]
    owned = experts // exp_count
    slots = owned * CAP
    longest = tokens * ctx_count // 2
    back = min(ctx_count - 1, -(-(longest - 1) // tokens))
    pieces = columns // 256 if columns % 256 == 0 else 2
    part = columns // pieces
    aligned = part % 128 == 0
    vmem = pl.BlockSpec(memory_space=pltpu.VMEM)
    hbm = pl.BlockSpec(memory_space=pltpu.HBM)
    bf16, f32, i32 = jnp.bfloat16, jnp.float32, jnp.int32
    dma = pltpu.SemaphoreType.DMA
    n = ctx_count
    stream = residual[0]
    if columns % 128:
        stream = stream.reshape(half, ctx_count, columns).transpose(1, 0, 2)
    slot_shape = (exp_count, slots, width) if aligned else (exp_count, n, pieces, slots, part)
    chosen, scale, gain = pl.pallas_call(
        functools.partial(kernel, (ctx_count, exp_count, back, pieces)),
        out_shape=(
            jax.ShapeDtypeStruct(slot_shape, bf16),
            jax.ShapeDtypeStruct((exp_count, slots), f32),
            jax.ShapeDtypeStruct((1, width), f32),
        ),
        in_specs=[hbm] * 10,
        out_specs=(vmem, vmem, vmem),
        scratch_shapes=[
            pltpu.VMEM((heads, tokens, size), bf16),
            pltpu.VMEM((tokens, groups, size), bf16),
            pltpu.VMEM((tokens, groups, size), bf16),
            pltpu.VMEM((1, tokens), i32),
            pltpu.VMEM((width // 128, 128), bf16),
            pltpu.VMEM((owned, width), bf16),
            pltpu.VMEM((1, half), i32),
            pltpu.VMEM((1, experts), i32),
            pltpu.VMEM((groups, 2, tokens, size), bf16),
            pltpu.VMEM((groups, back, 2, tokens, size), bf16),
            pltpu.VMEM((groups, 2, tokens, size), bf16),
            pltpu.VMEM((heads, tokens, size), bf16),
            pltpu.VMEM((1, tokens), i32),
            pltpu.VMEM((8, 128) if aligned else (n, pieces, owned, part), bf16),
            pltpu.VMEM((exp_count, slots, 128), f32),
            pltpu.VMEM((exp_count, slots, owned), f32),
            pltpu.VMEM((back, 1, tokens), i32),
            pltpu.VMEM((n, groups, tokens, features // groups), bf16),
            pltpu.VMEM((features, columns), bf16),
            pltpu.VMEM((n, half, columns), bf16),
            pltpu.VMEM((n, pieces, 2, half, part), f32),
            pltpu.VMEM((n, pieces, half, part), bf16),
            pltpu.VMEM((n, pieces, half, part), bf16),
            pltpu.VMEM((n, pieces, half, part), bf16),
            pltpu.VMEM((n, pieces, half, part), bf16),
            pltpu.VMEM((2, pieces, half, part), bf16),
            pltpu.VMEM((exp_count * slots, half), bf16),
            pltpu.VMEM((exp_count - 1, n, pieces, slots, part), bf16),
            pltpu.SemaphoreType.REGULAR((3,)),
            dma((10,)),
            dma((groups, back)),
            dma((groups, back)),
            dma((back,)),
            dma((back,)),
            dma((2 * groups + 1,)),
            dma((2 * groups + 1,)),
            dma((1,)),
            dma((1,)),
            dma((n, groups)),
            dma((1,)),
            dma((n,)),
            dma((1,)),
            dma((n, pieces)),
            dma((2,)),
            dma((2,)),
            dma((exp_count - 1,)),
            dma((exp_count - 1, n, pieces)),
        ],
        compiler_params=pltpu.CompilerParams(
            collective_id=0, has_side_effects=True, vmem_limit_bytes=40 << 20
        ),
    )(
        *(
            pltpu.with_memory_space_constraint(operand, pltpu.HBM)
            for operand in (
                queries[0].transpose(1, 0, 2),
                key_states[0],
                values[0],
                doc_ids,
                stream,
                out_proj,
                norm_gain.reshape(width // 128, 128),
                router.T,
                expert_ids.reshape(1, half),
                keep_counts.reshape(1, experts),
            )
        )
    )
    if not aligned:
        chosen = chosen.transpose(0, 3, 1, 2, 4).reshape(exp_count, slots, width)
    scaled = chosen.astype(f32) * scale[:, :, None] * gain
    return scaled.astype(bf16).reshape(exp_count, owned, CAP, width)


def solution(mesh):
    placed = (
        P(("groups", "exp"), "ctx", "tp", None),
        P(("groups", "exp"), "ctx", "tp", None),
        P(("groups", "exp"), "ctx", "tp", None),
        P(("groups", "exp"), "ctx"),
        P(("groups", "exp"), ("ctx", "tp"), None),
        P("tp", "ctx"),
        P(),
        P(None, "exp"),
        P(("groups", "exp"), ("ctx", "tp"), None),
        P("groups"),
    )
    return jax.shard_map(
        on_device,
        mesh=mesh,
        in_specs=placed,
        out_specs=P(("groups", "ctx", "tp"), "exp", None, None),
        check_vma=False,
    )
```

```python
import functools
import math

import jax
import jax.numpy as jnp
from jax import lax
from jax.experimental import pallas as pl
from jax.experimental.pallas import tpu as pltpu
from jax.sharding import PartitionSpec as P

CAP = 2
EPSILON = 1e-05
WIDE = 5
MESH = pl.DeviceIdType.MESH


def kernel(
    sizes,
    q_hbm,
    key_hbm,
    value_hbm,
    doc_hbm,
    residual_hbm,
    weight_hbm,
    gain_hbm,
    router_hbm,
    ids_hbm,
    keep_hbm,
    slot_in,
    scale_ref,
    gain_row,
    q_ref,
    key_ref,
    value_ref,
    doc_ref,
    gain_ref,
    router_ref,
    ids_ref,
    keep_ref,
    kv_out,
    kv_in,
    kv_next,
    q_next,
    doc_next,
    routed,
    tally,
    logits,
    doc_in,
    attn,
    weight,
    residual,
    product,
    part_out,
    part_in,
    res_out,
    res_in,
    passing,
    tables,
    slot_out,
    begun,
    load_sem,
    kv_send,
    kv_recv,
    doc_send,
    doc_recv,
    next_send,
    next_recv,
    right_send,
    left_send,
    attn_recv,
    part_send,
    part_recv,
    res_send,
    res_recv,
    pass_send,
    pass_recv,
    slot_send,
    slot_recv,
):
    ctx_count, exp_count, back, pieces = sizes
    heads, tokens, size = q_ref.shape
    groups = kv_out.shape[0]
    ratio = heads // groups
    half = tokens // 2
    columns = weight.shape[1]
    depth = weight.shape[0] // groups
    slots = slot_out.shape[3]
    part = columns // pieces
    width = columns * ctx_count
    aligned = part % 128 == 0
    me = lax.axis_index("ctx")
    mine = lax.axis_index("exp")
    core = lax.axis_index("tp")
    rest = ctx_count - 1 - me
    early = (rest == 0) & (me > 1)

    barrier = pltpu.get_barrier_semaphore()
    for ok, step in ((rest > 0, 1), (me > 0, -1)):

        @pl.when(ok)
        def _(step=step):
            pl.semaphore_signal(
                barrier, inc=1, device_id={"ctx": me + step}, device_id_type=MESH
            )

    for shift in range(1, exp_count):
        pl.semaphore_signal(
            barrier,
            inc=1,
            device_id={"exp": lax.rem(mine + shift, exp_count)},
            device_id_type=MESH,
        )
    pl.semaphore_signal(barrier, inc=1, device_id={"tp": 1 - core}, device_id_type=MESH)

    loads = {}

    def load(name, source, target):
        loads[name] = pltpu.make_async_copy(source, target, load_sem.at[len(loads)])
        loads[name].start()

    load("key", key_hbm, key_ref)
    load("value", value_hbm, value_ref)
    load("doc", doc_hbm, doc_ref)
    load("query", q_hbm, q_ref)
    load("ids", ids_hbm, ids_ref)
    load("keep", keep_hbm, keep_ref)
    load("gain", gain_hbm, gain_ref)
    load("router", router_hbm, router_ref)
    load("weight", weight_hbm, weight)
    for block in range(ctx_count):
        there = slice(block * columns, (block + 1) * columns)
        pltpu.make_async_copy(
            residual_hbm.at[:, there] if columns % 128 == 0 else residual_hbm.at[block],
            residual.at[block],
            load_sem.at[len(loads)],
        ).start()

    loads["key"].wait()
    loads["value"].wait()
    for group in range(groups):
        kv_out[group, 0] = key_ref[:, group, :]
        kv_out[group, 1] = value_ref[:, group, :]
    loads["doc"].wait()

    both = (me > 0) & (rest > 0)
    pl.semaphore_wait(barrier, exp_count + jnp.where(both, 2, 1))

    def kv_copy(group, shift, hops=1):
        return pltpu.make_async_remote_copy(
            src_ref=kv_out.at[group] if shift == hops else kv_in.at[group, shift - 2],
            dst_ref=kv_in.at[group, shift - 1],
            send_sem=kv_send.at[group, shift - 1],
            recv_sem=kv_recv.at[group, shift - 1],
            device_id={"ctx": lax.rem(me + hops, ctx_count)},
            device_id_type=MESH,
        )

    def doc_copy(shift):
        return pltpu.make_async_remote_copy(
            src_ref=doc_ref if shift == 1 else doc_in.at[shift - 2],
            dst_ref=doc_in.at[shift - 1],
            send_sem=doc_send.at[shift - 1],
            recv_sem=doc_recv.at[shift - 1],
            device_id={"ctx": lax.rem(me + 1, ctx_count)},
            device_id_type=MESH,
        )

    def next_copy(source, target, index):
        return pltpu.make_async_remote_copy(
            src_ref=source,
            dst_ref=target,
            send_sem=next_send.at[index],
            recv_sem=next_recv.at[index],
            device_id={"ctx": lax.rem(me + ctx_count - 1, ctx_count)},
            device_id_type=MESH,
        )

    def next_doc():
        return next_copy(doc_ref, doc_next, 2 * groups)

    def next_kv(group):
        return next_copy(kv_out.at[group], kv_next.at[group], 2 * group)

    def next_query(group):
        these = pl.ds(group * ratio, ratio)
        return next_copy(q_ref.at[these], q_next.at[these], 2 * group + 1)

    def kv_direct():
        for group in range(groups - 1):
            kv_copy(group, 2, 2).start()

    if back > 1:

        @pl.when(me == 1)
        def _():
            pl.semaphore_signal(
                begun.at[2], inc=1, device_id={"ctx": me - 1}, device_id_type=MESH
            )

    @pl.when(me < ctx_count - 1)
    def _():
        doc_copy(1).start()
        for group in range(groups):
            if back > 1 and group == groups - 1:

                @pl.when(me == 0)
                def _():
                    pl.semaphore_wait(begun.at[2], 1)
                    kv_direct()

            kv_copy(group, 1).start()

    loads["query"].wait()

    @pl.when(me > 0)
    def _():
        next_doc().start()
        for group in range(groups):
            next_kv(group).start()
            next_query(group).start()

    def tell(side):
        pl.semaphore_signal(
            begun.at[side],
            inc=1,
            device_id={"ctx": me + (-1, 1)[side]},
            device_id_type=MESH,
        )

    def pass_word(side, ok):
        inward, outward = ((rest > 0, me > 0), (me > 0, rest > 0))[side]

        @pl.when(inward & ok)
        def _():
            pl.semaphore_wait(begun.at[side], 1)

        @pl.when(outward & ok)
        def _():
            tell(side)

    @pl.when(me == 0)
    def _():
        tell(1)

    @pl.when(rest == 0)
    def _():
        tell(0)

    for shift in range(1, back + 1):

        @pl.when(me < shift)
        def _(shift=shift):
            doc_in[shift - 1] = jnp.full(doc_in.shape[1:], -1, jnp.int32)
            for group in range(groups):
                kv_in[group, shift - 1] = jnp.zeros(kv_in.shape[2:], kv_in.dtype)

    def kv_arrive(group, shift):
        @pl.when(me >= shift)
        def _():
            kv_copy(group, shift).wait_recv()
            if shift < back:
                relayed = (me > 1) | (shift > 1) | (group == groups - 1)

                @pl.when((me < ctx_count - 1) & relayed)
                def _():
                    kv_copy(group, shift + 1).start()

    loads["ids"].wait()
    loads["keep"].wait()
    row = lax.broadcasted_iota(jnp.int32, (half, half), 0)
    lane = lax.broadcasted_iota(jnp.int32, (half, half), 1)
    ids_row = ids_ref[...]
    ids_column = jnp.sum(jnp.where(row == lane, ids_row, 0), axis=1, keepdims=True)
    ranking = jnp.sum(
        jnp.where((ids_column == ids_row) & (row < lane), 1, 0), axis=0, keepdims=True
    )
    experts = keep_ref.shape[1]
    square_row = lax.broadcasted_iota(jnp.int32, (experts, experts), 0)
    square_lane = lax.broadcasted_iota(jnp.int32, (experts, experts), 1)
    keep_column = jnp.sum(
        jnp.where(square_row == square_lane, keep_ref[...], 0), axis=1, keepdims=True
    )
    expert_row = lax.broadcasted_iota(jnp.int32, (experts, half), 0)
    limits = jnp.sum(jnp.where(expert_row == ids_row, keep_column, 0), axis=0, keepdims=True)
    target = jnp.where(ranking < limits, ids_row * CAP + ranking, -1)
    slot_row = lax.broadcasted_iota(jnp.int32, (slots, half), 0)
    for shift in range(exp_count):
        peer = lax.rem(mine + shift, exp_count)
        tables[shift * slots : (shift + 1) * slots] = jnp.where(
            slot_row + peer * slots == target, 1.0, 0.0
        ).astype(jnp.bfloat16)

    square = lax.broadcasted_iota(jnp.int32, (tokens, tokens), 0)
    across = lax.broadcasted_iota(jnp.int32, (tokens, tokens), 1)
    scale = 1.0 / math.sqrt(size)

    def visible(doc_row, earlier):
        doc_column = jnp.sum(jnp.where(square == across, doc_row, 0), axis=1, keepdims=True)
        masks = [(across <= square) & (doc_row == doc_column)]
        masks += [other == doc_column for other in earlier]
        return jnp.concatenate([jnp.where(mask, 1.0, 0.0) for mask in masks], axis=1) > 0.5

    def attend(block, group, allowed, query, pairs):
        keys = jnp.concatenate([pair[0] for pair in pairs], axis=0)
        vals = jnp.concatenate([pair[1] for pair in pairs], axis=0)
        count = keys.shape[0]
        stacked = query[group * ratio : (group + 1) * ratio].reshape(ratio * tokens, size)
        scores = lax.dot_general(
            stacked, keys, (((1,), (1,)), ((), ())), preferred_element_type=jnp.float32
        ).reshape(ratio, tokens, count)
        masked = jnp.where(allowed[None], scores * scale, -1e30)
        highest = jnp.max(masked, axis=2, keepdims=True)
        weights = jnp.exp(masked - highest)
        totals = jnp.sum(weights, axis=2, keepdims=True)
        mixed = jnp.dot(
            weights.astype(jnp.bfloat16).reshape(ratio * tokens, count),
            vals,
            preferred_element_type=jnp.float32,
        ).reshape(ratio, tokens, size)
        mixed = (mixed / totals).astype(jnp.bfloat16)
        for head in range(ratio):
            attn[block, group, :, head * size : (head + 1) * size] = mixed[head]

    def attn_copy(block, group, rightward):
        to = me + 1 if rightward else me - 1
        sends = right_send if rightward else left_send
        return pltpu.make_async_remote_copy(
            src_ref=attn.at[block, group],
            dst_ref=attn.at[block, group],
            send_sem=sends.at[0],
            recv_sem=attn_recv.at[block, group],
            device_id={"ctx": lax.rem(to + ctx_count, ctx_count)},
            device_id_type=MESH,
        )


    def attend_own(group):
        if back:
            kv_arrive(group, back)
        attend(
            me,
            group,
            allowed,
            q_ref,
            [kv_out.at[group]] + [kv_in.at[group, shift] for shift in range(back)],
        )
        soon = group < groups - 1

        @pl.when((me < ctx_count - 1) & (soon | (me == 0) | (rest == 1)))
        def _():
            attn_copy(me, group, True).start()

    def kv_last():
        for shift in range(1, back):
            kv_arrive(groups - 1, shift)

    for group in range(groups - 1):
        for shift in range(1, back):
            kv_arrive(group, shift)
    if groups > 1:

        @pl.when(me >= back)
        def _():
            kv_last()

    for shift in range(1, back + 1):

        @pl.when(me >= shift)
        def _(shift=shift):
            doc_copy(shift).wait_recv()
            if shift < back:

                @pl.when(me < ctx_count - 1)
                def _():
                    doc_copy(shift + 1).start()

    allowed = visible(doc_ref[...], [doc_in[shift] for shift in range(back)])
    for group in range(groups - 1):
        attend_own(group)

    @pl.when(me == 0)
    def _():
        attend_own(groups - 1)

    lower = me < ctx_count // 2
    inside = (me > 0) & (rest > 0)
    pass_word(1, lower & inside)
    pass_word(0, jnp.logical_not(lower) & inside)

    def item(turn, count):
        order = turn - 1
        spot = jnp.where(count > 0, lax.rem(order, jnp.maximum(count, 1)), 0)
        group = sum((order >= count * number).astype(jnp.int32) for number in range(1, groups))
        group = group if groups > 1 else jnp.int32(0)
        final = group == groups - 1
        active = (turn >= 1) & (turn <= groups * count)
        return group, jnp.where(final, count - spot, spot + 1), final, active

    beyond = jnp.maximum(rest - 1, 0)
    skipped = jnp.where(early, 1, 0)
    upstream = me - skipped

    def from_left(turn):
        group, far, final, active = item(turn, upstream)
        block = upstream - far

        @pl.when(active)
        def _():
            attn_copy(block, group, True).wait_recv()

            @pl.when(me < ctx_count - 1)
            def _():
                attn_copy(block, group, True).start()

                @pl.when((turn == groups * me) & (rest > 1))
                def _():
                    attn_copy(me, groups - 1, True).start()

        return block, active & final

    def from_right(turn):
        group = lax.rem(turn - 1, groups)
        block = me + 2 + (turn - 1) // groups
        final, active = group == groups - 1, turn <= groups * beyond

        @pl.when(active)
        def _():
            attn_copy(block, group, False).wait_recv()

            @pl.when(me > 0)
            def _():
                attn_copy(block, group, False).start()

        return block, active & final

    def attend_next(group):
        @pl.when(rest > 0)
        def _():
            next_kv(group).wait_recv()
            next_query(group).wait_recv()
            attend(
                me + 1,
                group,
                visible(
                    doc_next[...],
                    ([doc_ref[...]] if back else []) + [doc_in[shift] for shift in range(back - 1)],
                ),
                q_next,
                [kv_next.at[group]]
                + ([kv_out.at[group]] if back else [])
                + [kv_in.at[group, shift] for shift in range(back - 1)],
            )

            @pl.when(me > 0)
            def _():
                attn_copy(me + 1, group, False).start()

    @pl.when(rest > 0)
    def _():
        next_doc().wait_recv()

    for group in range(groups - 1):
        attend_next(group)

    @pl.when((me < back) | (groups == 1))
    def _():
        kv_last()

    from_left(1)
    pass_word(0, lower & inside)
    pass_word(1, jnp.logical_not(lower) & inside)
    attend_next(groups - 1)

    @pl.when(me > 0)
    def _():
        attend_own(groups - 1)

    def part_copy(block, piece):
        return pltpu.make_async_remote_copy(
            src_ref=part_out.at[block, piece],
            dst_ref=part_in.at[block, piece],
            send_sem=part_send.at[0],
            recv_sem=part_recv.at[block],
            device_id={"tp": 1 - core},
            device_id_type=MESH,
        )

    def res_copy(block, peer, piece):
        return pltpu.make_async_remote_copy(
            src_ref=res_out.at[block, piece],
            dst_ref=res_in.at[me, piece],
            send_sem=res_send.at[0],
            recv_sem=res_recv.at[peer, piece],
            device_id={"ctx": block},
            device_id_type=MESH,
        )

    routes = ((1, ctx_count - 3), (-1, 2)) if ctx_count > 3 else ()

    def pass_copy(side):
        sign, source = routes[side]
        return pltpu.make_async_remote_copy(
            src_ref=res_out.at[source + 2 * sign],
            dst_ref=passing.at[side],
            send_sem=res_send.at[0],
            recv_sem=pass_recv.at[side],
            device_id={"ctx": source + sign},
            device_id_type=MESH,
        )

    def onward_copy(side, piece):
        sign, source = routes[side]
        return pltpu.make_async_remote_copy(
            src_ref=passing.at[side, piece],
            dst_ref=res_in.at[source, piece],
            send_sem=pass_send.at[side],
            recv_sem=res_recv.at[source, piece],
            device_id={"ctx": source + 2 * sign},
            device_id_type=MESH,
        )

    def pass_on():
        for side, (sign, source) in enumerate(routes):

            @pl.when(me == source + sign)
            def _(side=side):
                pass_copy(side).wait_recv()
                for piece in range(pieces):
                    onward_copy(side, piece).start()

    def slot_at(peer, block, piece):
        if aligned:
            first = pl.multiple_of(block * columns + piece * part, 128)
            return slot_in.at[peer, :, pl.ds(first, part)]
        return slot_in.at[peer, block, piece]

    def slot_copy(shift, block, index, piece):
        return pltpu.make_async_remote_copy(
            src_ref=slot_out.at[shift - 1, block, piece],
            dst_ref=slot_at(mine, block, piece),
            send_sem=slot_send.at[shift - 1],
            recv_sem=slot_recv.at[index, block, piece],
            device_id={"exp": lax.rem(mine + shift, exp_count)},
            device_id_type=MESH,
        )

    def project(block):
        for start in range(0, pieces, WIDE):
            some = range(start, min(start + WIDE, pieces))
            there = slice(start * part, (some[-1] + 1) * part)
            total = None
            for group in range(groups):
                term = jnp.dot(
                    attn[block, group],
                    weight[group * depth : (group + 1) * depth, there],
                    preferred_element_type=jnp.float32,
                )
                total = term if total is None else total + term
            for piece in some:
                here = slice((piece - start) * part, (piece - start + 1) * part)
                product[block, piece, 0] = total[:half, here]
                product[block, piece, 1] = total[half:, here]
                part_out[block, piece] = product[block, piece, 1 - core].astype(jnp.bfloat16)
                part_copy(block, piece).start()

    def parts_arrive(block):
        pltpu.make_async_remote_copy(
            src_ref=part_out.at[block],
            dst_ref=part_in.at[block],
            send_sem=part_send.at[0],
            recv_sem=part_recv.at[block],
            device_id={"tp": 1 - core},
            device_id_type=MESH,
        ).wait_recv()

    def finish(block, piece):
        return (
            product[block, piece, core] + part_in[block, piece].astype(jnp.float32)
        ).astype(jnp.bfloat16)

    def send(block):
        for piece in range(pieces):
            res_copy(block, me, piece).start()

    def place(block, piece):
        hidden = (
            residual[block, :, piece * part : (piece + 1) * part].astype(jnp.float32)
            + res_in[block, piece].astype(jnp.float32)
        ).astype(jnp.bfloat16)
        rows = jnp.dot(tables[...], hidden, preferred_element_type=jnp.float32)
        rows = rows.astype(jnp.bfloat16)
        for shift in (*range(1, exp_count), 0):
            chosen = rows[shift * slots : (shift + 1) * slots]
            if shift == 0:
                slot_at(mine, block, piece)[...] = chosen
            else:
                slot_out[shift - 1, block, piece] = chosen
                slot_copy(shift, block, exp_count - shift - 1, piece).start()

    def absorb(shift, block, piece):
        peer = lax.rem(mine + shift, exp_count)
        if shift:
            slot_copy(1, block, shift - 1, piece).wait_recv()
        hidden = slot_at(peer, block, piece)[...]
        if aligned:
            first = pl.multiple_of(block * columns + piece * part, 128)
            columns_here = routed[:, pl.ds(first, part)]
        else:
            columns_here = routed[block, piece]
        logits[shift] += lax.dot_general(
            hidden,
            columns_here,
            (((1,), (1,)), ((), ())),
            preferred_element_type=jnp.float32,
        )
        wide = hidden.astype(jnp.float32)
        wide = wide * wide
        if aligned:
            total = wide[:, :128]
            for first in range(128, part, 128):
                total = total + wide[:, first : first + 128]
            tally[shift] += total
        else:
            tally[shift, :, :1] += jnp.sum(wide, axis=1, keepdims=True)

    loads["weight"].wait()
    project(me)

    @pl.when(rest > 0)
    def _():
        project(me + 1)

    loads["gain"].wait()
    loads["router"].wait()
    wide = gain_ref[...].astype(jnp.float32)
    for line in range(wide.shape[0]):
        there = slice(line * 128, (line + 1) * 128)
        gain_row[:, there] = wide[line : line + 1]
        router_ref[:, there] = (
            router_ref[:, there].astype(jnp.float32) * wide[line : line + 1]
        ).astype(jnp.bfloat16)
    if not aligned:
        for block in range(ctx_count):
            for piece in range(pieces):
                first = block * columns + piece * part
                routed[block, piece] = router_ref[:, first : first + part]
    else:
        routed = router_ref
    tally[...] = jnp.zeros_like(tally)
    logits[...] = jnp.zeros_like(logits)
    pltpu.make_async_copy(residual, residual, load_sem.at[len(loads)]).wait()

    def reply(block, now):
        parts_arrive(block)
        for piece in range(pieces):
            res_out[block, piece] = finish(block, piece)
            if now is not None:

                @pl.when(now)
                def _(piece=piece):
                    res_copy(block, me, piece).start()

        for side, (sign, source) in enumerate(routes):

            @pl.when((me == source) & (block == source + 2 * sign))
            def _(side=side):
                pass_copy(side).start()

    def send(block):
        for piece in range(pieces):
            res_copy(block, me, piece).start()

    def order(number):
        inner = jnp.where(number <= rest, me + number, number - rest - 1)
        inner = jnp.where(number == 0, me - 1, inner)
        return jnp.where(me == 0, jnp.where(number == 0, 1, ctx_count - number), inner)

    def send_far():
        def body(number, carry):
            send(ctx_count - 1 - number)
            return carry

        lax.fori_loop(0, beyond, body, 0)

    def gather(block, before, piece):
        absorb(0, block, piece)
        for shift in range(1, exp_count):
            absorb(shift, before, piece)

    def settle(number, before, last_one=False):
        block = order(number)
        for piece in range(pieces):
            res_copy(me, block, piece).wait_recv()
            if piece == 0:

                @pl.when((me == 0) & (number == 1))
                def _():
                    send_far()

            place(block, piece)
            if not last_one:
                gather(block, before, piece)
        if last_one:
            for piece in range(pieces):
                gather(block, before, piece)

        direct = me > (2 if routes else 1)

        @pl.when((number == 0) & direct & (rest > 0))
        def _():
            send(0)

        @pl.when((number == 1) & (me > 0) & (rest > (2 if routes else 1)))
        def _():
            send_far()

        @pl.when(number == 0)
        def _():
            pass_on()

        return block

    last = jnp.maximum(groups * upstream - 1, groups * beyond)

    late = (rest == 1) & (me > 1)

    def own():
        parts_arrive(me)
        for piece in range(pieces):
            res_in[me, piece] = finish(me, piece)
            place(me, piece)
            absorb(0, me, piece)

        @pl.when(rest > 0)
        def _():
            reply(me + 1, None)

        @pl.when((rest > 0) & jnp.logical_not(late))
        def _():
            send(me + 1)

    @pl.when(early)
    def _():
        for group in range(groups):
            attn_copy(me - 1, group, True).wait_recv()
        project(me - 1)

    @pl.when((me == 0) | (rest == 0))
    def _():
        own()

    pass_word(0, me == 0)
    pass_word(1, rest == 0)

    @pl.when(early)
    def _():
        reply(me - 1, None)
        send(me - 1)

    def step(turn, carry):
        left, left_whole = from_left(turn + 1)
        right, right_whole = from_right(turn)

        @pl.when((turn == 1) & (me > 0) & (rest > 0))
        def _():
            own()

        whole = ((left, left_whole), (right, right_whole))
        for block, has in whole:

            @pl.when(has)
            def _(block=block):
                project(block)

        prompt = (left < me - 1) & (early | (left > 0))
        for (block, has), now in zip(whole, (prompt, None)):

            @pl.when(has)
            def _(block=block, now=now):
                reply(block, now)

        @pl.when(late & (turn == groups * me - 2))
        def _():
            send(me + 1)

        @pl.when(early & (turn == (groups - 1) * upstream))
        def _():
            settle(0, me)

        return carry

    lax.fori_loop(1, jnp.maximum(last, 1) + 1, step, 0)

    @pl.when((me > 0) & (rest > 0) | (me == 1))
    def _():
        send(me - 1)

    block = lax.fori_loop(
        jnp.where(early, 1, 0), ctx_count - 2, settle, jnp.where(early, me - 1, me)
    )
    block = settle(jnp.int32(ctx_count - 2), block, True)
    for piece in range(pieces):
        for shift in range(1, exp_count):
            absorb(shift, block, piece)

    spread = lax.broadcasted_iota(jnp.int32, logits.shape[1:], 0) // CAP
    expert = lax.broadcasted_iota(jnp.int32, logits.shape[1:], 1)
    slot_across = lax.broadcasted_iota(jnp.int32, (slots, slots), 0) == (
        lax.broadcasted_iota(jnp.int32, (slots, slots), 1)
    )
    for shift in range(exp_count):
        peer = lax.rem(mine + shift, exp_count)
        power = tally[shift] if aligned else tally[shift, :, :1]
        power = jnp.sum(power, axis=1, keepdims=True) / width
        factor = lax.rsqrt(power + EPSILON)
        logit = jnp.sum(jnp.where(spread == expert, logits[shift], 0.0), axis=1, keepdims=True)
        gate = jax.nn.sigmoid(logit * factor)
        column = gate * factor
        scale_ref[pl.ds(peer, 1)] = jnp.sum(
            jnp.where(slot_across, column, 0.0), axis=0, keepdims=True
        )

    @pl.when(me < ctx_count - 1)
    def _():
        for group in range(groups):
            kv_copy(group, 1).wait_send()
            if back > 1 and group < groups - 1:

                @pl.when(me == 0)
                def _(group=group):
                    kv_copy(group, 2, 2).wait_send()

            for shift in range(1, back):
                relayed = (me > 1) | (shift > 1) | (group == groups - 1)

                @pl.when((me >= shift) & relayed)
                def _(group=group, shift=shift):
                    kv_copy(group, shift + 1).wait_send()

    for shift in range(1, back + 1):

        @pl.when((me >= shift - 1) & (me < ctx_count - 1))
        def _(shift=shift):
            doc_copy(shift).wait_send()

    @pl.when(me > 0)
    def _():
        next_doc().wait_send()
        for group in range(groups):
            next_kv(group).wait_send()
            next_query(group).wait_send()

    def sent(source, semaphore):
        pltpu.make_async_remote_copy(
            src_ref=source,
            dst_ref=source,
            send_sem=semaphore,
            recv_sem=semaphore,
            device_id={"tp": 1 - core},
            device_id_type=MESH,
        ).wait_send()

    sent(part_out, part_send.at[0])
    sent(res_out.at[pl.ds(0, ctx_count - 1)], res_send.at[0])
    for side, (sign, source) in enumerate(routes):

        @pl.when(me == source + sign)
        def _(side=side):
            sent(passing.at[side], pass_send.at[side])

    for shift in range(1, exp_count):
        sent(slot_out.at[shift - 1], slot_send.at[shift - 1])

    for count in range(1, ctx_count):

        @pl.when((me + 1 == count) & (rest > 0))
        def _(count=count):
            sent(attn.at[pl.ds(0, count)], right_send.at[0])

        @pl.when((rest == count) & (me > 0))
        def _(count=count):
            sent(attn.at[pl.ds(0, count)], left_send.at[0])


def on_device(
    queries,
    key_states,
    values,
    doc_ids,
    residual,
    out_proj,
    norm_gain,
    router,
    expert_ids,
    keep_counts,
):
    tokens, heads, size = queries.shape[1:]
    groups = key_states.shape[2]
    ctx_count = lax.axis_size("ctx")
    exp_count = lax.axis_size("exp")
    features, columns = out_proj.shape
    half = residual.shape[1]
    width = residual.shape[2]
    experts = keep_counts.shape[0]
    owned = experts // exp_count
    slots = owned * CAP
    longest = tokens * ctx_count // 2
    back = min(ctx_count - 1, -(-(longest - 1) // tokens))
    pieces = columns // 256 if columns % 256 == 0 else 2
    part = columns // pieces
    aligned = part % 128 == 0
    vmem = pl.BlockSpec(memory_space=pltpu.VMEM)
    hbm = pl.BlockSpec(memory_space=pltpu.HBM)
    bf16, f32, i32 = jnp.bfloat16, jnp.float32, jnp.int32
    dma = pltpu.SemaphoreType.DMA
    n = ctx_count
    stream = residual[0]
    if columns % 128:
        stream = stream.reshape(half, ctx_count, columns).transpose(1, 0, 2)
    slot_shape = (exp_count, slots, width) if aligned else (exp_count, n, pieces, slots, part)
    chosen, scale, gain = pl.pallas_call(
        functools.partial(kernel, (ctx_count, exp_count, back, pieces)),
        out_shape=(
            jax.ShapeDtypeStruct(slot_shape, bf16),
            jax.ShapeDtypeStruct((exp_count, slots), f32),
            jax.ShapeDtypeStruct((1, width), f32),
        ),
        in_specs=[hbm] * 10,
        out_specs=(vmem, vmem, vmem),
        scratch_shapes=[
            pltpu.VMEM((heads, tokens, size), bf16),
            pltpu.VMEM((tokens, groups, size), bf16),
            pltpu.VMEM((tokens, groups, size), bf16),
            pltpu.VMEM((1, tokens), i32),
            pltpu.VMEM((width // 128, 128), bf16),
            pltpu.VMEM((owned, width), bf16),
            pltpu.VMEM((1, half), i32),
            pltpu.VMEM((1, experts), i32),
            pltpu.VMEM((groups, 2, tokens, size), bf16),
            pltpu.VMEM((groups, back, 2, tokens, size), bf16),
            pltpu.VMEM((groups, 2, tokens, size), bf16),
            pltpu.VMEM((heads, tokens, size), bf16),
            pltpu.VMEM((1, tokens), i32),
            pltpu.VMEM((8, 128) if aligned else (n, pieces, owned, part), bf16),
            pltpu.VMEM((exp_count, slots, 128), f32),
            pltpu.VMEM((exp_count, slots, owned), f32),
            pltpu.VMEM((back, 1, tokens), i32),
            pltpu.VMEM((n, groups, tokens, features // groups), bf16),
            pltpu.VMEM((features, columns), bf16),
            pltpu.VMEM((n, half, columns), bf16),
            pltpu.VMEM((n, pieces, 2, half, part), f32),
            pltpu.VMEM((n, pieces, half, part), bf16),
            pltpu.VMEM((n, pieces, half, part), bf16),
            pltpu.VMEM((n, pieces, half, part), bf16),
            pltpu.VMEM((n, pieces, half, part), bf16),
            pltpu.VMEM((2, pieces, half, part), bf16),
            pltpu.VMEM((exp_count * slots, half), bf16),
            pltpu.VMEM((exp_count - 1, n, pieces, slots, part), bf16),
            pltpu.SemaphoreType.REGULAR((3,)),
            dma((10,)),
            dma((groups, back)),
            dma((groups, back)),
            dma((back,)),
            dma((back,)),
            dma((2 * groups + 1,)),
            dma((2 * groups + 1,)),
            dma((1,)),
            dma((1,)),
            dma((n, groups)),
            dma((1,)),
            dma((n,)),
            dma((1,)),
            dma((n, pieces)),
            dma((2,)),
            dma((2,)),
            dma((exp_count - 1,)),
            dma((exp_count - 1, n, pieces)),
        ],
        compiler_params=pltpu.CompilerParams(
            collective_id=0, has_side_effects=True, vmem_limit_bytes=40 << 20
        ),
    )(
        *(
            pltpu.with_memory_space_constraint(operand, pltpu.HBM)
            for operand in (
                queries[0].transpose(1, 0, 2),
                key_states[0],
                values[0],
                doc_ids,
                stream,
                out_proj,
                norm_gain.reshape(width // 128, 128),
                router.T,
                expert_ids.reshape(1, half),
                keep_counts.reshape(1, experts),
            )
        )
    )
    if not aligned:
        chosen = chosen.transpose(0, 3, 1, 2, 4).reshape(exp_count, slots, width)
    scaled = chosen.astype(f32) * scale[:, :, None] * gain
    return scaled.astype(bf16).reshape(exp_count, owned, CAP, width)


def solution(mesh):
    placed = (
        P(("groups", "exp"), "ctx", "tp", None),
        P(("groups", "exp"), "ctx", "tp", None),
        P(("groups", "exp"), "ctx", "tp", None),
        P(("groups", "exp"), "ctx"),
        P(("groups", "exp"), ("ctx", "tp"), None),
        P("tp", "ctx"),
        P(),
        P(None, "exp"),
        P(("groups", "exp"), ("ctx", "tp"), None),
        P("groups"),
    )
    return jax.shard_map(
        on_device,
        mesh=mesh,
        in_specs=placed,
        out_specs=P(("groups", "ctx", "tp"), "exp", None, None),
        check_vma=False,
    )
```
